32 devices in a mesh: dp: 8 (over z, y), expert: 4 (over x, core).
Axes of the slice: x: 2, y: 2, z: 4, core: 2. Of those that a mesh axis runs over, the one named last changes fastest.
Arguments:
- inputs: bfloat16 [8192, 1024], P(('dp', 'expert')), may hold values from -6 to 6
- lengths: int32 [32], P(('dp', 'expert')), may hold values from 129 to 256, as said below
- routes: int32 [8192, 8], P(('dp', 'expert')), may hold values from 0 to 15, all different within a row; in each aligned block of 256 rows (0 to 255, 256 to 511, ...) at most 192 rows name the same one
- adapter_of_sequence: int32 [32], P(('dp', 'expert')), may hold values from 0 to 7
- first_norm_gain: float32 [1024], replicated, may hold values from 0.5 to 1.5
- query_weight: bfloat16 [1024, 1024], replicated, may hold values from -0.1875 to 0.1875
- key_value_weight: bfloat16 [1024, 1024], replicated, may hold values from -0.1875 to 0.1875
- output_weight: bfloat16 [1024, 1024], replicated, may hold values from -0.75 to 0.75
- second_norm_gain: float32 [1024], replicated, may hold values from 0.5 to 1.5
- router_weight: bfloat16 [1024, 16], replicated, may hold values from -0.09375 to 0.09375
- expert_input_weight: bfloat16 [16, 1024, 1024], P('expert'), may hold values from -0.1875 to 0.1875
- expert_down_weight: bfloat16 [16, 512, 1024], P('expert'), may hold values from -0.75 to 0.75
- attention_first_factors: bfloat16 [1024, 384], replicated, may hold values from -0.1875 to 0.1875
- query_second_factors: bfloat16 [128, 1024], replicated, may hold values from -0.59765625 to 0.59765625
- key_value_second_factors: bfloat16 [2, 128, 512], replicated, may hold values from -0.59765625 to 0.59765625
- output_first_factors: bfloat16 [1024, 128], replicated, may hold values from -0.75 to 0.75
- output_second_factors: bfloat16 [128, 1024], replicated, may hold values from -1.5 to 1.5
- expert_input_first_factors: bfloat16 [16, 1024, 256], P('expert'), may hold values from -0.1875 to 0.1875
- expert_input_second_factors: bfloat16 [16, 2, 128, 512], P('expert'), may hold values from -0.59765625 to 0.59765625
- expert_down_first_factors: bfloat16 [16, 512, 128], P('expert'), may hold values from -0.25 to 0.25
- expert_down_second_factors: bfloat16 [16, 128, 1024], P('expert'), may hold values from -1.796875 to 1.796875
- output_gradient: bfloat16 [8192, 1024], P(('dp', 'expert')), may hold values from -6 to 6
Outputs:
- output: bfloat16 [8192, 1024], P(('dp', 'expert'))
- grad_input: float32 [8192, 1024], P(('dp', 'expert'))
- grad_attn_lora_a: float32 [1024, 384], replicated
- grad_q_lora_b: float32 [128, 1024], replicated
- grad_kv_lora_b: float32 [2, 128, 512], replicated
- grad_o_lora_a: float32 [1024, 128], replicated
- grad_o_lora_b: float32 [128, 1024], replicated
- grad_exp_lora_a_in: float32 [16, 1024, 256], P('expert')
- grad_exp_lora_b_in: float32 [16, 2, 128, 512], P('expert')
- grad_exp_lora_a_down: float32 [16, 512, 128], P('expert')
- grad_exp_lora_b_down: float32 [16, 128, 1024], P('expert')
The draws below stay inside these ranges and needn't reach their ends.
Inputs may be any that keep to these rules, and one draw needn't show every extreme that they name: `lengths`: every sequence holds more than half of its 256 slots; some sequence in every draw fills all 256. `routes`: the 8 experts of a row differ. In each aligned block of 256 rows (one sequence) no expert is named by more than 192 rows, a bound that some block reaches.
All inputs are finite; a program needn't handle non-finite values.
Results may differ from the reference program's by a relative error of at most 0.02.
Values may be sent and summed in bfloat16 or wider, within the bound.
No kernel may reach another device: no remote copies, remote signals or barrier semaphores. Data moves between devices by JAX's collectives and lax.ppermute only.
A program may use at most 192 MiB of HBM per device.

```python
import math
import jax
import jax.numpy as jnp
import numpy as np
from jax import lax

MODEL_WIDTH = 1024
QUERY_HEAD_COUNT = 16
KEY_VALUE_HEADS = 8
HEAD_WIDTH = 64
HIDDEN_UNITS = 512
TOP = 8
ADAPTER_COUNT = 8
ADAPTER_RANK = 16
TOK_DEV = 256
EXPERT_TOTAL = 16
CAP = 192
SEQS = 32
TOKENS = 8192


def draw_lengths(key, part):
    first_key = jax.random.fold_in(key, 11)
    second_key = jax.random.fold_in(key, 23)
    drawn = jax.random.randint(first_key, (SEQS,), TOK_DEV // 2 + 1, TOK_DEV + 1, dtype=jnp.int32)
    longest = jax.random.randint(second_key, (), 0, SEQS, dtype=jnp.int32)
    return jnp.where(jnp.arange(SEQS, dtype=jnp.int32) == longest, TOK_DEV, drawn).astype(jnp.int32)


def set_ends(entries, key, low, largest):
    dims = entries.shape
    place = [jax.random.randint(jax.random.fold_in(key, axis), (), 0, dims[axis]) for axis in range(len(dims))]
    entries = entries.at[tuple(place)].set(low)
    longest = dims.index(max(dims))
    place[longest] = (place[longest] + 1) % dims[longest]
    return entries.at[tuple(place)].set(largest)


def block_levels(stream_key, dims, pieces, low, high):
    loudness = 1.0
    for axis_at, blocks in pieces:
        steps = jax.random.uniform(jax.random.fold_in(jax.random.fold_in(stream_key, 6), axis_at), (blocks,), jnp.float32, low / len(pieces), high / len(pieces))
        loudness = loudness * jnp.repeat(jnp.exp(steps), dims[axis_at] // blocks).reshape((-1,) + (1,) * (len(dims) - 1 - axis_at))
    return loudness


def deal_out(own_key, own, number, rows, count, top, most, lean):
    order = jax.random.permutation(own_key, count)
    crowded, common = portions_of(count, rows * top, most, lean, True), portions_of(count, rows * top, most, lean, False)
    places = jnp.arange(count)

    def named(sizes, rotation):
        used = int((sizes > 0).sum())
        fixed = max(1, used // 4)
        passed = fixed + (places - fixed + rotation * (used - fixed)) % max(1, count - fixed)
        return jnp.zeros((count,), jnp.int32).at[order[jnp.where(places < fixed, places, passed)]].set(jnp.asarray(sizes, jnp.int32))

    sizes = jnp.where(number % 4 == 0, named(crowded, number // 4), named(common, number - number // 4 - 1))
    mixed = jax.random.permutation(jax.random.fold_in(own, 3), count)
    donor, sink = mixed[0:count // 2 * 2:2], mixed[1:count // 2 * 2:2]
    slack = jnp.minimum(sizes[donor] - 1, most - sizes[sink]) // 2
    slack = jnp.where((donor == order[0]) | (sink == order[0]) | (sizes[sink] == 0), 0, jnp.maximum(slack, 0))
    passed = jax.random.randint(jax.random.fold_in(own, 4), (count // 2,), 0, 1 << 20) % (slack + 1)
    sizes = sizes.at[donor].add(-passed).at[sink].add(passed)
    members = jnp.searchsorted(jnp.cumsum(sizes), jnp.arange(rows * top), side="right").astype(jnp.int32)
    listing = members.reshape(top, rows).T
    listing = listing[jax.random.permutation(jax.random.fold_in(own, 1), rows)]
    rotation = jax.random.randint(jax.random.fold_in(own, 2), (rows, 1), 0, top)
    return jnp.take_along_axis(listing, (jnp.arange(top)[None, :] + rotation) % top, axis=1)


def portions_of(number_of, total, limit, skew, full):
    portions = [(1 << 20) // math.isqrt(standing ** skew) + 1 for standing in range(1, number_of + 1)]
    largest = limit if full else min(limit, max(-(-total // number_of), total * portions[0] // sum(portions)))
    least = 1 if total - largest >= number_of - 1 else 0
    counts, rest = [largest] + [least] * (number_of - 1), total - largest - least * (number_of - 1)
    while rest > 0:
        free = [i for i in range(1, number_of) if counts[i] < largest] or [i for i in range(1, number_of) if counts[i] < limit]
        mass, left = sum([portions[i] for i in free]), rest
        for i in free:
            extra = min(limit - counts[i], max(1, left * portions[i] // mass), rest)
            counts[i] = counts[i] + extra
            rest = rest - extra
    return np.array(counts)


def bell_draw(key, dims, width, most, pieces=(), kind=jnp.bfloat16):
    level = block_levels(key, dims, pieces, -0.22, 0.18) if pieces else 1.0
    values = jax.random.normal(key, dims, jnp.float32) * width * level
    return jnp.minimum(jnp.maximum(values, -most), most).astype(kind)


def setup_inputs(seed: int = 0) -> dict:
    arg_keys = jax.random.split(jax.random.key(seed), 23)
    inputs = bell_draw(arg_keys[0], (TOKENS, MODEL_WIDTH), 1.0, 6.0, ((0, 32),))
    lengths = draw_lengths(jax.random.fold_in(arg_keys[22], 71), 0)
    routes_keys = jax.random.split(jax.random.fold_in(arg_keys[2], 1), TOKENS // TOK_DEV)
    routes_turns = jax.random.permutation(jax.random.fold_in(arg_keys[2], 3), TOKENS // TOK_DEV)
    routes = jax.vmap(lambda own, number: deal_out(jax.random.fold_in(arg_keys[2], 2), own, number, TOK_DEV, EXPERT_TOTAL, TOP, CAP, 2))(routes_keys, routes_turns).reshape((TOKENS, TOP))
    adapter_of_sequence = set_ends(jax.random.randint(arg_keys[3], (SEQS,), 0, ADAPTER_COUNT), jax.random.fold_in(arg_keys[3], 1), 0, ADAPTER_COUNT - 1).astype(jnp.int32)
    first_norm_gain = jnp.clip(1.0 + 0.1 * jax.random.normal(arg_keys[4], (MODEL_WIDTH,), jnp.float32), 0.5, 1.5)
    query_weight = bell_draw(arg_keys[5], (MODEL_WIDTH, QUERY_HEAD_COUNT * HEAD_WIDTH), MODEL_WIDTH ** -0.5, 0.1875)
    key_value_weight = bell_draw(arg_keys[6], (MODEL_WIDTH, 2 * KEY_VALUE_HEADS * HEAD_WIDTH), MODEL_WIDTH ** -0.5, 0.1875)
    output_weight = bell_draw(arg_keys[7], (QUERY_HEAD_COUNT * HEAD_WIDTH, MODEL_WIDTH), (QUERY_HEAD_COUNT * HEAD_WIDTH // 16) ** -0.5, 0.75)
    second_norm_gain = jnp.clip(1.0 + 0.1 * jax.random.normal(arg_keys[8], (MODEL_WIDTH,), jnp.float32), 0.5, 1.5)
    router_weight = bell_draw(arg_keys[9], (MODEL_WIDTH, EXPERT_TOTAL), (4 * MODEL_WIDTH) ** -0.5, 0.09375)
    expert_input_weight = bell_draw(arg_keys[10], (EXPERT_TOTAL, MODEL_WIDTH, 2 * HIDDEN_UNITS), MODEL_WIDTH ** -0.5, 0.1875, ((0, 4),))
    expert_down_weight = bell_draw(arg_keys[11], (EXPERT_TOTAL, HIDDEN_UNITS, MODEL_WIDTH), (HIDDEN_UNITS // 8) ** -0.5, 0.75, ((0, 4),))
    attention_first_factors = bell_draw(arg_keys[12], (MODEL_WIDTH, 3 * ADAPTER_COUNT * ADAPTER_RANK), MODEL_WIDTH ** -0.5, 0.1875)
    query_second_factors = bell_draw(arg_keys[13], (ADAPTER_COUNT * ADAPTER_RANK, QUERY_HEAD_COUNT * HEAD_WIDTH), 0.1, 0.59765625)
    key_value_second_factors = bell_draw(arg_keys[14], (2, ADAPTER_COUNT * ADAPTER_RANK, KEY_VALUE_HEADS * HEAD_WIDTH), 0.1, 0.59765625)
    output_first_factors = bell_draw(arg_keys[15], (QUERY_HEAD_COUNT * HEAD_WIDTH, ADAPTER_COUNT * ADAPTER_RANK), (QUERY_HEAD_COUNT * HEAD_WIDTH // 16) ** -0.5, 0.75)
    output_second_factors = bell_draw(arg_keys[16], (ADAPTER_COUNT * ADAPTER_RANK, MODEL_WIDTH), 0.25, 1.5)
    expert_input_first_factors = bell_draw(arg_keys[17], (EXPERT_TOTAL, MODEL_WIDTH, 2 * ADAPTER_COUNT * ADAPTER_RANK), MODEL_WIDTH ** -0.5, 0.1875, ((0, 4),))
    expert_input_second_factors = bell_draw(arg_keys[18], (EXPERT_TOTAL, 2, ADAPTER_COUNT * ADAPTER_RANK, HIDDEN_UNITS), 0.1, 0.59765625, ((0, 4),))
    expert_down_first_factors = bell_draw(arg_keys[19], (EXPERT_TOTAL, HIDDEN_UNITS, ADAPTER_COUNT * ADAPTER_RANK), HIDDEN_UNITS ** -0.5, 0.25, ((0, 4),))
    expert_down_second_factors = bell_draw(arg_keys[20], (EXPERT_TOTAL, ADAPTER_COUNT * ADAPTER_RANK, MODEL_WIDTH), 0.3, 1.796875, ((0, 4),))
    output_gradient = bell_draw(arg_keys[21], (TOKENS, MODEL_WIDTH), 1.0, 6.0, ((0, 32),))
    return dict(inputs=inputs, lengths=lengths, routes=routes, adapter_of_sequence=adapter_of_sequence, first_norm_gain=first_norm_gain, query_weight=query_weight, key_value_weight=key_value_weight, output_weight=output_weight, second_norm_gain=second_norm_gain, router_weight=router_weight, expert_input_weight=expert_input_weight, expert_down_weight=expert_down_weight, attention_first_factors=attention_first_factors, query_second_factors=query_second_factors, key_value_second_factors=key_value_second_factors, output_first_factors=output_first_factors, output_second_factors=output_second_factors, expert_input_first_factors=expert_input_first_factors, expert_input_second_factors=expert_input_second_factors, expert_down_first_factors=expert_down_first_factors, expert_down_second_factors=expert_down_second_factors, output_gradient=output_gradient)


norm_eps = 1e-06
rope_base = 10000.0
highest_precision = lax.Precision.HIGHEST

@jax.custom_vjp
def reduced_rank(v):
    return lax.optimization_barrier(v.astype(jnp.bfloat16)).astype(jnp.float32)

@jax.custom_vjp
def reduced_rank_backward(v):
    return v

def low_keep(v):
    return (reduced_rank(v), None)

def low_pass(kept, grad):
    return (grad,)

def back_keep(v):
    return (v, None)

def back_low(kept, grad):
    return (reduced_rank(grad),)
reduced_rank.defvjp(low_keep, low_pass)
reduced_rank_backward.defvjp(back_keep, back_low)

def rms_norm(value_rows, gain):
    factor = lax.rsqrt(lax.optimization_barrier(jnp.mean(value_rows * value_rows, axis=-1, keepdims=True)) + norm_eps)
    return value_rows * factor * gain

def rope_tables(row_count, head_dim):
    half_dim = head_dim // 2
    positions = jnp.arange(row_count, dtype=jnp.float32)
    inverse = rope_base ** (-2.0 * jnp.arange(half_dim, dtype=jnp.float32) / head_dim)
    angles = positions[:, None] * inverse[None, :]
    cosine_table = jnp.concatenate([jnp.cos(angles), jnp.cos(angles)], axis=1)
    sine_table = jnp.concatenate([jnp.sin(angles), jnp.sin(angles)], axis=1)
    return (cosine_table, sine_table)

def rotate(value_rows, cosine_table, sine_table, head_dim):
    row_count = value_rows.shape[0]
    head_values = value_rows.reshape(row_count, -1, head_dim)
    half_dim = head_dim // 2
    turned = jnp.concatenate([-head_values[..., half_dim:], head_values[..., :half_dim]], axis=-1)
    result = head_values * cosine_table[:, None, :] + turned * sine_table[:, None, :]
    return result.reshape(row_count, -1)

def slot_tables(route_rows, expert_count, capacity):
    row_count = route_rows.shape[0]
    top_count = route_rows.shape[1]
    pair_count = row_count * top_count
    flat_routes = route_rows.reshape(-1).astype(jnp.int32)
    onehot = (flat_routes[:, None] == jnp.arange(expert_count, dtype=jnp.int32)[None, :]).astype(jnp.int32)
    before = jnp.cumsum(onehot, axis=0, dtype=jnp.int32) - onehot
    slot_rank = lax.optimization_barrier(jnp.sum(before * onehot, axis=1, dtype=jnp.int32))
    slot_flat = (flat_routes * capacity + slot_rank).astype(jnp.int32)
    slot_pair = jnp.full((expert_count * capacity,), pair_count, jnp.int32).at[slot_flat].set(jnp.arange(pair_count, dtype=jnp.int32))
    slot_token = (slot_pair // top_count).astype(jnp.int32)
    return (slot_flat.reshape(row_count, top_count), slot_pair, slot_token)

def layer_block(inputs, length, adapter, route_rows, frozen, trainable_params):
    first_norm_gain, query_weight, key_value_weight, output_weight, second_norm_gain, router_weight, expert_input_weight, expert_down_weight = frozen
    attention_first_factors, query_second_factors, key_value_second_factors, output_first_factors, output_second_factors, expert_input_first_factors, expert_input_second_factors, expert_down_first_factors, expert_down_second_factors = trainable_params
    rank_total_width = ADAPTER_COUNT * ADAPTER_RANK
    key_value_width = KEY_VALUE_HEADS * HEAD_WIDTH
    groups = QUERY_HEAD_COUNT // KEY_VALUE_HEADS
    positions = jnp.arange(TOK_DEV, dtype=jnp.int32)
    live = (positions < length).astype(jnp.float32)[:, None]
    column_selector_mask = (jnp.arange(rank_total_width, dtype=jnp.int32) // ADAPTER_RANK == adapter).astype(jnp.float32)
    normalized_input = reduced_rank(rms_norm(inputs, first_norm_gain))
    rank_projection = reduced_rank_backward(reduced_rank(jnp.dot(normalized_input, attention_first_factors, precision=highest_precision) * jnp.concatenate([column_selector_mask, column_selector_mask, column_selector_mask])))
    query_preactivation = reduced_rank_backward(jnp.dot(normalized_input, query_weight, precision=highest_precision) + jnp.dot(rank_projection[:, :rank_total_width], query_second_factors, precision=highest_precision))
    key_value_base = jnp.dot(normalized_input, key_value_weight, precision=highest_precision)
    key_preactivation = reduced_rank_backward(key_value_base[:, :key_value_width] + jnp.dot(rank_projection[:, rank_total_width:2 * rank_total_width], key_value_second_factors[0], precision=highest_precision))
    value_rows = reduced_rank_backward(reduced_rank(key_value_base[:, key_value_width:] + jnp.dot(rank_projection[:, 2 * rank_total_width:], key_value_second_factors[1], precision=highest_precision)))
    cosine_table, sine_table = rope_tables(TOK_DEV, HEAD_WIDTH)
    queries = reduced_rank(rotate(query_preactivation, cosine_table, sine_table, HEAD_WIDTH))
    key_rows = reduced_rank(rotate(key_preactivation, cosine_table, sine_table, HEAD_WIDTH))
    query_heads = queries.reshape(TOK_DEV, KEY_VALUE_HEADS, groups, HEAD_WIDTH)
    key_heads = key_rows.reshape(TOK_DEV, KEY_VALUE_HEADS, HEAD_WIDTH)
    value_heads = value_rows.reshape(TOK_DEV, KEY_VALUE_HEADS, HEAD_WIDTH)
    scores = reduced_rank_backward(jnp.einsum('qjgd,kjd->jgqk', query_heads, key_heads, precision=highest_precision) * HEAD_WIDTH ** (-0.5))
    allowed = (positions[None, :] <= positions[:, None]) & (positions[None, :] < length)
    masked = jnp.where(allowed, scores, -1e+30)
    exponent = jnp.exp(masked - lax.optimization_barrier(jnp.max(masked, axis=-1, keepdims=True)))
    probs = reduced_rank_backward(reduced_rank(exponent / lax.optimization_barrier(jnp.sum(exponent, axis=-1, keepdims=True))))
    attention_result = reduced_rank_backward(reduced_rank(jnp.einsum('jgqk,kjd->qjgd', probs, value_heads, precision=highest_precision).reshape(TOK_DEV, QUERY_HEAD_COUNT * HEAD_WIDTH)))
    output_rank_values = reduced_rank_backward(reduced_rank(jnp.dot(attention_result, output_first_factors, precision=highest_precision) * column_selector_mask))
    adapter_branch = reduced_rank_backward(jnp.dot(attention_result, output_weight, precision=highest_precision) + jnp.dot(output_rank_values, output_second_factors, precision=highest_precision))
    hidden = inputs + adapter_branch
    normed2 = reduced_rank(rms_norm(hidden, second_norm_gain))
    logits = jnp.dot(normed2, router_weight, precision=highest_precision)
    chosen = jnp.take_along_axis(logits, route_rows, axis=1)
    chosen_exp = jnp.exp(chosen - lax.optimization_barrier(jnp.max(chosen, axis=1, keepdims=True)))
    pair_gates = chosen_exp / lax.optimization_barrier(jnp.sum(chosen_exp, axis=1, keepdims=True)) * live
    slot_of, unused_pair, slot_token = slot_tables(route_rows, EXPERT_TOTAL, CAP)
    padded = jnp.concatenate([normed2, jnp.zeros((1, MODEL_WIDTH), jnp.float32)], axis=0)
    rows_per_expert = reduced_rank_backward(padded[slot_token]).reshape(EXPERT_TOTAL, CAP, MODEL_WIDTH)
    combined_masks = jnp.concatenate([column_selector_mask, column_selector_mask])
    rank_projection_input = reduced_rank_backward(reduced_rank(jnp.einsum('bma,bal->bml', rows_per_expert, expert_input_first_factors, precision=highest_precision) * combined_masks))
    gate_and_up = jnp.einsum('ecd,edf->ecf', rows_per_expert, expert_input_weight, precision=highest_precision)
    gate_preactivation = reduced_rank_backward(gate_and_up[..., :HIDDEN_UNITS] + jnp.einsum('jxo,jon->jxn', rank_projection_input[..., :rank_total_width], expert_input_second_factors[:, 0], precision=highest_precision))
    upward_projection = reduced_rank_backward(gate_and_up[..., HIDDEN_UNITS:] + jnp.einsum('jxo,jon->jxn', rank_projection_input[..., rank_total_width:], expert_input_second_factors[:, 1], precision=highest_precision))
    active_adapter = reduced_rank_backward(reduced_rank(jax.nn.silu(gate_preactivation) * upward_projection))
    down_rank_values = reduced_rank_backward(reduced_rank(jnp.einsum('ljh,lho->ljo', active_adapter, expert_down_first_factors, precision=highest_precision) * column_selector_mask))
    expert_output_rows = reduced_rank_backward(reduced_rank(jnp.einsum('soa,sat->sot', active_adapter, expert_down_weight, precision=highest_precision) + jnp.einsum('wza,was->wzs', down_rank_values, expert_down_second_factors, precision=highest_precision)))
    picked = expert_output_rows.reshape(EXPERT_TOTAL * CAP, MODEL_WIDTH)[slot_of]
    mixture = lax.optimization_barrier(jnp.sum(pair_gates[:, :, None] * picked, axis=1))
    return live * (hidden + mixture)

def reference(inputs, lengths, routes, adapter_of_sequence, first_norm_gain, query_weight, key_value_weight, output_weight, second_norm_gain, router_weight, expert_input_weight, expert_down_weight, attention_first_factors, query_second_factors, key_value_second_factors, output_first_factors, output_second_factors, expert_input_first_factors, expert_input_second_factors, expert_down_first_factors, expert_down_second_factors, output_gradient):
    frozen = tuple((weight_matrix.astype(jnp.float32) for weight_matrix in (first_norm_gain, query_weight, key_value_weight, output_weight, second_norm_gain, router_weight, expert_input_weight, expert_down_weight)))
    adapter_params = tuple((weight_matrix.astype(jnp.float32) for weight_matrix in (attention_first_factors, query_second_factors, key_value_second_factors, output_first_factors, output_second_factors, expert_input_first_factors, expert_input_second_factors, expert_down_first_factors, expert_down_second_factors)))
    source = inputs.astype(jnp.float32).reshape(SEQS, TOK_DEV, MODEL_WIDTH)
    route_blocks = routes.astype(jnp.int32).reshape(SEQS, TOK_DEV, TOP)

    def forward(value_rows, trainable_params):

        def one_block(packed):
            return layer_block(packed[0], packed[1], packed[2], packed[3], frozen, trainable_params)
        return lax.map(jax.checkpoint(one_block), (value_rows, lengths.astype(jnp.int32), adapter_of_sequence.astype(jnp.int32), route_blocks))
    result, pullback = jax.vjp(forward, source, adapter_params)
    grad_source, grad_adapters = pullback(output_gradient.astype(jnp.float32).reshape(SEQS, TOK_DEV, MODEL_WIDTH))
    return (result.reshape(TOKENS, MODEL_WIDTH).astype(jnp.bfloat16), grad_source.reshape(TOKENS, MODEL_WIDTH), grad_adapters[0], grad_adapters[1], grad_adapters[2], grad_adapters[3], grad_adapters[4], grad_adapters[5], grad_adapters[6], grad_adapters[7], grad_adapters[8])
```

```python
import functools

import jax
import jax.numpy as jnp
from jax import lax
from jax.experimental import pallas as pl
from jax.experimental.pallas import tpu as pltpu
from jax.sharding import PartitionSpec as P

MODEL_WIDTH = 1024
QUERY_HEAD_COUNT = 16
KEY_VALUE_HEADS = 8
HEAD_WIDTH = 64
HIDDEN_UNITS = 512
TOP = 8
EXP_DEV = 4
ADAPTER_COUNT = 8
ADAPTER_RANK = 16
TOK_DEV = 256


norm_eps = 1e-06
rope_base = 10000.0


def rms_norm(value_rows, gain):
    factor = lax.rsqrt(jnp.mean(value_rows * value_rows, axis=-1, keepdims=True) + norm_eps)
    return value_rows * factor * gain


def rope_tables(row_count, head_dim):
    half_dim = head_dim // 2
    positions = jnp.arange(row_count, dtype=jnp.float32)
    inverse = rope_base ** (-2.0 * jnp.arange(half_dim, dtype=jnp.float32) / head_dim)
    angles = positions[:, None] * inverse[None, :]
    cosine_table = jnp.concatenate([jnp.cos(angles), jnp.cos(angles)], axis=1)
    sine_table = jnp.concatenate([jnp.sin(angles), jnp.sin(angles)], axis=1)
    return (cosine_table, sine_table)


def rotate(value_rows, cosine_table, sine_table, head_dim):
    row_count = value_rows.shape[0]
    head_values = value_rows.reshape(row_count, -1, head_dim)
    half_dim = head_dim // 2
    turned = jnp.concatenate([-head_values[..., half_dim:], head_values[..., :half_dim]], axis=-1)
    result = head_values * cosine_table[:, None, :] + turned * sine_table[:, None, :]
    return result.reshape(row_count, -1)


def rotate_back(grads, cosine_table, sine_table, head_dim):
    unused_value, pullback = jax.vjp(
        lambda value_rows: rotate(value_rows, cosine_table, sine_table, head_dim),
        jnp.zeros_like(grads),
    )
    return pullback(grads)[0]


def swap(values, axis, bit):
    size = lax.axis_size(axis)
    return lax.ppermute(values, axis, [(i, i ^ (1 << bit)) for i in range(size)])


def axis_bits(axis):
    return lax.axis_size(axis).bit_length() - 1


def gather_blocks(values):
    blocks = [values]
    for bit in reversed(range(axis_bits("expert"))):
        blocks = blocks + [swap(block, "expert", bit) for block in blocks]
    return jnp.concatenate(blocks, axis=0)


def scatter_blocks(partial):
    for bit in range(axis_bits("expert")):
        half = partial.shape[0] // 2
        got = swap(partial[half:], "expert", bit)
        total = partial[:half].astype(F32) + got.astype(F32)
        partial = total if half == TOK_DEV else total.astype(BF)
    return partial


def cube_sum(values, stages):
    done = []
    for axis, bit in stages:
        rows, width = values.shape
        if rows % 16 == 0:
            side = (lax.axis_index(axis) >> bit) & 1
            halves = values.reshape(2, rows // 2, width)
            keep = lax.dynamic_index_in_dim(halves, side, 0, keepdims=False)
            send = lax.dynamic_index_in_dim(halves, 1 - side, 0, keepdims=False)
            done.append((axis, bit, side))
        else:
            keep = send = values
        got = swap(send, axis, bit)
        values = (keep.astype(F32) + got.astype(F32)).astype(BF)
    for axis, bit, side in reversed(done):
        got = swap(values, axis, bit)
        low = jnp.where(side == 0, values, got)
        high = jnp.where(side == 0, got, values)
        values = jnp.concatenate([low, high], axis=0)
    return values


F32=jnp.float32; BF=jnp.bfloat16

def nt(a,b): return lax.dot_general(a,b,(((1,),(1,)),((),())),preferred_element_type=F32)
def nn(a,b): return lax.dot_general(a,b,(((1,),(0,)),((),())),preferred_element_type=F32)
def tn(a,b): return lax.dot_general(a,b,(((0,),(0,)),((),())),preferred_element_type=F32)

def expert_body(eid_ref, xm_ref, g_ref, win_ref, wdn_ref, ain_ref, bin_ref, adn_ref, bdn_ref, *rest, first, last, row_blocks, experts):
    if first:
        f_in=b_in_=c_in=None; rest=rest
    else:
        f_in,b_in_,c_in=rest[:3]; rest=rest[3:]
    if last:
        wr_ref=rest[0]; rest=rest[1:]
        f_out,b_out,pack_ref=rest[:3]; rest=rest[3:]
    else:
        f_out,b_out,c_out,pack_ref=rest[:4]; rest=rest[4:]
    acc_a,acc_bi,acc_ad,acc_bd=rest
    step=pl.program_id(0)
    eid=eid_ref[0]
    rows=xm_ref.shape[0]
    x=xm_ref[:, :1024]
    meta=xm_ref[:, 1024:1152].astype(F32)
    lane=lax.broadcasted_iota(jnp.int32,(rows,128),1)
    adapter=meta[:, 96:97].astype(jnp.int32)
    mask=(lane//16==adapter)
    low=pltpu.roll(meta,96,1)
    gates=jnp.where(lane<experts, meta+low, 0.0)
    here=lane==eid
    g_e=jnp.sum(jnp.where(here,gates,0.0),axis=1,keepdims=True)
    grad=g_ref[...]
    lr=nn(x,ain_ref[0])
    lrg=jnp.where(mask,lr[:, :128],0.0).astype(BF)
    lru=jnp.where(mask,lr[:,128:],0.0).astype(BF)
    gate=nn(x,win_ref[0,:, :512])+nn(lrg,bin_ref[0,0])
    up=nn(x,win_ref[0,:,512:])+nn(lru,bin_ref[0,1])
    sig=1.0/(1.0+jnp.exp(-gate))
    silu=gate*sig
    act=(silu*up).astype(BF)
    dr=jnp.where(mask,nn(act,adn_ref[0]),0.0).astype(BF)
    gradf=grad.astype(F32)
    eo=nn(act,wdn_ref[0])+nn(dr,bdn_ref[0])
    gg=jnp.sum(eo*gradf,axis=1,keepdims=True)
    fo=g_e*eo
    if not first: fo=fo+f_in[...].astype(F32)
    f_out[...]=fo.astype(f_out.dtype)
    gs=(g_e*gradf).astype(BF)
    gdr=jnp.where(mask,nt(gs,bdn_ref[0]),0.0).astype(BF)
    ga=(nt(gs,wdn_ref[0])+nt(gdr,adn_ref[0]))
    gate_grad=(ga*up*sig*(1.0+gate*(1.0-sig))).astype(BF)
    up_grad=(ga*silu).astype(BF)
    glg=jnp.where(mask,nt(gate_grad,bin_ref[0,0]),0.0).astype(BF)
    glu=jnp.where(mask,nt(up_grad,bin_ref[0,1]),0.0).astype(BF)
    grow=nt(gate_grad,win_ref[0,:, :512])+nt(up_grad,win_ref[0,:,512:])+nt(glg,ain_ref[0,:, :128])+nt(glu,ain_ref[0,:,128:])
    c=(g_e*gg)*(jnp.where(here,1.0,0.0)-gates)
    if not first:
        grow=grow+b_in_[...].astype(F32); c=c+c_in[...]
    if last:
        grow=grow+nt(c.astype(BF),wr_ref[...])
    else:
        c_out[...]=c
    b_out[...]=grow.astype(b_out.dtype)
    ga_t=jnp.concatenate([tn(glg,x),tn(glu,x)],axis=0)
    gbi=jnp.concatenate([tn(lrg,gate_grad),tn(lru,up_grad)],axis=1)
    gad=tn(gdr,act)
    gbd=tn(dr,gs)
    @pl.when(step==0)
    def _():
        acc_a[...]=ga_t; acc_bi[...]=gbi; acc_ad[...]=gad; acc_bd[...]=gbd
    @pl.when(step>0)
    def _():
        acc_a[...]+=ga_t; acc_bi[...]+=gbi; acc_ad[...]+=gad; acc_bd[...]+=gbd
    @pl.when(step==row_blocks-1)
    def _():
        pack_ref[0:256,:]=acc_a[...].astype(BF)
        pack_ref[256:384,:]=acc_bi[...].astype(BF)
        pack_ref[384:512,:]=acc_bd[...].astype(BF)
        pack_ref[512:576,0:512]=acc_ad[0:64,:].astype(BF)
        pack_ref[512:576,512:1024]=acc_ad[64:128,:].astype(BF)

def expert_call(e, eid, xm, grad, win,wdn,ain,bin_,adn,bdn, prev, wr, experts, rows=256, acc_dtype=F32):
    total=xm.shape[0]; n=total//rows
    first=prev is None; last=wr is not None
    one=pl.Buffered(1)
    rb=lambda w: pl.BlockSpec((rows,w),lambda i,*_:(i,0))
    wspec=lambda *s: pl.BlockSpec((1,)+s,lambda i,*_:(e,)+(0,)*len(s),pipeline_mode=one)
    in_specs=[rb(1152),rb(1024),wspec(1024,1024),wspec(512,1024),wspec(1024,256),wspec(2,128,512),wspec(512,128),wspec(128,1024)]
    args=[xm,grad,win,wdn,ain,bin_,adn,bdn]
    if not first:
        in_specs+= [rb(1024),rb(1024),rb(128)]
        args+=list(prev)
    if last:
        in_specs.append(pl.BlockSpec((1024,128),lambda i,*_:(0,0),pipeline_mode=one)); args.append(wr)
    S=jax.ShapeDtypeStruct
    od=BF if last else acc_dtype
    outs=[S((total,1024),od),S((total,1024),od)]; ospecs=[rb(1024),rb(1024)]
    if not last:
        outs.append(S((total,128),F32)); ospecs.append(rb(128))
    outs.append(S((576,1024),BF)); ospecs.append(pl.BlockSpec((576,1024),lambda i,*_:(0,0)))
    return pl.pallas_call(
        functools.partial(expert_body,first=first,last=last,row_blocks=n,experts=experts),
        out_shape=outs,
        grid_spec=pltpu.PrefetchScalarGridSpec(num_scalar_prefetch=1,grid=(n,),in_specs=in_specs,out_specs=ospecs,
            scratch_shapes=[pltpu.VMEM((256,1024),F32),pltpu.VMEM((128,1024),F32),pltpu.VMEM((128,512),F32),pltpu.VMEM((128,1024),F32)]),
        compiler_params=pltpu.CompilerParams(dimension_semantics=("arbitrary",),vmem_limit_bytes=60*1024*1024),
        cost_estimate=pl.CostEstimate(flops=total*9_800_000,bytes_accessed=20_000_000,transcendentals=total*512),
        name="expert_step",
    )(eid,*args)


def on_device(
    inputs,
    lengths,
    routes,
    adapter_of_sequence,
    first_norm_gain,
    query_weight,
    key_value_weight,
    output_weight,
    second_norm_gain,
    router_weight,
    expert_input_weight,
    expert_down_weight,
    attention_first_factors,
    query_second_factors,
    key_value_second_factors,
    output_first_factors,
    output_second_factors,
    expert_input_first_factors,
    expert_input_second_factors,
    expert_down_first_factors,
    expert_down_second_factors,
    output_gradient,
):
    experts = EXP_DEV * lax.axis_size("expert")
    rank_total_width = ADAPTER_COUNT * ADAPTER_RANK
    key_value_width = KEY_VALUE_HEADS * HEAD_WIDTH
    groups = QUERY_HEAD_COUNT // KEY_VALUE_HEADS
    score_scale = HEAD_WIDTH ** (-0.5)
    block_rows = min(512, TOK_DEV)
    length = lengths[0]
    adapter = adapter_of_sequence[0]
    start_offset = adapter * ADAPTER_RANK
    positions = jnp.arange(TOK_DEV, dtype=jnp.int32)
    live = (positions < length).astype(jnp.float32)[:, None]
    source = inputs.astype(jnp.float32)
    normalized_input = rms_norm(source, first_norm_gain).astype(jnp.bfloat16)
    adapter_input = jnp.concatenate(
        [
            lax.dynamic_slice_in_dim(
                attention_first_factors,
                portion_index * rank_total_width + start_offset,
                ADAPTER_RANK,
                1,
            )
            for portion_index in range(3)
        ],
        axis=1,
    )
    query_second_factor = lax.dynamic_slice_in_dim(
        query_second_factors, start_offset, ADAPTER_RANK, 0
    )
    key_second_factor = lax.dynamic_slice_in_dim(
        key_value_second_factors[0], start_offset, ADAPTER_RANK, 0
    )
    value_second_factor = lax.dynamic_slice_in_dim(
        key_value_second_factors[1], start_offset, ADAPTER_RANK, 0
    )
    output_first_factor = lax.dynamic_slice_in_dim(
        output_first_factors, start_offset, ADAPTER_RANK, 1
    )
    output_second_factor = lax.dynamic_slice_in_dim(
        output_second_factors, start_offset, ADAPTER_RANK, 0
    )
    rank_projection = jnp.dot(
        normalized_input, adapter_input, preferred_element_type=jnp.float32
    ).astype(jnp.bfloat16)
    rank_query = rank_projection[:, :ADAPTER_RANK]
    rank_key = rank_projection[:, ADAPTER_RANK : 2 * ADAPTER_RANK]
    rank_value = rank_projection[:, 2 * ADAPTER_RANK :]
    query_preactivation = jnp.dot(
        normalized_input, query_weight, preferred_element_type=jnp.float32
    ) + jnp.dot(rank_query, query_second_factor, preferred_element_type=jnp.float32)
    key_value_base = jnp.dot(normalized_input, key_value_weight, preferred_element_type=jnp.float32)
    key_preactivation = key_value_base[:, :key_value_width] + jnp.dot(
        rank_key, key_second_factor, preferred_element_type=jnp.float32
    )
    value_rows = (
        key_value_base[:, key_value_width:]
        + jnp.dot(rank_value, value_second_factor, preferred_element_type=jnp.float32)
    ).astype(jnp.bfloat16)
    cosine_table, sine_table = rope_tables(TOK_DEV, HEAD_WIDTH)
    queries = rotate(query_preactivation, cosine_table, sine_table, HEAD_WIDTH).astype(jnp.bfloat16)
    key_rows = rotate(key_preactivation, cosine_table, sine_table, HEAD_WIDTH).astype(jnp.bfloat16)
    query_heads = queries.reshape(TOK_DEV, KEY_VALUE_HEADS, groups, HEAD_WIDTH)
    key_heads = key_rows.reshape(TOK_DEV, KEY_VALUE_HEADS, HEAD_WIDTH)
    value_heads = value_rows.reshape(TOK_DEV, KEY_VALUE_HEADS, HEAD_WIDTH)

    def block_scores(row_start):
        raw_scores = (
            jnp.einsum("qjgd,kjd->jgqk", query_heads, key_heads, preferred_element_type=jnp.float32)
            * score_scale
        )
        block_positions = row_start + jnp.arange(block_rows, dtype=jnp.int32)
        allowed = (positions[None, :] <= block_positions[:, None]) & (positions[None, :] < length)
        return (query_heads, jnp.where(allowed, raw_scores, -1e30))

    row_start = 0
    query_block, masked = block_scores(row_start)
    top_score = jnp.max(masked, axis=-1, keepdims=True)
    exponent = jnp.exp(masked - top_score)
    row_total = jnp.sum(exponent, axis=-1, keepdims=True)
    probs_block = (exponent / row_total).astype(jnp.bfloat16)
    log_totals = [top_score + jnp.log(row_total)]
    attended_parts = jnp.einsum(
        "jgqk,kjd->qjgd", probs_block, value_heads, preferred_element_type=jnp.float32
    ).astype(jnp.bfloat16)
    attention_result = attended_parts.reshape(TOK_DEV, QUERY_HEAD_COUNT * HEAD_WIDTH)
    output_rank_values = jnp.dot(
        attention_result, output_first_factor, preferred_element_type=jnp.float32
    ).astype(jnp.bfloat16)
    hidden = (
        source
        + jnp.dot(attention_result, output_weight, preferred_element_type=jnp.float32)
        + jnp.dot(output_rank_values, output_second_factor, preferred_element_type=jnp.float32)
    )
    normed2 = rms_norm(hidden, second_norm_gain).astype(jnp.bfloat16)
    logits = jnp.dot(normed2, router_weight, preferred_element_type=jnp.float32)
    expert_numbers = jnp.arange(experts, dtype=jnp.int32)
    selected = jnp.any(routes[:, :, None] == expert_numbers[None, None, :], axis=1)
    top_logit = jnp.max(jnp.where(selected, logits, -1e30), axis=1, keepdims=True)
    chosen_exp = jnp.where(selected, jnp.exp(jnp.minimum(logits - top_logit, 0.0)), 0.0)
    gates = chosen_exp / jnp.sum(chosen_exp, axis=1, keepdims=True) * live
    gate_high = gates.astype(jnp.bfloat16)
    gate_low = (gates - gate_high.astype(jnp.float32)).astype(jnp.bfloat16)
    spare = jnp.zeros((TOK_DEV, 32 - experts), jnp.bfloat16)
    adapter_lane = jnp.full((TOK_DEV, 32), adapter, jnp.bfloat16)
    payload = jnp.concatenate(
        [
            normed2,
            gate_high,
            spare,
            gate_low,
            spare,
            jnp.zeros((TOK_DEV, 32), jnp.bfloat16),
            adapter_lane,
        ],
        axis=1,
    )
    grad_output = output_gradient.astype(jnp.float32) * live
    all_grads = gather_blocks(output_gradient)
    all_rows = gather_blocks(payload)
    router_wide = jnp.concatenate(
        [router_weight, jnp.zeros((MODEL_WIDTH, 128 - experts), jnp.bfloat16)], axis=1
    )
    carried = None
    packs = []
    first_expert = EXP_DEV * lax.axis_index("expert")
    for local in range(EXP_DEV):
        results = expert_call(
            local,
            (first_expert + local)[None],
            all_rows,
            all_grads,
            expert_input_weight,
            expert_down_weight,
            expert_input_first_factors,
            expert_input_second_factors,
            expert_down_first_factors,
            expert_down_second_factors,
            carried,
            router_wide if local == EXP_DEV - 1 else None,
            experts,
        )
        packs.append(results[-1])
        carried = results[:-1]
    mixture_part, row_part = carried
    grad_normed2 = scatter_blocks(row_part)
    mixture = hidden + scatter_blocks(mixture_part)
    output = (live * mixture).astype(jnp.bfloat16)
    dp_stages = [("dp", bit) for bit in range(axis_bits("dp"))]
    packs = [cube_sum(pack, dp_stages) for pack in packs]
    stacked = jnp.stack(packs).astype(jnp.float32)
    summed_experts = (
        jnp.swapaxes(stacked[:, :256], 1, 2),
        jnp.stack(
            [stacked[:, 256:384, :HIDDEN_UNITS], stacked[:, 256:384, HIDDEN_UNITS:]], axis=1
        ),
        jnp.swapaxes(
            jnp.concatenate(
                [stacked[:, 512:, :HIDDEN_UNITS], stacked[:, 512:, HIDDEN_UNITS:]], axis=1
            ),
            1,
            2,
        ),
        stacked[:, 384:512],
    )
    unused_hidden, norm2_back = jax.vjp(
        lambda values_in: rms_norm(values_in, second_norm_gain), hidden
    )
    grad_hidden = grad_output + norm2_back(grad_normed2)[0]
    grad_branch = grad_hidden.astype(jnp.bfloat16)
    grad_b_out = jnp.dot(output_rank_values.T, grad_branch, preferred_element_type=jnp.float32)
    grad_out_rank = jnp.dot(
        grad_branch, output_second_factor.T, preferred_element_type=jnp.float32
    ).astype(jnp.bfloat16)
    grad_a_out = jnp.dot(grad_out_rank.T, attention_result, preferred_element_type=jnp.float32)
    grad_attended = jnp.dot(grad_branch, output_weight.T, preferred_element_type=jnp.float32)
    grad_attended = (
        grad_attended
        + jnp.dot(grad_out_rank, output_first_factor.T, preferred_element_type=jnp.float32)
    ).astype(jnp.bfloat16)
    grad_heads = grad_attended.reshape(TOK_DEV, KEY_VALUE_HEADS, groups, HEAD_WIDTH)
    grad_keys = jnp.zeros((TOK_DEV, KEY_VALUE_HEADS, HEAD_WIDTH), jnp.float32)
    grad_values = jnp.zeros((TOK_DEV, KEY_VALUE_HEADS, HEAD_WIDTH), jnp.float32)
    query_parts = []
    for block_index, row_start in enumerate(range(0, TOK_DEV, block_rows)):
        query_block, masked = block_scores(row_start)
        probs_exact = jnp.exp(masked - log_totals[block_index])
        probs_block = probs_exact.astype(jnp.bfloat16)
        grad_values = jnp.einsum(
            "jgqk,qjgd->kjd", probs_block, grad_heads, preferred_element_type=jnp.float32
        )
        grad_probs = jnp.einsum(
            "qjgd,kjd->jgqk", grad_heads, value_heads, preferred_element_type=jnp.float32
        ).astype(jnp.bfloat16)
        row_inner = jnp.sum(grad_probs * probs_exact, axis=-1, keepdims=True)
        grad_scores = (probs_exact * (grad_probs - row_inner)).astype(jnp.bfloat16)
        query_parts.append(
            jnp.einsum("jgqk,kjd->qjgd", grad_scores, key_heads, preferred_element_type=jnp.float32)
            * score_scale
        )
        grad_keys = (
            jnp.einsum(
                "jgqk,qjgd->kjd", grad_scores, query_block, preferred_element_type=jnp.float32
            )
            * score_scale
        )
    grad_query = query_parts[0].reshape(TOK_DEV, QUERY_HEAD_COUNT * HEAD_WIDTH)
    grad_query_pre = rotate_back(grad_query, cosine_table, sine_table, HEAD_WIDTH).astype(
        jnp.bfloat16
    )
    grad_key_pre = rotate_back(
        grad_keys.reshape(TOK_DEV, key_value_width), cosine_table, sine_table, HEAD_WIDTH
    ).astype(jnp.bfloat16)
    grad_value = grad_values.reshape(TOK_DEV, key_value_width).astype(jnp.bfloat16)
    grad_b_query = jnp.dot(rank_query.T, grad_query_pre, preferred_element_type=jnp.float32)
    grad_b_key = jnp.dot(rank_key.T, grad_key_pre, preferred_element_type=jnp.float32)
    grad_b_value = jnp.dot(rank_value.T, grad_value, preferred_element_type=jnp.float32)
    gradient_rank_values = jnp.concatenate(
        [
            jnp.dot(grad_query_pre, query_second_factor.T, preferred_element_type=jnp.float32),
            jnp.dot(grad_key_pre, key_second_factor.T, preferred_element_type=jnp.float32),
            jnp.dot(grad_value, value_second_factor.T, preferred_element_type=jnp.float32),
        ],
        axis=1,
    ).astype(jnp.bfloat16)
    gradient_adapter_input = jnp.dot(
        gradient_rank_values.T, normalized_input, preferred_element_type=jnp.float32
    )
    gradient_of_normed = jnp.dot(grad_query_pre, query_weight.T, preferred_element_type=jnp.float32)
    gradient_of_normed = gradient_of_normed + jnp.dot(
        jnp.concatenate([grad_key_pre, grad_value], axis=1),
        key_value_weight.T,
        preferred_element_type=jnp.float32,
    )
    gradient_of_normed = gradient_of_normed + jnp.dot(
        gradient_rank_values, adapter_input.T, preferred_element_type=jnp.float32
    )
    unused_source, norm1_back = jax.vjp(
        lambda values_in: rms_norm(values_in, first_norm_gain), source
    )
    grad_input = grad_hidden + norm1_back(gradient_of_normed)[0]
    compact = jnp.concatenate(
        [
            gradient_adapter_input,
            grad_b_query,
            jnp.concatenate([grad_b_key, grad_b_value], axis=1),
            grad_a_out,
            grad_b_out,
        ],
        axis=0,
    ).reshape(7, 1, ADAPTER_RANK, MODEL_WIDTH)
    owned = (jnp.arange(ADAPTER_COUNT, dtype=jnp.int32) == adapter)[None, :, None, None]
    spread = jnp.where(owned, compact, 0.0).astype(jnp.bfloat16)
    stages = [("expert", bit) for bit in range(axis_bits("expert"))] + dp_stages
    summed = cube_sum(spread.reshape(7 * rank_total_width, MODEL_WIDTH), stages).astype(jnp.float32)
    return (
        output,
        grad_input,
        summed[:384].T,
        summed[384:512],
        jnp.stack([summed[512:640, :key_value_width], summed[512:640, key_value_width:]]),
        summed[640:768].T,
        summed[768:896],
        *summed_experts,
    )


def solution(mesh):
    placed = (
        P(("dp", "expert"), None),
        P(("dp", "expert")),
        P(("dp", "expert"), None),
        P(("dp", "expert")),
        P(),
        P(),
        P(),
        P(),
        P(),
        P(),
        P("expert", None, None),
        P("expert", None, None),
        P(),
        P(),
        P(),
        P(),
        P(),
        P("expert", None, None),
        P("expert", None, None, None),
        P("expert", None, None),
        P("expert", None, None),
        P(("dp", "expert"), None),
    )
    return jax.shard_map(
        on_device,
        mesh=mesh,
        in_specs=placed,
        out_specs=(
            P(("dp", "expert"), None),
            P(("dp", "expert"), None),
            P(),
            P(),
            P(),
            P(),
            P(),
            P("expert", None, None),
            P("expert", None, None, None),
            P("expert", None, None),
            P("expert", None, None),
        ),
        check_vma=False,
    )
```

```python
import functools

import jax
import jax.numpy as jnp
import numpy as np
from jax import lax
from jax.experimental import pallas as pl
from jax.experimental.pallas import tpu as pltpu
from jax.sharding import PartitionSpec as P

MODEL_WIDTH = 1024
HALF_WIDTH = 512
HEAD_WIDTH = 64
ADAPTER_RANK = 16
TOK_DEV = 256
EXP_DEV = 4
LANES = 128
META = MODEL_WIDTH + LANES
PACK_ROWS = 576
ATT_ROWS = 896
NORM_EPS = 1e-06
ROPE_BASE = 10000.0
F32 = jnp.float32
BF = jnp.bfloat16
ANY = pl.BlockSpec(memory_space=pl.ANY)
SMEM = pl.BlockSpec(memory_space=pltpu.SMEM)
VMEM = pl.BlockSpec(memory_space=pltpu.VMEM)
VMEM_LIMIT = 60 * 1024 * 1024


def nn(a, b):
    return lax.dot_general(a, b, (((1,), (0,)), ((), ())), preferred_element_type=F32)


def nt(a, b):
    return lax.dot_general(a, b, (((1,), (1,)), ((), ())), preferred_element_type=F32)


def tn(a, b):
    return lax.dot_general(a, b, (((0,), (0,)), ((), ())), preferred_element_type=F32)


def shape(*dims, dtype=BF):
    return jax.ShapeDtypeStruct(dims, dtype)


def rope_tables():
    inverse = ROPE_BASE ** (-2.0 * np.arange(HEAD_WIDTH // 2, dtype=np.float64) / HEAD_WIDTH)
    angles = np.arange(TOK_DEV, dtype=np.float64)[:, None] * inverse[None, :]
    cosine = np.tile(np.cos(angles), (1, 4)).astype(np.float32)
    sine = np.sin(angles)
    signed = np.concatenate([-sine, sine, -sine, sine], axis=1).astype(np.float32)
    return cosine, signed


def lanes_of(rows):
    return lax.broadcasted_iota(jnp.int32, (rows, LANES), 1)


def swap_halves(block):
    first = lanes_of(block.shape[0]) % HEAD_WIDTH < HEAD_WIDTH // 2
    return jnp.where(first, pltpu.roll(block, LANES - 32, 1), pltpu.roll(block, 32, 1))


def both(block, odd):
    low = lanes_of(block.shape[0]) < HEAD_WIDTH
    wide = block.astype(F32)
    other = pltpu.roll(wide, HEAD_WIDTH, 1)
    return (jnp.where(low, other, wide) if odd else jnp.where(low, wide, other)).astype(BF)


def stacked(block):
    low = lanes_of(block.shape[0]) < HEAD_WIDTH
    wide = block.astype(F32)
    return jnp.concatenate(
        [jnp.where(low, wide, 0.0).astype(BF), jnp.where(low, 0.0, wide).astype(BF)], axis=0
    )


def unstacked(pair):
    low = lanes_of(TOK_DEV) < HEAD_WIDTH
    return jnp.where(low, pair[:TOK_DEV], pair[TOK_DEV:])


def allowed_keys(length):
    row = lax.broadcasted_iota(jnp.int32, (2 * TOK_DEV, TOK_DEV), 0) % TOK_DEV
    col = lax.broadcasted_iota(jnp.int32, (2 * TOK_DEV, TOK_DEV), 1)
    return (col <= row) & (col < length)


def softmax(query_pair, key_both, allowed):
    scores = jnp.where(allowed, nt(query_pair, key_both) * (HEAD_WIDTH**-0.5), -1e30)
    exponent = jnp.exp(scores - jnp.max(scores, axis=1, keepdims=True))
    return exponent * (1.0 / jnp.sum(exponent, axis=1, keepdims=True))


def column(index):
    return slice(index * LANES, (index + 1) * LANES)


def forward_body(
    scalars, x_ref, g1_ref, g2_ref, cos_ref, sin_ref, routes_ref, router_ref,
    aat_h, wq_h, bq_h, wkv_h, bkv_h, ao_h, wo_h, bo_h,
    hidden_ref, payload_ref, normed_ref, lowrank_ref, q_ref, k_ref, v_ref, att_ref, orank_ref, wide_ref,
    aat, wq, bq, wkv, bkv, ao, wo, bo, sems, *, experts,
):
    copies = [
        pltpu.make_async_copy(source, target, sems.at[index])
        for index, (source, target) in enumerate(
            [(aat_h, aat), (wq_h, wq), (bq_h, bq), (wkv_h, wkv), (bkv_h, bkv), (ao_h, ao), (wo_h, wo), (bo_h, bo)]
        )
    ]
    for copy in copies:
        copy.start()
    adapter = scalars[0]
    length = scalars[1]
    lane = lanes_of(TOK_DEV)
    mask = lane // ADAPTER_RANK == adapter
    x = x_ref[...].astype(F32)
    factor = lax.rsqrt(jnp.mean(x * x, axis=1, keepdims=True) + NORM_EPS)
    normed = (x * factor * g1_ref[...]).astype(BF)
    normed_ref[...] = normed
    copies[0].wait()
    low = nn(normed, aat[...])
    ranks = [jnp.where(mask, low[:, column(i)], 0.0).astype(BF) for i in range(3)]
    for i in range(3):
        lowrank_ref[:, column(i)] = ranks[i]
    cosine = cos_ref[...]
    sine = sin_ref[...]
    copies[1].wait()
    copies[2].wait()
    query_pre = nn(normed, wq[...]) + nn(ranks[0], bq[...])
    for j in range(8):
        block = query_pre[:, column(j)]
        q_ref[:, column(j)] = (block * cosine + swap_halves(block) * sine).astype(BF)
    copies[3].wait()
    copies[4].wait()
    pre = nn(normed, wkv[...])
    key_pre = pre[:, :HALF_WIDTH] + nn(ranks[1], bkv[0])
    v_ref[...] = (pre[:, HALF_WIDTH:] + nn(ranks[2], bkv[1])).astype(BF)
    for j in range(4):
        block = key_pre[:, column(j)]
        k_ref[:, column(j)] = (block * cosine + swap_halves(block) * sine).astype(BF)
    allowed = allowed_keys(length)
    for j in range(8):
        pair = stacked(q_ref[:, column(j)])
        probs = softmax(pair, both(k_ref[:, column(j // 2)], j % 2), allowed).astype(BF)
        att_ref[:, column(j)] = unstacked(nn(probs, both(v_ref[:, column(j // 2)], j % 2))).astype(BF)
    attended = att_ref[...]
    for copy in copies[5:]:
        copy.wait()
    orank = jnp.where(mask, nn(attended, ao[...]), 0.0).astype(BF)
    orank_ref[...] = orank
    hidden = x + nn(attended, wo[...]) + nn(orank, bo[...])
    hidden_ref[...] = hidden
    factor2 = lax.rsqrt(jnp.mean(hidden * hidden, axis=1, keepdims=True) + NORM_EPS)
    normed2 = (hidden * factor2 * g2_ref[...]).astype(BF)
    spread = jnp.where(
        lax.broadcasted_iota(jnp.int32, (experts, LANES), 0)
        == lax.broadcasted_iota(jnp.int32, (experts, LANES), 1), 1.0, 0.0,
    ).astype(BF)
    wide = nn(router_ref[...], spread).astype(BF)
    wide_ref[...] = wide
    logits = nn(normed2, wide)
    routes = routes_ref[...]
    selected = routes[:, 0:1] == lane
    for k in range(1, routes.shape[1]):
        selected = selected | (routes[:, k : k + 1] == lane)
    top = jnp.max(jnp.where(selected, logits, -1e30), axis=1, keepdims=True)
    chosen = jnp.where(selected, jnp.exp(jnp.minimum(logits - top, 0.0)), 0.0)
    live = lax.broadcasted_iota(jnp.int32, (TOK_DEV, 1), 0) < length
    gates = chosen * jnp.where(live, 1.0 / jnp.sum(chosen, axis=1, keepdims=True), 0.0)
    high = gates.astype(BF).astype(F32)
    meta = high + pltpu.roll(gates - high, 32, 1) + jnp.where(lane >= 96, adapter.astype(F32), 0.0)
    payload_ref[:, :MODEL_WIDTH] = normed2
    payload_ref[:, MODEL_WIDTH:] = meta.astype(BF)


def attention_forward(scalars, x, g1, g2, cosine, sine, routes, router, weights):
    experts = router.shape[1]
    return pl.pallas_call(
        functools.partial(forward_body, experts=experts),
        out_shape=[
            shape(TOK_DEV, MODEL_WIDTH, dtype=F32),
            shape(TOK_DEV, META),
            shape(TOK_DEV, MODEL_WIDTH),
            shape(TOK_DEV, 3 * LANES),
            shape(TOK_DEV, MODEL_WIDTH),
            shape(TOK_DEV, HALF_WIDTH),
            shape(TOK_DEV, HALF_WIDTH),
            shape(TOK_DEV, MODEL_WIDTH),
            shape(TOK_DEV, LANES),
            shape(MODEL_WIDTH, LANES),
        ],
        in_specs=[SMEM] + [VMEM] * 7 + [ANY] * 8,
        out_specs=[VMEM] * 10,
        scratch_shapes=[pltpu.VMEM(w.shape, BF) for w in weights] + [pltpu.SemaphoreType.DMA((8,))],
        compiler_params=pltpu.CompilerParams(vmem_limit_bytes=VMEM_LIMIT),
        cost_estimate=pl.CostEstimate(flops=3_000_000_000, bytes_accessed=20_000_000, transcendentals=1_000_000),
        name="attention_forward",
    )(scalars, x, g1, g2, cosine, sine, routes, router, *weights)


def backward_body(
    scalars, x_ref, g1_ref, g2_ref, cos_ref, sin_ref, hidden_ref, keep_ref, got_ref, og_ref,
    normed_ref, lowrank_ref, q_ref, k_ref, v_ref, att_ref, orank_ref,
    aat_h, wq_h, bq_h, wkv_h, bkv_h, ao_h, wo_h, bo_h,
    gi_ref, mine_ref, send_ref,
    aat, wq, bq, wkv, bkv, ao, wo, bo, pack, gq_s, gk_s, gv_s, sems,
):
    order = [(bo_h, bo), (wo_h, wo), (ao_h, ao), (bq_h, bq), (bkv_h, bkv), (wq_h, wq), (wkv_h, wkv), (aat_h, aat)]
    copies = [
        pltpu.make_async_copy(source, target, sems.at[index]) for index, (source, target) in enumerate(order)
    ]
    for copy in copies:
        copy.start()
    adapter = scalars[0]
    length = scalars[1]
    side = scalars[2]
    mask = lanes_of(TOK_DEV) // ADAPTER_RANK == adapter

    def masked(values):
        return jnp.where(mask, values, 0.0).astype(BF)

    hidden = hidden_ref[...]
    factor2 = lax.rsqrt(jnp.mean(hidden * hidden, axis=1, keepdims=True) + NORM_EPS)
    live = lax.broadcasted_iota(jnp.int32, (TOK_DEV, 1), 0) < length
    grad_live = jnp.where(live, og_ref[...].astype(F32), 0.0)
    y = (keep_ref[...].astype(F32) + got_ref[...].astype(F32)) * g2_ref[...]
    inner = jnp.mean(y * hidden, axis=1, keepdims=True)
    grad_hidden = grad_live + factor2 * (y - hidden * (factor2 * factor2 * inner))
    gi_ref[...] = grad_hidden
    branch = grad_hidden.astype(BF)
    pack[768:896, :] = tn(orank_ref[...], branch).astype(BF)
    for copy in copies[:3]:
        copy.wait()
    grad_orank = masked(nt(branch, bo[...]))
    pack[640:768, :] = tn(grad_orank, att_ref[...]).astype(BF)
    grad_att = (nt(branch, wo[...]) + nt(grad_orank, ao[...])).astype(BF)
    allowed = allowed_keys(length)
    cosine = cos_ref[...]
    sine = sin_ref[...]
    low = lanes_of(TOK_DEV) < HEAD_WIDTH
    scale = HEAD_WIDTH**-0.5
    kept = None
    for j in range(8):
        pair = stacked(q_ref[:, column(j)])
        key_both = both(k_ref[:, column(j // 2)], j % 2)
        value_both = both(v_ref[:, column(j // 2)], j % 2)
        probs = softmax(pair, key_both, allowed)
        grad_pair = stacked(grad_att[:, column(j)])
        grad_probs = nt(grad_pair, value_both).astype(BF).astype(F32)
        grad_v = tn(probs.astype(BF), grad_pair)
        scores = (probs * (grad_probs - jnp.sum(grad_probs * probs, axis=1, keepdims=True))).astype(BF)
        grad_q = unstacked(nn(scores, key_both)) * scale
        gq_s[:, column(j)] = (grad_q * cosine - swap_halves(grad_q) * sine).astype(BF)
        grad_k = tn(scores, pair) * scale
        grad_v = grad_v + pltpu.roll(grad_v, HEAD_WIDTH, 1)
        grad_k = grad_k + pltpu.roll(grad_k, HEAD_WIDTH, 1)
        if j % 2 == 0:
            kept = (grad_k, grad_v)
        else:
            block = jnp.where(low, kept[0], grad_k)
            gk_s[:, column(j // 2)] = (block * cosine - swap_halves(block) * sine).astype(BF)
            gv_s[:, column(j // 2)] = jnp.where(low, kept[1], grad_v).astype(BF)
    gq = gq_s[...]
    gk = gk_s[...]
    gv = gv_s[...]
    pack[384:512, :] = tn(lowrank_ref[:, column(0)], gq).astype(BF)
    pack[512:640, :HALF_WIDTH] = tn(lowrank_ref[:, column(1)], gk).astype(BF)
    pack[512:640, HALF_WIDTH:] = tn(lowrank_ref[:, column(2)], gv).astype(BF)
    copies[3].wait()
    copies[4].wait()
    grad_rank = jnp.concatenate(
        [masked(nt(gq, bq[...])), masked(nt(gk, bkv[0])), masked(nt(gv, bkv[1]))], axis=1
    )
    pack[0:384, :] = tn(grad_rank, normed_ref[...]).astype(BF)
    for copy in copies[5:]:
        copy.wait()
    grad_normed = (
        nt(gq, wq[...])
        + nt(jnp.concatenate([gk, gv], axis=1), wkv[...])
        + nt(grad_rank, aat[...])
    )
    x = x_ref[...].astype(F32)
    factor = lax.rsqrt(jnp.mean(x * x, axis=1, keepdims=True) + NORM_EPS)
    z = grad_normed * g1_ref[...]
    inner = jnp.mean(z * x, axis=1, keepdims=True)
    gi_ref[...] += factor * (z - x * (factor * factor * inner))
    half = ATT_ROWS // 2
    mine_ref[...] = pack[pl.ds(pl.multiple_of(side * half, 16), half), :]
    send_ref[...] = pack[pl.ds(pl.multiple_of((1 - side) * half, 16), half), :]


def attention_backward(scalars, arrays, weights):
    half = ATT_ROWS // 2
    return pl.pallas_call(
        backward_body,
        out_shape=[shape(TOK_DEV, MODEL_WIDTH, dtype=F32), shape(half, MODEL_WIDTH), shape(half, MODEL_WIDTH)],
        in_specs=[SMEM] + [VMEM] * len(arrays) + [ANY] * 8,
        out_specs=[VMEM] * 3,
        scratch_shapes=[pltpu.VMEM(w.shape, BF) for w in weights]
        + [
            pltpu.VMEM((ATT_ROWS, MODEL_WIDTH), BF),
            pltpu.VMEM((TOK_DEV, MODEL_WIDTH), BF),
            pltpu.VMEM((TOK_DEV, HALF_WIDTH), BF),
            pltpu.VMEM((TOK_DEV, HALF_WIDTH), BF),
            pltpu.SemaphoreType.DMA((8,)),
        ],
        compiler_params=pltpu.CompilerParams(vmem_limit_bytes=VMEM_LIMIT),
        cost_estimate=pl.CostEstimate(flops=6_000_000_000, bytes_accessed=24_000_000, transcendentals=1_000_000),
        name="attention_backward",
    )(scalars, *arrays, *weights)


def expert_body(scalars, *refs, expert, first, last, count, experts):
    refs = list(refs)

    def take(number):
        taken = refs[:number]
        del refs[:number]
        return taken

    x_blocks = take(count)
    g_blocks = take(count)
    ain_h, win_h, bin_h, adn_h, wdn_h, bdn_h = take(6)
    if not first:
        f_in, b_in, c_in = take(3)
    if last:
        (wr_ref,) = take(1)
        f_out, b_out = take(2)
    else:
        f_out, b_out, c_out = take(3)
    mine_ref, send_ref = take(2)
    xs, gs_buf, ain, win, bin_, adn, wdn, bdn, acc_a, acc_bi, acc_ad, acc_bd, pack, xsem, gsem, wsem = refs
    step = pl.program_id(0)
    slot = lax.rem(step, 2)
    early = [
        pltpu.make_async_copy(source.at[expert], target, wsem.at[index])
        for index, (source, target) in enumerate([(ain_h, ain), (win_h, win), (bin_h, bin_)])
    ]
    late = [
        pltpu.make_async_copy(source.at[expert], target, wsem.at[3 + index])
        for index, (source, target) in enumerate([(adn_h, adn), (wdn_h, wdn), (bdn_h, bdn)])
    ]

    def fetch(block):
        pltpu.make_async_copy(x_blocks[block], xs.at[block % 2], xsem.at[block % 2]).start()
        pltpu.make_async_copy(g_blocks[block], gs_buf.at[block % 2], gsem.at[block % 2]).start()

    @pl.when(step == 0)
    def _():
        fetch(0)
        for copy in early + late:
            copy.start()
        for copy in early:
            copy.wait()

    for block in range(1, count):
        @pl.when(step == block - 1)
        def _(block=block):
            fetch(block)

    pltpu.make_async_copy(x_blocks[0], xs.at[slot], xsem.at[slot]).wait()
    pltpu.make_async_copy(g_blocks[0], gs_buf.at[slot], gsem.at[slot]).wait()
    eid = scalars[0]
    side = scalars[1]
    x = xs[slot, :, :MODEL_WIDTH]
    meta = xs[slot, :, MODEL_WIDTH:].astype(F32)
    lane = lanes_of(TOK_DEV)
    adapter = meta[:, 96:97].astype(jnp.int32)
    mask = lane // ADAPTER_RANK == adapter

    def masked(values):
        return jnp.where(mask, values, 0.0).astype(BF)

    gates = jnp.where(lane < experts, meta + pltpu.roll(meta, 96, 1), 0.0)
    here = lane == eid
    gate_e = jnp.sum(jnp.where(here, gates, 0.0), axis=1, keepdims=True)
    low = nn(x, ain[...])
    low_gate = masked(low[:, :LANES])
    low_up = masked(low[:, LANES:])
    gate = nn(x, win[:, :HALF_WIDTH]) + nn(low_gate, bin_[0])
    up = nn(x, win[:, HALF_WIDTH:]) + nn(low_up, bin_[1])
    sig = 1.0 / (1.0 + jnp.exp(-gate))
    silu = gate * sig
    active = (silu * up).astype(BF)

    @pl.when(step == 0)
    def _():
        for copy in late:
            copy.wait()

    down = masked(nn(active, adn[...]))
    grad = gs_buf[slot].astype(F32)
    out = nn(active, wdn[...]) + nn(down, bdn[...])
    grad_gate_e = jnp.sum(out * grad, axis=1, keepdims=True)
    weighted = gate_e * out
    if not first:
        weighted = weighted + f_in[...].astype(F32)
    f_out[...] = weighted.astype(f_out.dtype)
    slot_grad = (gate_e * grad).astype(BF)
    grad_down = masked(nt(slot_grad, bdn[...]))
    grad_active = nt(slot_grad, wdn[...]) + nt(grad_down, adn[...])
    gate_grad = (grad_active * up * sig * (1.0 + gate * (1.0 - sig))).astype(BF)
    up_grad = (grad_active * silu).astype(BF)
    grad_low = jnp.concatenate([masked(nt(gate_grad, bin_[0])), masked(nt(up_grad, bin_[1]))], axis=1)
    both_grads = jnp.concatenate([gate_grad, up_grad], axis=1)
    rows = nt(both_grads, win[...]) + nt(grad_low, ain[...])
    part = (gate_e * grad_gate_e) * (jnp.where(here, 1.0, 0.0) - gates)
    if not first:
        rows = rows + b_in[...].astype(F32)
        part = part + c_in[...]
    if last:
        rows = rows + nt(part.astype(BF), wr_ref[...])
    else:
        c_out[...] = part
    b_out[...] = rows.astype(b_out.dtype)
    grads = [
        tn(grad_low, x),
        jnp.concatenate([tn(low_gate, gate_grad), tn(low_up, up_grad)], axis=1),
        tn(grad_down, active),
        tn(down, slot_grad),
    ]
    sums = [acc_a, acc_bi, acc_ad, acc_bd]

    @pl.when(step == 0)
    def _():
        for total, value in zip(sums, grads):
            total[...] = value

    @pl.when(step > 0)
    def _():
        for total, value in zip(sums, grads):
            total[...] += value

    @pl.when(step == count - 1)
    def _():
        pack[0:256, :] = acc_a[...].astype(BF)
        pack[256:384, :] = acc_bi[...].astype(BF)
        pack[384:512, :] = acc_bd[...].astype(BF)
        pack[512:576, :HALF_WIDTH] = acc_ad[0:64, :].astype(BF)
        pack[512:576, HALF_WIDTH:] = acc_ad[64:128, :].astype(BF)
        half = PACK_ROWS // 2
        mine_ref[...] = pack[pl.ds(pl.multiple_of(side * half, 16), half), :]
        send_ref[...] = pack[pl.ds(pl.multiple_of((1 - side) * half, 16), half), :]


def expert_call(expert, scalars, x_blocks, g_blocks, weights, carried, router_wide, experts):
    count = len(x_blocks)
    total = count * TOK_DEV
    first = carried is None
    last = router_wide is not None
    rows = lambda width: pl.BlockSpec((TOK_DEV, width), lambda i, *_: (i, 0))
    whole = lambda *dims: pl.BlockSpec(dims, lambda i, *_: (0,) * len(dims), pipeline_mode=pl.Buffered(1))
    in_specs = [ANY] * (2 * count + 6)
    args = [*x_blocks, *g_blocks, *weights]
    if not first:
        in_specs += [rows(MODEL_WIDTH), rows(MODEL_WIDTH), rows(LANES)]
        args += list(carried)
    if last:
        in_specs.append(whole(MODEL_WIDTH, LANES))
        args.append(router_wide)
    kind = BF if last else F32
    outs = [shape(total, MODEL_WIDTH, dtype=kind), shape(total, MODEL_WIDTH, dtype=kind)]
    out_specs = [rows(MODEL_WIDTH), rows(MODEL_WIDTH)]
    if not last:
        outs.append(shape(total, LANES, dtype=F32))
        out_specs.append(rows(LANES))
    half = PACK_ROWS // 2
    for _ in range(2):
        outs.append(shape(half, MODEL_WIDTH))
        out_specs.append(pl.BlockSpec((half, MODEL_WIDTH), lambda i, *_: (0, 0)))
    scratch = [pltpu.VMEM((2, TOK_DEV, META), BF), pltpu.VMEM((2, TOK_DEV, MODEL_WIDTH), BF)]
    scratch += [pltpu.VMEM(w.shape[1:], BF) for w in weights]
    scratch += [
        pltpu.VMEM((256, MODEL_WIDTH), F32),
        pltpu.VMEM((128, MODEL_WIDTH), F32),
        pltpu.VMEM((128, HALF_WIDTH), F32),
        pltpu.VMEM((128, MODEL_WIDTH), F32),
        pltpu.VMEM((PACK_ROWS, MODEL_WIDTH), BF),
        pltpu.SemaphoreType.DMA((2,)),
        pltpu.SemaphoreType.DMA((2,)),
        pltpu.SemaphoreType.DMA((6,)),
    ]
    return pl.pallas_call(
        functools.partial(
            expert_body, expert=expert, first=first, last=last, count=count, experts=experts
        ),
        out_shape=outs,
        grid_spec=pltpu.PrefetchScalarGridSpec(
            num_scalar_prefetch=1, grid=(count,), in_specs=in_specs, out_specs=out_specs, scratch_shapes=scratch
        ),
        compiler_params=pltpu.CompilerParams(
            dimension_semantics=("arbitrary",), vmem_limit_bytes=VMEM_LIMIT
        ),
        cost_estimate=pl.CostEstimate(
            flops=total * 9_800_000, bytes_accessed=20_000_000, transcendentals=total * 512
        ),
        name="expert_step",
    )(scalars, *args)


def expert_finish_body(scalars, *refs):
    pieces = refs[: 2 * EXP_DEV]
    a_in, b_in, a_down, b_down, pack = refs[2 * EXP_DEV :]
    side = scalars[0]
    half = PACK_ROWS // 2
    step = pl.program_id(0)
    for expert in range(EXP_DEV):
        @pl.when(step == expert)
        def _(expert=expert):
            pack[pl.ds(pl.multiple_of(side * half, 16), half), :] = pieces[2 * expert][...]
            pack[pl.ds(pl.multiple_of((1 - side) * half, 16), half), :] = pieces[2 * expert + 1][...]
    a_in[0] = pack[0:256, :].astype(F32).T
    b_in[0, 0] = pack[256:384, :HALF_WIDTH].astype(F32)
    b_in[0, 1] = pack[256:384, HALF_WIDTH:].astype(F32)
    b_down[0] = pack[384:512, :].astype(F32)
    a_down[0] = jnp.concatenate([pack[512:576, :HALF_WIDTH], pack[512:576, HALF_WIDTH:]], axis=0).astype(F32).T


def expert_finish(side, pieces):
    half = PACK_ROWS // 2
    block = lambda *dims: pl.BlockSpec((1,) + dims, lambda i, *_: (i,) + (0,) * len(dims))
    dims = [(MODEL_WIDTH, 256), (2, 128, HALF_WIDTH), (HALF_WIDTH, 128), (128, MODEL_WIDTH)]
    return pl.pallas_call(
        expert_finish_body,
        out_shape=[shape(EXP_DEV, *d, dtype=F32) for d in dims],
        grid_spec=pltpu.PrefetchScalarGridSpec(
            num_scalar_prefetch=1,
            grid=(EXP_DEV,),
            in_specs=[
                pl.BlockSpec((half, MODEL_WIDTH), lambda i, *_: (0, 0), pipeline_mode=pl.Buffered(1))
            ] * (2 * EXP_DEV),
            out_specs=[block(*d) for d in dims],
            scratch_shapes=[pltpu.VMEM((PACK_ROWS, MODEL_WIDTH), BF)],
        ),
        compiler_params=pltpu.CompilerParams(
            dimension_semantics=("arbitrary",), vmem_limit_bytes=VMEM_LIMIT
        ),
        cost_estimate=pl.CostEstimate(flops=1_000_000, bytes_accessed=15_000_000, transcendentals=0),
        name="expert_finish",
    )(side, *pieces)


def attention_finish_body(scalars, mine_ref, got_ref, a_ref, bq_ref, bkv_ref, oa_ref, ob_ref, pack):
    side = scalars[0]
    half = ATT_ROWS // 2
    pack[pl.ds(pl.multiple_of(side * half, 16), half), :] = mine_ref[...]
    pack[pl.ds(pl.multiple_of((1 - side) * half, 16), half), :] = got_ref[...]
    a_ref[...] = pack[0:384, :].astype(F32).T
    bq_ref[...] = pack[384:512, :].astype(F32)
    bkv_ref[0] = pack[512:640, :HALF_WIDTH].astype(F32)
    bkv_ref[1] = pack[512:640, HALF_WIDTH:].astype(F32)
    oa_ref[...] = pack[640:768, :].astype(F32).T
    ob_ref[...] = pack[768:896, :].astype(F32)


def attention_finish(side, mine, got):
    dims = [(MODEL_WIDTH, 384), (128, MODEL_WIDTH), (2, 128, HALF_WIDTH), (MODEL_WIDTH, 128), (128, MODEL_WIDTH)]
    return pl.pallas_call(
        attention_finish_body,
        out_shape=[shape(*d, dtype=F32) for d in dims],
        in_specs=[SMEM, VMEM, VMEM],
        out_specs=[VMEM] * 5,
        scratch_shapes=[pltpu.VMEM((ATT_ROWS, MODEL_WIDTH), BF)],
        compiler_params=pltpu.CompilerParams(vmem_limit_bytes=VMEM_LIMIT),
        cost_estimate=pl.CostEstimate(flops=1_000_000, bytes_accessed=6_000_000, transcendentals=0),
        name="attention_finish",
    )(side, mine, got)


def swap(values, axis, bit):
    size = lax.axis_size(axis)
    return lax.ppermute(values, axis, [(i, i ^ (1 << bit)) for i in range(size)])


def axis_bits(axis):
    return lax.axis_size(axis).bit_length() - 1


def gather_blocks(values):
    blocks = [values]
    for bit in reversed(range(axis_bits("expert"))):
        blocks = blocks + [swap(block, "expert", bit) for block in blocks]
    return blocks


def return_stages(partial):
    for bit in range(axis_bits("expert")):
        half = partial.shape[0] // 2
        got = swap(partial[half:], "expert", bit)
        if half == TOK_DEV:
            return partial[:half], got
        partial = (partial[:half].astype(F32) + got.astype(F32)).astype(BF)


class Sum:
    def __init__(self, mine, send, stages):
        self.path = []
        self.stages = list(stages)
        self.mine = mine
        self.send = send
        self.begin(True)

    def begin(self, halved):
        axis, bit = self.stages.pop(0)
        self.path.append((axis, bit, halved))
        self.got = swap(self.send, axis, bit)

    def split(self, values):
        axis, bit = self.stages[0]
        rows, width = values.shape
        if rows % 16:
            self.mine = self.send = values
            return False
        side = (lax.axis_index(axis) >> bit) & 1
        halves = values.reshape(2, rows // 2, width)
        self.mine = lax.dynamic_index_in_dim(halves, side, 0, keepdims=False)
        self.send = lax.dynamic_index_in_dim(halves, 1 - side, 0, keepdims=False)
        return True

    def advance(self):
        if self.stages:
            values = (self.mine.astype(F32) + self.got.astype(F32)).astype(BF)
            halved = self.split(values)
            self.begin(halved)
            return
        if self.path[-1][2] is not None:
            self.values = (self.mine.astype(F32) + self.got.astype(F32)).astype(BF)
            while not self.path[-1][2]:
                self.path.pop()
            self.path.append((None, None, None))
        else:
            self.path.pop()
            axis, bit, _ = self.path.pop()
            side = (lax.axis_index(axis) >> bit) & 1
            low = jnp.where(side == 0, self.values, self.got)
            high = jnp.where(side == 0, self.got, self.values)
            self.values = jnp.concatenate([low, high], axis=0)
            self.path.append((None, None, None))
        axis, bit, _ = self.path[-2]
        self.got = swap(self.values, axis, bit)

    def pending(self):
        return bool(self.stages) or self.path[-1][2] is not None or len(self.path) > 2

    def finish(self):
        while self.pending():
            self.advance()
        return self.values, self.got


def tie(first, second):
    return lax.optimization_barrier((first, second))


def on_device(
    inputs,
    lengths,
    routes,
    adapter_of_sequence,
    first_norm_gain,
    query_weight,
    key_value_weight,
    output_weight,
    second_norm_gain,
    router_weight,
    expert_input_weight,
    expert_down_weight,
    attention_first_factors,
    query_second_factors,
    key_value_second_factors,
    output_first_factors,
    output_second_factors,
    expert_input_first_factors,
    expert_input_second_factors,
    expert_down_first_factors,
    expert_down_second_factors,
    output_gradient,
):
    experts = EXP_DEV * lax.axis_size("expert")
    place = lax.axis_index("expert")
    dp_side = lax.axis_index("dp") & 1
    core_side = place & 1
    grad_blocks = gather_blocks(output_gradient)
    cosine, sine = rope_tables()
    scalars = jnp.stack([adapter_of_sequence[0], lengths[0], core_side]).astype(jnp.int32)
    g1 = first_norm_gain[None]
    g2 = second_norm_gain[None]
    weights = [
        attention_first_factors,
        query_weight,
        query_second_factors,
        key_value_weight,
        key_value_second_factors,
        output_first_factors,
        output_weight,
        output_second_factors,
    ]
    hidden, payload, normed, lowrank, queries, keys, values, attended, out_rank, router_wide = attention_forward(
        scalars, inputs, g1, g2, cosine, sine, routes, router_weight, weights
    )
    row_blocks = gather_blocks(payload)
    expert_weights = [
        expert_input_first_factors,
        expert_input_weight,
        expert_input_second_factors,
        expert_down_first_factors,
        expert_down_weight,
        expert_down_second_factors,
    ]
    dp_stages = [("dp", bit) for bit in range(axis_bits("dp"))]
    carried = None
    sums = []
    for local in range(EXP_DEV):
        number = jnp.stack([EXP_DEV * place + local, dp_side]).astype(jnp.int32)
        for older in sums[: max(local - 1, 0)]:
            older.got, number = tie(older.got, number)
            older.advance()
        *carried, mine, send = expert_call(
            local,
            number,
            row_blocks,
            grad_blocks,
            expert_weights,
            carried,
            router_wide if local == EXP_DEV - 1 else None,
            experts,
        )
        sums.append(Sum(mine, send, dp_stages))
    mixture_part, row_part = carried
    row_mine, row_got = return_stages(row_part)
    grad_input, att_mine, att_send = attention_backward(
        scalars,
        [inputs, g1, g2, cosine, sine, hidden, row_mine, row_got, output_gradient]
        + [normed, lowrank, queries, keys, values, attended, out_rank],
        weights,
    )
    mix_mine, mix_got = return_stages(mixture_part)
    live = (jnp.arange(TOK_DEV, dtype=jnp.int32) < lengths[0]).astype(F32)[:, None]
    output = (live * (hidden + mix_mine.astype(F32) + mix_got.astype(F32))).astype(BF)
    stages = [("expert", bit) for bit in range(axis_bits("expert"))] + dp_stages
    attention_sum = Sum(att_mine, att_send, stages).finish()
    pieces = [piece for one in sums for piece in one.finish()]
    expert_grads = expert_finish(dp_side[None].astype(jnp.int32), pieces)
    attention_grads = attention_finish(core_side[None].astype(jnp.int32), *attention_sum)
    return (output, grad_input, *attention_grads, *expert_grads)


def solution(mesh):
    rows = P(("dp", "expert"), None)
    each = P(("dp", "expert"))
    three = P("expert", None, None)
    four = P("expert", None, None, None)
    return jax.shard_map(
        on_device,
        mesh=mesh,
        in_specs=(
            (rows, each, rows, each)
            + (P(),) * 6
            + (three, three)
            + (P(),) * 5
            + (three, four, three, three, rows)
        ),
        out_specs=(rows, rows) + (P(),) * 5 + (three, four, three, three),
        check_vma=False,
    )
```

```python
import functools

import jax
import jax.numpy as jnp
import numpy as np
from jax import lax
from jax.experimental import pallas as pl
from jax.experimental.pallas import tpu as pltpu
from jax.sharding import PartitionSpec as P

MODEL_WIDTH = 1024
HALF_WIDTH = 512
HEAD_WIDTH = 64
ADAPTER_RANK = 16
TOK_DEV = 256
EXP_DEV = 4
LANES = 128
META = MODEL_WIDTH + LANES
PACK_ROWS = 576
ATT_ROWS = 896
NORM_EPS = 1e-06
ROPE_BASE = 10000.0
F32 = jnp.float32
BF = jnp.bfloat16
ANY = pl.BlockSpec(memory_space=pl.ANY)
SMEM = pl.BlockSpec(memory_space=pltpu.SMEM)
VMEM = pl.BlockSpec(memory_space=pltpu.VMEM)
VMEM_LIMIT = 60 * 1024 * 1024


def nn(a, b):
    return lax.dot_general(a, b, (((1,), (0,)), ((), ())), preferred_element_type=F32)


def nt(a, b):
    return lax.dot_general(a, b, (((1,), (1,)), ((), ())), preferred_element_type=F32)


def tn(a, b):
    return lax.dot_general(a, b, (((0,), (0,)), ((), ())), preferred_element_type=F32)


def shape(*dims, dtype=BF):
    return jax.ShapeDtypeStruct(dims, dtype)


def rope_tables():
    inverse = ROPE_BASE ** (-2.0 * np.arange(HEAD_WIDTH // 2, dtype=np.float64) / HEAD_WIDTH)
    angles = np.arange(TOK_DEV, dtype=np.float64)[:, None] * inverse[None, :]
    cosine = np.tile(np.cos(angles), (1, 4)).astype(np.float32)
    sine = np.sin(angles)
    signed = np.concatenate([-sine, sine, -sine, sine], axis=1).astype(np.float32)
    return cosine, signed


def lanes_of(rows):
    return lax.broadcasted_iota(jnp.int32, (rows, LANES), 1)


def swap_halves(block):
    first = lanes_of(block.shape[0]) % HEAD_WIDTH < HEAD_WIDTH // 2
    return jnp.where(first, pltpu.roll(block, LANES - 32, 1), pltpu.roll(block, 32, 1))


def both(block, odd):
    low = lanes_of(block.shape[0]) < HEAD_WIDTH
    wide = block.astype(F32)
    other = pltpu.roll(wide, HEAD_WIDTH, 1)
    return (jnp.where(low, other, wide) if odd else jnp.where(low, wide, other)).astype(BF)


def stacked(block):
    low = lanes_of(block.shape[0]) < HEAD_WIDTH
    wide = block.astype(F32)
    return jnp.concatenate(
        [jnp.where(low, wide, 0.0).astype(BF), jnp.where(low, 0.0, wide).astype(BF)], axis=0
    )


def unstacked(pair):
    low = lanes_of(TOK_DEV) < HEAD_WIDTH
    return jnp.where(low, pair[:TOK_DEV], pair[TOK_DEV:])


def allowed_keys(length):
    row = lax.broadcasted_iota(jnp.int32, (2 * TOK_DEV, TOK_DEV), 0) % TOK_DEV
    col = lax.broadcasted_iota(jnp.int32, (2 * TOK_DEV, TOK_DEV), 1)
    return (col <= row) & (col < length)


def softmax(query_pair, key_both, allowed):
    scores = jnp.where(allowed, nt(query_pair, key_both) * (HEAD_WIDTH**-0.5), -1e30)
    exponent = jnp.exp(scores - jnp.max(scores, axis=1, keepdims=True))
    return exponent * (1.0 / jnp.sum(exponent, axis=1, keepdims=True))


def column(index):
    return slice(index * LANES, (index + 1) * LANES)


def forward_body(
    scalars, x_ref, g1_ref, g2_ref, cos_ref, sin_ref, routes_ref, router_ref,
    aat_h, wq_h, bq_h, wkv_h, bkv_h, ao_h, wo_h, bo_h,
    hidden_ref, payload_ref, normed_ref, lowrank_ref, q_ref, k_ref, v_ref, att_ref, orank_ref, wide_ref,
    aat, wq, bq, wkv, bkv, ao, wo, bo, sems, *, experts,
):
    copies = [
        pltpu.make_async_copy(source, target, sems.at[index])
        for index, (source, target) in enumerate(
            [(aat_h, aat), (wq_h, wq), (bq_h, bq), (wkv_h, wkv), (bkv_h, bkv), (ao_h, ao), (wo_h, wo), (bo_h, bo)]
        )
    ]
    for copy in copies:
        copy.start()
    adapter = scalars[0]
    length = scalars[1]
    lane = lanes_of(TOK_DEV)
    mask = lane // ADAPTER_RANK == adapter
    x = x_ref[...].astype(F32)
    factor = lax.rsqrt(jnp.mean(x * x, axis=1, keepdims=True) + NORM_EPS)
    normed = (x * factor * g1_ref[...]).astype(BF)
    normed_ref[...] = normed
    copies[0].wait()
    low = nn(normed, aat[...])
    ranks = [jnp.where(mask, low[:, column(i)], 0.0).astype(BF) for i in range(3)]
    for i in range(3):
        lowrank_ref[:, column(i)] = ranks[i]
    cosine = cos_ref[...]
    sine = sin_ref[...]
    copies[1].wait()
    copies[2].wait()
    query_pre = nn(normed, wq[...]) + nn(ranks[0], bq[...])
    for j in range(8):
        block = query_pre[:, column(j)]
        q_ref[:, column(j)] = (block * cosine + swap_halves(block) * sine).astype(BF)
    copies[3].wait()
    copies[4].wait()
    pre = nn(normed, wkv[...])
    key_pre = pre[:, :HALF_WIDTH] + nn(ranks[1], bkv[0])
    v_ref[...] = (pre[:, HALF_WIDTH:] + nn(ranks[2], bkv[1])).astype(BF)
    for j in range(4):
        block = key_pre[:, column(j)]
        k_ref[:, column(j)] = (block * cosine + swap_halves(block) * sine).astype(BF)
    allowed = allowed_keys(length)
    for j in range(8):
        pair = stacked(q_ref[:, column(j)])
        probs = softmax(pair, both(k_ref[:, column(j // 2)], j % 2), allowed).astype(BF)
        att_ref[:, column(j)] = unstacked(nn(probs, both(v_ref[:, column(j // 2)], j % 2))).astype(BF)
    attended = att_ref[...]
    for copy in copies[5:]:
        copy.wait()
    orank = jnp.where(mask, nn(attended, ao[...]), 0.0).astype(BF)
    orank_ref[...] = orank
    hidden = x + nn(attended, wo[...]) + nn(orank, bo[...])
    hidden_ref[...] = hidden
    factor2 = lax.rsqrt(jnp.mean(hidden * hidden, axis=1, keepdims=True) + NORM_EPS)
    normed2 = (hidden * factor2 * g2_ref[...]).astype(BF)
    spread = jnp.where(
        lax.broadcasted_iota(jnp.int32, (experts, LANES), 0)
        == lax.broadcasted_iota(jnp.int32, (experts, LANES), 1), 1.0, 0.0,
    ).astype(BF)
    wide = tn(router_ref[...], spread).astype(BF)
    wide_ref[...] = wide
    logits = nn(normed2, wide)
    routes = routes_ref[...]
    number = lax.broadcasted_iota(jnp.int32, (LANES, TOK_DEV), 0)
    named = routes[0:1, :] == number
    for k in range(1, routes.shape[0]):
        named = named | (routes[k : k + 1, :] == number)
    selected = jnp.where(named, 1.0, 0.0).T > 0.5
    top = jnp.max(jnp.where(selected, logits, -1e30), axis=1, keepdims=True)
    chosen = jnp.where(selected, jnp.exp(jnp.minimum(logits - top, 0.0)), 0.0)
    live = lax.broadcasted_iota(jnp.int32, (TOK_DEV, 1), 0) < length
    gates = chosen * jnp.where(live, 1.0 / jnp.sum(chosen, axis=1, keepdims=True), 0.0)
    high = gates.astype(BF).astype(F32)
    meta = high + pltpu.roll(gates - high, 32, 1) + jnp.where(lane >= 96, adapter.astype(F32), 0.0)
    payload_ref[:, :MODEL_WIDTH] = normed2
    payload_ref[:, MODEL_WIDTH:] = meta.astype(BF)


def attention_forward(scalars, x, g1, g2, cosine, sine, routes, router, weights):
    experts = router.shape[0]
    return pl.pallas_call(
        functools.partial(forward_body, experts=experts),
        out_shape=[
            shape(TOK_DEV, MODEL_WIDTH, dtype=F32),
            shape(TOK_DEV, META),
            shape(TOK_DEV, MODEL_WIDTH),
            shape(TOK_DEV, 3 * LANES),
            shape(TOK_DEV, MODEL_WIDTH),
            shape(TOK_DEV, HALF_WIDTH),
            shape(TOK_DEV, HALF_WIDTH),
            shape(TOK_DEV, MODEL_WIDTH),
            shape(TOK_DEV, LANES),
            shape(MODEL_WIDTH, LANES),
        ],
        in_specs=[SMEM] + [VMEM] * 7 + [ANY] * 8,
        out_specs=[VMEM] * 10,
        scratch_shapes=[pltpu.VMEM(w.shape, BF) for w in weights] + [pltpu.SemaphoreType.DMA((8,))],
        compiler_params=pltpu.CompilerParams(vmem_limit_bytes=VMEM_LIMIT),
        cost_estimate=pl.CostEstimate(flops=3_000_000_000, bytes_accessed=20_000_000, transcendentals=1_000_000),
        name="attention_forward",
    )(scalars, x, g1, g2, cosine, sine, routes, router, *weights)


def backward_body(
    scalars, x_ref, g1_ref, g2_ref, cos_ref, sin_ref, hidden_ref, keep_ref, got_ref, og_ref,
    normed_ref, lowrank_ref, q_ref, k_ref, v_ref, att_ref, orank_ref,
    aat_h, wq_h, bq_h, wkv_h, bkv_h, ao_h, wo_h, bo_h,
    gi_ref, mine_ref, send_ref,
    aat, wq, bq, wkv, bkv, ao, wo, bo, pack, gq_s, gk_s, gv_s, sems,
):
    order = [(bo_h, bo), (wo_h, wo), (ao_h, ao), (bq_h, bq), (bkv_h, bkv), (wq_h, wq), (wkv_h, wkv), (aat_h, aat)]
    copies = [
        pltpu.make_async_copy(source, target, sems.at[index]) for index, (source, target) in enumerate(order)
    ]
    for copy in copies:
        copy.start()
    adapter = scalars[0]
    length = scalars[1]
    side = scalars[2]
    mask = lanes_of(TOK_DEV) // ADAPTER_RANK == adapter

    def masked(values):
        return jnp.where(mask, values, 0.0).astype(BF)

    hidden = hidden_ref[...]
    factor2 = lax.rsqrt(jnp.mean(hidden * hidden, axis=1, keepdims=True) + NORM_EPS)
    live = lax.broadcasted_iota(jnp.int32, (TOK_DEV, 1), 0) < length
    grad_live = jnp.where(live, og_ref[...].astype(F32), 0.0)
    y = (keep_ref[...].astype(F32) + got_ref[...].astype(F32)) * g2_ref[...]
    inner = jnp.mean(y * hidden, axis=1, keepdims=True)
    grad_hidden = grad_live + factor2 * (y - hidden * (factor2 * factor2 * inner))
    gi_ref[...] = grad_hidden
    branch = grad_hidden.astype(BF)
    pack[768:896, :] = tn(orank_ref[...], branch).astype(BF)
    for copy in copies[:3]:
        copy.wait()
    grad_orank = masked(nt(branch, bo[...]))
    pack[640:768, :] = tn(grad_orank, att_ref[...]).astype(BF)
    grad_att = (nt(branch, wo[...]) + nt(grad_orank, ao[...])).astype(BF)
    allowed = allowed_keys(length)
    cosine = cos_ref[...]
    sine = sin_ref[...]
    low = lanes_of(TOK_DEV) < HEAD_WIDTH
    scale = HEAD_WIDTH**-0.5
    kept = None
    for j in range(8):
        pair = stacked(q_ref[:, column(j)])
        key_both = both(k_ref[:, column(j // 2)], j % 2)
        value_both = both(v_ref[:, column(j // 2)], j % 2)
        probs = softmax(pair, key_both, allowed)
        grad_pair = stacked(grad_att[:, column(j)])
        grad_probs = nt(grad_pair, value_both).astype(BF).astype(F32)
        grad_v = tn(probs.astype(BF), grad_pair)
        scores = (probs * (grad_probs - jnp.sum(grad_probs * probs, axis=1, keepdims=True))).astype(BF)
        grad_q = unstacked(nn(scores, key_both)) * scale
        gq_s[:, column(j)] = (grad_q * cosine - swap_halves(grad_q) * sine).astype(BF)
        grad_k = tn(scores, pair) * scale
        grad_v = grad_v + pltpu.roll(grad_v, HEAD_WIDTH, 1)
        grad_k = grad_k + pltpu.roll(grad_k, HEAD_WIDTH, 1)
        if j % 2 == 0:
            kept = (grad_k, grad_v)
        else:
            block = jnp.where(low, kept[0], grad_k)
            gk_s[:, column(j // 2)] = (block * cosine - swap_halves(block) * sine).astype(BF)
            gv_s[:, column(j // 2)] = jnp.where(low, kept[1], grad_v).astype(BF)
    gq = gq_s[...]
    gk = gk_s[...]
    gv = gv_s[...]
    pack[384:512, :] = tn(lowrank_ref[:, column(0)], gq).astype(BF)
    pack[512:640, :HALF_WIDTH] = tn(lowrank_ref[:, column(1)], gk).astype(BF)
    pack[512:640, HALF_WIDTH:] = tn(lowrank_ref[:, column(2)], gv).astype(BF)
    copies[3].wait()
    copies[4].wait()
    grad_rank = jnp.concatenate(
        [masked(nt(gq, bq[...])), masked(nt(gk, bkv[0])), masked(nt(gv, bkv[1]))], axis=1
    )
    pack[0:384, :] = tn(grad_rank, normed_ref[...]).astype(BF)
    for copy in copies[5:]:
        copy.wait()
    grad_normed = (
        nt(gq, wq[...])
        + nt(jnp.concatenate([gk, gv], axis=1), wkv[...])
        + nt(grad_rank, aat[...])
    )
    x = x_ref[...].astype(F32)
    factor = lax.rsqrt(jnp.mean(x * x, axis=1, keepdims=True) + NORM_EPS)
    z = grad_normed * g1_ref[...]
    inner = jnp.mean(z * x, axis=1, keepdims=True)
    gi_ref[...] += factor * (z - x * (factor * factor * inner))
    half = ATT_ROWS // 2
    mine_ref[...] = pack[pl.ds(pl.multiple_of(side * half, 16), half), :]
    send_ref[...] = pack[pl.ds(pl.multiple_of((1 - side) * half, 16), half), :]


def attention_backward(scalars, arrays, weights):
    half = ATT_ROWS // 2
    return pl.pallas_call(
        backward_body,
        out_shape=[shape(TOK_DEV, MODEL_WIDTH, dtype=F32), shape(half, MODEL_WIDTH), shape(half, MODEL_WIDTH)],
        in_specs=[SMEM] + [VMEM] * len(arrays) + [ANY] * 8,
        out_specs=[VMEM] * 3,
        scratch_shapes=[pltpu.VMEM(w.shape, BF) for w in weights]
        + [
            pltpu.VMEM((ATT_ROWS, MODEL_WIDTH), BF),
            pltpu.VMEM((TOK_DEV, MODEL_WIDTH), BF),
            pltpu.VMEM((TOK_DEV, HALF_WIDTH), BF),
            pltpu.VMEM((TOK_DEV, HALF_WIDTH), BF),
            pltpu.SemaphoreType.DMA((8,)),
        ],
        compiler_params=pltpu.CompilerParams(vmem_limit_bytes=VMEM_LIMIT),
        cost_estimate=pl.CostEstimate(flops=6_000_000_000, bytes_accessed=24_000_000, transcendentals=1_000_000),
        name="attention_backward",
    )(scalars, *arrays, *weights)


def expert_body(
    scalars, *refs, expert, start, count, blocks, experts, carried, seeded, emit, last,
):
    refs = list(refs)

    def take(number):
        taken = refs[:number]
        del refs[:number]
        return taken

    x_blocks = take(count)
    g_blocks = take(count)
    ain_h, win_h, bin_h, adn_h, wdn_h, bdn_h = take(6)
    if carried:
        f_in, b_in, c_in = take(3)
    if start:
        take(3)
    seeds = take(4) if seeded else None
    if last:
        wr_ref, f_top, f_low, b_top, b_low = take(5)
    else:
        f_out, b_out, c_out = take(3)
    if emit:
        emitted = take(4)
    else:
        mine_ref, send_ref = take(2)
    xs, gs_buf, ain, win, bin_, adn, wdn, bdn, acc_a, acc_bi, acc_ad, acc_bd, pack, xsem, gsem, wsem = refs
    sums = [acc_a, acc_bi, acc_ad, acc_bd]
    step = pl.program_id(0)
    slot = lax.rem(step, 2)
    early = [
        pltpu.make_async_copy(source.at[expert], target, wsem.at[index])
        for index, (source, target) in enumerate([(ain_h, ain), (win_h, win), (bin_h, bin_)])
    ]
    late = [
        pltpu.make_async_copy(source.at[expert], target, wsem.at[3 + index])
        for index, (source, target) in enumerate([(adn_h, adn), (wdn_h, wdn), (bdn_h, bdn)])
    ]

    def fetch(block):
        pltpu.make_async_copy(x_blocks[block], xs.at[block % 2], xsem.at[block % 2]).start()
        pltpu.make_async_copy(g_blocks[block], gs_buf.at[block % 2], gsem.at[block % 2]).start()

    @pl.when(step == 0)
    def _():
        fetch(0)
        for copy in early + late:
            copy.start()
        for index, total in enumerate(sums):
            total[...] = seeds[index][...] if seeded else jnp.zeros_like(total)
        for copy in early:
            copy.wait()

    for block in range(1, count):
        @pl.when(step == block - 1)
        def _(block=block):
            fetch(block)

    pltpu.make_async_copy(x_blocks[0], xs.at[slot], xsem.at[slot]).wait()
    pltpu.make_async_copy(g_blocks[0], gs_buf.at[slot], gsem.at[slot]).wait()
    eid = scalars[0]
    side = scalars[1]
    x = xs[slot, :, :MODEL_WIDTH]
    meta = xs[slot, :, MODEL_WIDTH:].astype(F32)
    lane = lanes_of(TOK_DEV)
    adapter = meta[:, 96:97].astype(jnp.int32)
    mask = lane // ADAPTER_RANK == adapter

    def masked(values):
        return jnp.where(mask, values, 0.0).astype(BF)

    gates = jnp.where(lane < experts, meta + pltpu.roll(meta, 96, 1), 0.0)
    here = lane == eid
    gate_e = jnp.sum(jnp.where(here, gates, 0.0), axis=1, keepdims=True)
    low = nn(x, ain[...])
    low_gate = masked(low[:, :LANES])
    low_up = masked(low[:, LANES:])
    gate = nn(x, win[:, :HALF_WIDTH]) + nn(low_gate, bin_[0])
    up = nn(x, win[:, HALF_WIDTH:]) + nn(low_up, bin_[1])
    sig = 1.0 / (1.0 + jnp.exp(-gate))
    silu = gate * sig
    active = (silu * up).astype(BF)

    @pl.when(step == 0)
    def _():
        for copy in late:
            copy.wait()

    down = masked(nn(active, adn[...]))
    grad = gs_buf[slot].astype(F32)
    out = nn(active, wdn[...]) + nn(down, bdn[...])
    grad_gate_e = jnp.sum(out * grad, axis=1, keepdims=True)
    weighted = gate_e * out
    if carried:
        weighted = weighted + f_in[...]
    if last:
        @pl.when(slot == 0)
        def _():
            f_top[...] = weighted.astype(BF)

        @pl.when(slot == 1)
        def _():
            f_low[...] = weighted.astype(BF)
    else:
        f_out[...] = weighted
    slot_grad = (gate_e * grad).astype(BF)
    grad_down = masked(nt(slot_grad, bdn[...]))
    grad_active = nt(slot_grad, wdn[...]) + nt(grad_down, adn[...])
    gate_grad = (grad_active * up * sig * (1.0 + gate * (1.0 - sig))).astype(BF)
    up_grad = (grad_active * silu).astype(BF)
    grad_low = jnp.concatenate([masked(nt(gate_grad, bin_[0])), masked(nt(up_grad, bin_[1]))], axis=1)
    both_grads = jnp.concatenate([gate_grad, up_grad], axis=1)
    rows = nt(both_grads, win[...]) + nt(grad_low, ain[...])
    part = (gate_e * grad_gate_e) * (jnp.where(here, 1.0, 0.0) - gates)
    if carried:
        rows = rows + b_in[...]
        part = part + c_in[...]
    if last:
        rows = rows + nt(part.astype(BF), wr_ref[...])

        @pl.when(slot == 0)
        def _():
            b_top[...] = rows.astype(BF)

        @pl.when(slot == 1)
        def _():
            b_low[...] = rows.astype(BF)
    else:
        c_out[...] = part
        b_out[...] = rows
    acc_a[...] += tn(grad_low, x)
    acc_bi[:, :HALF_WIDTH] += tn(low_gate, gate_grad)
    acc_bi[:, HALF_WIDTH:] += tn(low_up, up_grad)
    acc_ad[...] += tn(grad_down, active)
    acc_bd[...] += tn(down, slot_grad)

    @pl.when(step == count - 1)
    def _():
        if emit:
            for target, total in zip(emitted, sums):
                target[...] = total[...]
        else:
            pack[0:256, :] = acc_a[...].astype(BF)
            pack[256:384, :] = acc_bi[...].astype(BF)
            pack[384:512, :] = acc_bd[...].astype(BF)
            pack[512:576, :HALF_WIDTH] = acc_ad[0:64, :].astype(BF)
            pack[512:576, HALF_WIDTH:] = acc_ad[64:128, :].astype(BF)
            half = PACK_ROWS // 2
            mine_ref[...] = pack[pl.ds(pl.multiple_of(side * half, 16), half), :]
            send_ref[...] = pack[pl.ds(pl.multiple_of((1 - side) * half, 16), half), :]


def expert_call(
    expert, scalars, x_blocks, g_blocks, weights, experts, blocks, start=0,
    carried=None, halves=None, seeds=None, emit=False, router_wide=None,
):
    count = len(x_blocks)
    total = blocks * TOK_DEV
    last = router_wide is not None
    rows = lambda width: pl.BlockSpec((TOK_DEV, width), lambda i, *_: (i + start, 0))
    pair = lambda width: pl.BlockSpec((TOK_DEV, width), lambda i, *_: (i // 2, 0))
    whole = lambda *dims: pl.BlockSpec(dims, lambda i, *_: (0,) * len(dims), pipeline_mode=pl.Buffered(1))
    fixed = lambda *dims: pl.BlockSpec(dims, lambda i, *_: (0,) * len(dims))
    sum_dims = [(256, MODEL_WIDTH), (128, MODEL_WIDTH), (128, HALF_WIDTH), (128, MODEL_WIDTH)]
    in_specs = [ANY] * (2 * count + 6)
    args = [*x_blocks, *g_blocks, *weights]
    aliases = {}
    if carried is not None:
        in_specs += [rows(MODEL_WIDTH), rows(MODEL_WIDTH), rows(LANES)]
        args += list(carried)
    if start:
        aliases = {1 + len(args) + i: i for i in range(3)}
        in_specs += [ANY] * 3
        args += list(halves)
    if seeds is not None:
        in_specs += [whole(*d) for d in sum_dims]
        args += list(seeds)
    if last:
        in_specs.append(whole(MODEL_WIDTH, LANES))
        args.append(router_wide)
        outs = [shape(total // 2, MODEL_WIDTH)] * 4
        out_specs = [pair(MODEL_WIDTH)] * 4
    else:
        outs = [
            shape(total, MODEL_WIDTH, dtype=F32),
            shape(total, MODEL_WIDTH, dtype=F32),
            shape(total, LANES, dtype=F32),
        ]
        out_specs = [rows(MODEL_WIDTH), rows(MODEL_WIDTH), rows(LANES)]
    half = PACK_ROWS // 2
    if emit:
        outs += [shape(*d, dtype=F32) for d in sum_dims]
        out_specs += [fixed(*d) for d in sum_dims]
    else:
        outs += [shape(half, MODEL_WIDTH)] * 2
        out_specs += [fixed(half, MODEL_WIDTH)] * 2
    scratch = [pltpu.VMEM((2, TOK_DEV, META), BF), pltpu.VMEM((2, TOK_DEV, MODEL_WIDTH), BF)]
    scratch += [pltpu.VMEM(w.shape[1:], BF) for w in weights]
    scratch += [pltpu.VMEM(d, F32) for d in sum_dims]
    scratch += [
        pltpu.VMEM((PACK_ROWS, MODEL_WIDTH), BF),
        pltpu.SemaphoreType.DMA((2,)),
        pltpu.SemaphoreType.DMA((2,)),
        pltpu.SemaphoreType.DMA((6,)),
    ]
    return pl.pallas_call(
        functools.partial(
            expert_body, expert=expert, start=start, count=count, blocks=blocks, experts=experts,
            carried=carried is not None, seeded=seeds is not None, emit=emit, last=last,
        ),
        out_shape=outs,
        grid_spec=pltpu.PrefetchScalarGridSpec(
            num_scalar_prefetch=1, grid=(count,), in_specs=in_specs, out_specs=out_specs, scratch_shapes=scratch
        ),
        input_output_aliases=aliases,
        compiler_params=pltpu.CompilerParams(
            dimension_semantics=("arbitrary",), vmem_limit_bytes=VMEM_LIMIT
        ),
        cost_estimate=pl.CostEstimate(
            flops=count * TOK_DEV * 9_800_000, bytes_accessed=5_000_000 * count, transcendentals=0
        ),
        name="expert_step",
    )(scalars, *args)


def expert_finish_body(scalars, *refs):
    pieces = refs[: 2 * EXP_DEV]
    a_in, b_in, a_down, b_down, pack = refs[2 * EXP_DEV :]
    side = scalars[0]
    half = PACK_ROWS // 2
    step = pl.program_id(0)
    for expert in range(EXP_DEV):
        @pl.when(step == expert)
        def _(expert=expert):
            pack[pl.ds(pl.multiple_of(side * half, 16), half), :] = pieces[2 * expert][...]
            pack[pl.ds(pl.multiple_of((1 - side) * half, 16), half), :] = pieces[2 * expert + 1][...]
    a_in[0] = pack[0:256, :].astype(F32).T
    b_in[0, 0] = pack[256:384, :HALF_WIDTH].astype(F32)
    b_in[0, 1] = pack[256:384, HALF_WIDTH:].astype(F32)
    b_down[0] = pack[384:512, :].astype(F32)
    a_down[0] = jnp.concatenate([pack[512:576, :HALF_WIDTH], pack[512:576, HALF_WIDTH:]], axis=0).astype(F32).T


def expert_finish(side, pieces):
    half = PACK_ROWS // 2
    block = lambda *dims: pl.BlockSpec((1,) + dims, lambda i, *_: (i,) + (0,) * len(dims))
    dims = [(MODEL_WIDTH, 256), (2, 128, HALF_WIDTH), (HALF_WIDTH, 128), (128, MODEL_WIDTH)]
    return pl.pallas_call(
        expert_finish_body,
        out_shape=[shape(EXP_DEV, *d, dtype=F32) for d in dims],
        grid_spec=pltpu.PrefetchScalarGridSpec(
            num_scalar_prefetch=1,
            grid=(EXP_DEV,),
            in_specs=[
                pl.BlockSpec((half, MODEL_WIDTH), lambda i, *_: (0, 0), pipeline_mode=pl.Buffered(1))
            ] * (2 * EXP_DEV),
            out_specs=[block(*d) for d in dims],
            scratch_shapes=[pltpu.VMEM((PACK_ROWS, MODEL_WIDTH), BF)],
        ),
        compiler_params=pltpu.CompilerParams(
            dimension_semantics=("arbitrary",), vmem_limit_bytes=VMEM_LIMIT
        ),
        cost_estimate=pl.CostEstimate(flops=1_000_000, bytes_accessed=15_000_000, transcendentals=0),
        name="expert_finish",
    )(side, *pieces)


def attention_finish_body(scalars, mine_ref, got_ref, a_ref, bq_ref, bkv_ref, oa_ref, ob_ref, pack):
    side = scalars[0]
    half = ATT_ROWS // 2
    pack[pl.ds(pl.multiple_of(side * half, 16), half), :] = mine_ref[...]
    pack[pl.ds(pl.multiple_of((1 - side) * half, 16), half), :] = got_ref[...]
    a_ref[...] = pack[0:384, :].astype(F32).T
    bq_ref[...] = pack[384:512, :].astype(F32)
    bkv_ref[0] = pack[512:640, :HALF_WIDTH].astype(F32)
    bkv_ref[1] = pack[512:640, HALF_WIDTH:].astype(F32)
    oa_ref[...] = pack[640:768, :].astype(F32).T
    ob_ref[...] = pack[768:896, :].astype(F32)


def attention_finish(side, mine, got):
    dims = [(MODEL_WIDTH, 384), (128, MODEL_WIDTH), (2, 128, HALF_WIDTH), (MODEL_WIDTH, 128), (128, MODEL_WIDTH)]
    return pl.pallas_call(
        attention_finish_body,
        out_shape=[shape(*d, dtype=F32) for d in dims],
        in_specs=[SMEM, VMEM, VMEM],
        out_specs=[VMEM] * 5,
        scratch_shapes=[pltpu.VMEM((ATT_ROWS, MODEL_WIDTH), BF)],
        compiler_params=pltpu.CompilerParams(vmem_limit_bytes=VMEM_LIMIT),
        cost_estimate=pl.CostEstimate(flops=1_000_000, bytes_accessed=6_000_000, transcendentals=0),
        name="attention_finish",
    )(side, mine, got)


def swap(values, axis, bit):
    size = lax.axis_size(axis)
    return lax.ppermute(values, axis, [(i, i ^ (1 << bit)) for i in range(size)])


def axis_bits(axis):
    return lax.axis_size(axis).bit_length() - 1


def tie(first, second):
    return lax.optimization_barrier((first, second))


def add(first, second):
    return (first.astype(F32) + second.astype(F32)).astype(BF)


def far_blocks(values):
    blocks = {0: values}
    for bit in reversed(range(1, axis_bits("expert"))):
        for index in list(blocks):
            blocks[index ^ (1 << bit)] = swap(blocks[index], "expert", bit)
    return blocks


def near_blocks(far):
    blocks = []
    for index in sorted(far):
        if index:
            blocks += [far[index], swap(far[index], "expert", 0)]
    return blocks


class Return:
    def __init__(self, top, low):
        self.bits = list(reversed(range(1, axis_bits("expert"))))
        self.mine = top
        self.got = swap(low, "expert", 0)

    def advance(self):
        half = self.mine.shape[0] // 2
        send = add(self.mine[half:], self.got[half:])
        self.mine = add(self.mine[:half], self.got[:half])
        return send

    def launch(self, send):
        self.got = swap(send, "expert", self.bits.pop(0))


class Sum:
    def __init__(self, mine, send, stages):
        self.path = []
        self.stages = list(stages)
        self.mine = mine
        self.send = send
        self.down = True
        self.target = self.stages.pop(0)
        self.path.append(self.target)
        self.launch()

    def launch(self):
        self.got = swap(self.send, *self.target)

    def prepare(self):
        if self.down:
            values = add(self.mine, self.got)
            if self.stages:
                self.target = self.stages.pop(0)
                axis, bit = self.target
                rows, width = values.shape
                if rows % 16:
                    self.mine = self.send = values
                    return
                self.path.append(self.target)
                side = (lax.axis_index(axis) >> bit) & 1
                halves = values.reshape(2, rows // 2, width)
                self.mine = lax.dynamic_index_in_dim(halves, side, 0, keepdims=False)
                self.send = lax.dynamic_index_in_dim(halves, 1 - side, 0, keepdims=False)
                return
            self.down = False
        else:
            axis, bit = self.path.pop()
            side = (lax.axis_index(axis) >> bit) & 1
            low = jnp.where(side == 0, self.mine, self.got)
            high = jnp.where(side == 0, self.got, self.mine)
            values = jnp.concatenate([low, high], axis=0)
        self.target = self.path[-1]
        self.mine = self.send = values

    def pending(self):
        return self.down or len(self.path) > 1

    def step(self):
        if self.pending():
            self.prepare()
            self.launch()


def sync(holders, *extras):
    arrays = tuple(holder.got for holder in holders) + extras
    arrays = lax.optimization_barrier(arrays)
    for holder, got in zip(holders, arrays):
        holder.got = got
    return arrays[len(holders) :]


def on_device(
    inputs,
    lengths,
    routes,
    adapter_of_sequence,
    first_norm_gain,
    query_weight,
    key_value_weight,
    output_weight,
    second_norm_gain,
    router_weight,
    expert_input_weight,
    expert_down_weight,
    attention_first_factors,
    query_second_factors,
    key_value_second_factors,
    output_first_factors,
    output_second_factors,
    expert_input_first_factors,
    expert_input_second_factors,
    expert_down_first_factors,
    expert_down_second_factors,
    output_gradient,
):
    blocks = lax.axis_size("expert")
    experts = EXP_DEV * blocks
    place = lax.axis_index("expert")
    dp_side = lax.axis_index("dp") & 1
    core_side = place & 1
    grad_far = far_blocks(output_gradient)
    cosine, sine = rope_tables()
    scalars = jnp.stack([adapter_of_sequence[0], lengths[0], core_side]).astype(jnp.int32)
    g1 = first_norm_gain[None]
    g2 = second_norm_gain[None]
    weights = [
        attention_first_factors,
        query_weight,
        query_second_factors,
        key_value_weight,
        key_value_second_factors,
        output_first_factors,
        output_weight,
        output_second_factors,
    ]
    hidden, payload, normed, lowrank, queries, keys, values, attended, out_rank, router_wide = attention_forward(
        scalars, inputs, g1, g2, cosine, sine, routes.T, router_weight.T, weights
    )
    for index in grad_far:
        if index:
            grad_far[index], payload = tie(grad_far[index], payload)
    row_far = far_blocks(payload)
    near = [[values, swap(values, "expert", 0)] for values in (payload, output_gradient)]
    expert_weights = [
        expert_input_first_factors,
        expert_input_weight,
        expert_input_second_factors,
        expert_down_first_factors,
        expert_down_weight,
        expert_down_second_factors,
    ]
    dp_stages = [("dp", bit) for bit in range(axis_bits("dp"))]
    sums = []
    first_number = EXP_DEV * place
    number = jnp.stack([first_number, dp_side]).astype(jnp.int32)
    *halves, s0, s1, s2, s3 = expert_call(
        0, number, *near, expert_weights, experts, blocks, emit=True
    )
    for far in (row_far, grad_far):
        for index in far:
            if index:
                far[index], s0 = tie(far[index], s0)
    row_blocks = near[0] + near_blocks(row_far)
    grad_blocks = near[1] + near_blocks(grad_far)
    *carried, mine, send = expert_call(
        0, number, row_blocks[2:], grad_blocks[2:], expert_weights, experts, blocks,
        start=2, halves=halves, seeds=(s0, s1, s2, s3),
    )
    sums.append(Sum(mine, send, dp_stages))
    for local in range(1, EXP_DEV):
        number = jnp.stack([first_number + local, dp_side]).astype(jnp.int32)
        (number,) = sync(sums[: local - 1], number)
        for older in sums[: local - 1]:
            older.step()
        *carried, mine, send = expert_call(
            local, number, row_blocks, grad_blocks, expert_weights, experts, blocks, carried=carried,
            router_wide=router_wide if local == EXP_DEV - 1 else None,
        )
        if local < EXP_DEV - 1:
            sums.append(Sum(mine, send, dp_stages))
    mix_top, mix_low, row_top, row_low = carried
    (row_low,) = sync(sums, row_low)
    row = Return(row_top, row_low)
    last_sum = Sum(mine, send, dp_stages)
    for one in sums:
        one.step()
    sums.append(last_sum)
    mix = Return(mix_top, mix_low)
    while row.bits:
        row.launch(row.advance())
    sync(sums + [row, mix])
    while mix.bits:
        mix.launch(mix.advance())
    for one in sums:
        one.step()
    grad_input, att_mine, att_send = attention_backward(
        scalars,
        [inputs, g1, g2, cosine, sine, hidden, row.mine, row.got, output_gradient]
        + [normed, lowrank, queries, keys, values, attended, out_rank],
        weights,
    )
    (att_send,) = sync(sums + [mix], att_send)
    stages = [("expert", bit) for bit in range(axis_bits("expert"))] + dp_stages
    total = Sum(att_mine, att_send, stages)
    for one in sums:
        one.step()
    turn = 0
    while total.pending() and (len(total.path) > 2 or total.down):
        total.step()
        turn += 1
        if turn % 2 and any(one.pending() for one in sums):
            sync(sums + [total])
            for one in sums:
                one.step()
    while any(one.pending() for one in sums):
        sync(sums)
        for one in sums:
            one.step()
    sync(sums)
    pieces = [piece for one in sums for piece in (one.mine, one.got)]
    expert_grads = list(expert_finish(dp_side[None].astype(jnp.int32), pieces))
    expert_grads[0], total.got = tie(expert_grads[0], total.got)
    total.step()
    live = (jnp.arange(TOK_DEV, dtype=jnp.int32) < lengths[0]).astype(F32)[:, None]
    output = (live * (hidden + mix.mine.astype(F32) + mix.got.astype(F32))).astype(BF)
    side = core_side[None].astype(jnp.int32)
    attention_grads = attention_finish(side, total.mine, total.got)
    return (output, grad_input, *attention_grads, *expert_grads)


def solution(mesh):
    rows = P(("dp", "expert"), None)
    each = P(("dp", "expert"))
    three = P("expert", None, None)
    four = P("expert", None, None, None)
    return jax.shard_map(
        on_device,
        mesh=mesh,
        in_specs=(
            (rows, each, rows, each)
            + (P(),) * 6
            + (three, three)
            + (P(),) * 5
            + (three, four, three, three, rows)
        ),
        out_specs=(rows, rows) + (P(),) * 5 + (three, four, three, three),
        check_vma=False,
    )
```

```python
import functools

import jax
import jax.numpy as jnp
import numpy as np
from jax import lax
from jax.experimental import pallas as pl
from jax.experimental.pallas import tpu as pltpu
from jax.sharding import PartitionSpec as P

MODEL_WIDTH = 1024
HALF_WIDTH = 512
HEAD_WIDTH = 64
ADAPTER_RANK = 16
TOK_DEV = 256
EXP_DEV = 4
LANES = 128
META = MODEL_WIDTH + LANES
PACK_ROWS = 576
ATT_ROWS = 896
NORM_EPS = 1e-06
ROPE_BASE = 10000.0
F32 = jnp.float32
BF = jnp.bfloat16
ANY = pl.BlockSpec(memory_space=pl.ANY)
SMEM = pl.BlockSpec(memory_space=pltpu.SMEM)
VMEM = pl.BlockSpec(memory_space=pltpu.VMEM)
VMEM_LIMIT = 60 * 1024 * 1024


def nn(a, b):
    return lax.dot_general(a, b, (((1,), (0,)), ((), ())), preferred_element_type=F32)


def nt(a, b):
    return lax.dot_general(a, b, (((1,), (1,)), ((), ())), preferred_element_type=F32)


def tn(a, b):
    return lax.dot_general(a, b, (((0,), (0,)), ((), ())), preferred_element_type=F32)


def shape(*dims, dtype=BF):
    return jax.ShapeDtypeStruct(dims, dtype)


def rope_tables():
    inverse = ROPE_BASE ** (-2.0 * np.arange(HEAD_WIDTH // 2, dtype=np.float64) / HEAD_WIDTH)
    angles = np.arange(TOK_DEV, dtype=np.float64)[:, None] * inverse[None, :]
    cosine = np.tile(np.cos(angles), (1, 4)).astype(np.float32)
    sine = np.sin(angles)
    signed = np.concatenate([-sine, sine, -sine, sine], axis=1).astype(np.float32)
    return cosine, signed


def lanes_of(rows):
    return lax.broadcasted_iota(jnp.int32, (rows, LANES), 1)


def swap_halves(block):
    first = lanes_of(block.shape[0]) % HEAD_WIDTH < HEAD_WIDTH // 2
    return jnp.where(first, pltpu.roll(block, LANES - 32, 1), pltpu.roll(block, 32, 1))


def both(block, odd):
    low = lanes_of(block.shape[0]) < HEAD_WIDTH
    wide = block.astype(F32)
    other = pltpu.roll(wide, HEAD_WIDTH, 1)
    return (jnp.where(low, other, wide) if odd else jnp.where(low, wide, other)).astype(BF)


def stacked(block):
    low = lanes_of(block.shape[0]) < HEAD_WIDTH
    wide = block.astype(F32)
    return jnp.concatenate(
        [jnp.where(low, wide, 0.0).astype(BF), jnp.where(low, 0.0, wide).astype(BF)], axis=0
    )


def unstacked(pair):
    low = lanes_of(TOK_DEV) < HEAD_WIDTH
    return jnp.where(low, pair[:TOK_DEV], pair[TOK_DEV:])


def allowed_keys(length):
    row = lax.broadcasted_iota(jnp.int32, (2 * TOK_DEV, TOK_DEV), 0) % TOK_DEV
    col = lax.broadcasted_iota(jnp.int32, (2 * TOK_DEV, TOK_DEV), 1)
    return (col <= row) & (col < length)


def softmax(query_pair, key_both, allowed):
    scores = jnp.where(allowed, nt(query_pair, key_both) * (HEAD_WIDTH**-0.5), -1e30)
    exponent = jnp.exp(scores - jnp.max(scores, axis=1, keepdims=True))
    return exponent * (1.0 / jnp.sum(exponent, axis=1, keepdims=True))


def column(index):
    return slice(index * LANES, (index + 1) * LANES)


def copies_of(pairs, sems, start=0):
    return [
        pltpu.make_async_copy(source, target, sems.at[start + index]) for index, (source, target) in enumerate(pairs)
    ]


def forward_body(
    scalars, x_ref, g1_ref, g2_ref, cos_ref, sin_ref, routes_ref, router_ref,
    aat_h, wq_h, bq_h, wkv_h, bkv_h, ao_h, wo_h, bo_h,
    hidden_ref, payload_ref, wide_ref, orank_ref, normed_h, lowrank_h, q_h, k_h, v_h, att_h, probs_h,
    aat, wq, bq, wkv, bkv, ao, wo, bo, normed_ref, lowrank_ref, q_ref, k_ref, v_ref, att_ref, probs_ref, sems,
    *, experts,
):
    copies = copies_of(
        [(aat_h, aat), (wq_h, wq), (bq_h, bq), (wkv_h, wkv), (bkv_h, bkv), (ao_h, ao), (wo_h, wo), (bo_h, bo)], sems
    )
    saves = copies_of(
        [(normed_ref, normed_h), (lowrank_ref, lowrank_h), (q_ref, q_h), (k_ref, k_h), (v_ref, v_h), (att_ref, att_h)]
        + [(probs_ref.at[j], probs_h.at[j]) for j in range(8)],
        sems,
        8,
    )
    for copy in copies:
        copy.start()
    adapter = scalars[0]
    length = scalars[1]
    lane = lanes_of(TOK_DEV)
    mask = lane // ADAPTER_RANK == adapter
    x = x_ref[...].astype(F32)
    factor = lax.rsqrt(jnp.mean(x * x, axis=1, keepdims=True) + NORM_EPS)
    normed = (x * factor * g1_ref[...]).astype(BF)
    normed_ref[...] = normed
    saves[0].start()
    copies[0].wait()
    low = nn(normed, aat[...])
    ranks = [jnp.where(mask, low[:, column(i)], 0.0).astype(BF) for i in range(3)]
    for i in range(3):
        lowrank_ref[:, column(i)] = ranks[i]
    saves[1].start()
    cosine = cos_ref[...]
    sine = sin_ref[...]
    copies[1].wait()
    copies[2].wait()
    query_pre = nn(normed, wq[...]) + nn(ranks[0], bq[...])
    for j in range(8):
        block = query_pre[:, column(j)]
        q_ref[:, column(j)] = (block * cosine + swap_halves(block) * sine).astype(BF)
    saves[2].start()
    copies[3].wait()
    copies[4].wait()
    pre = nn(normed, wkv[...])
    key_pre = pre[:, :HALF_WIDTH] + nn(ranks[1], bkv[0])
    v_ref[...] = (pre[:, HALF_WIDTH:] + nn(ranks[2], bkv[1])).astype(BF)
    saves[4].start()
    for j in range(4):
        block = key_pre[:, column(j)]
        k_ref[:, column(j)] = (block * cosine + swap_halves(block) * sine).astype(BF)
    saves[3].start()
    allowed = allowed_keys(length)
    for j in range(8):
        pair = stacked(q_ref[:, column(j)])
        probs = softmax(pair, both(k_ref[:, column(j // 2)], j % 2), allowed).astype(BF)
        probs_ref[j] = probs
        saves[6 + j].start()
        att_ref[:, column(j)] = unstacked(nn(probs, both(v_ref[:, column(j // 2)], j % 2))).astype(BF)
    saves[5].start()
    attended = att_ref[...]
    for copy in copies[5:]:
        copy.wait()
    orank = jnp.where(mask, nn(attended, ao[...]), 0.0).astype(BF)
    orank_ref[...] = orank
    hidden = x + nn(attended, wo[...]) + nn(orank, bo[...])
    hidden_ref[...] = hidden
    factor2 = lax.rsqrt(jnp.mean(hidden * hidden, axis=1, keepdims=True) + NORM_EPS)
    normed2 = (hidden * factor2 * g2_ref[...]).astype(BF)
    spread = jnp.where(
        lax.broadcasted_iota(jnp.int32, (experts, LANES), 0)
        == lax.broadcasted_iota(jnp.int32, (experts, LANES), 1), 1.0, 0.0,
    ).astype(BF)
    wide = tn(router_ref[...], spread).astype(BF)
    wide_ref[...] = wide
    logits = nn(normed2, wide)
    routes = routes_ref[...]
    number = lax.broadcasted_iota(jnp.int32, (LANES, TOK_DEV), 0)
    named = routes[0:1, :] == number
    for k in range(1, routes.shape[0]):
        named = named | (routes[k : k + 1, :] == number)
    selected = jnp.where(named, 1.0, 0.0).T > 0.5
    top = jnp.max(jnp.where(selected, logits, -1e30), axis=1, keepdims=True)
    chosen = jnp.where(selected, jnp.exp(jnp.minimum(logits - top, 0.0)), 0.0)
    live = lax.broadcasted_iota(jnp.int32, (TOK_DEV, 1), 0) < length
    gates = chosen * jnp.where(live, 1.0 / jnp.sum(chosen, axis=1, keepdims=True), 0.0)
    high = gates.astype(BF).astype(F32)
    meta = high + pltpu.roll(gates - high, 32, 1) + jnp.where(lane >= 96, adapter.astype(F32), 0.0)
    payload_ref[:, :MODEL_WIDTH] = normed2
    payload_ref[:, MODEL_WIDTH:] = meta.astype(BF)
    for save in saves:
        save.wait()


def attention_forward(scalars, x, g1, g2, cosine, sine, routes, router, weights):
    experts = router.shape[0]
    saved = [
        (TOK_DEV, MODEL_WIDTH),
        (TOK_DEV, 3 * LANES),
        (TOK_DEV, MODEL_WIDTH),
        (TOK_DEV, HALF_WIDTH),
        (TOK_DEV, HALF_WIDTH),
        (TOK_DEV, MODEL_WIDTH),
        (8, 2 * TOK_DEV, TOK_DEV),
    ]
    return pl.pallas_call(
        functools.partial(forward_body, experts=experts),
        out_shape=[
            shape(TOK_DEV, MODEL_WIDTH, dtype=F32),
            shape(TOK_DEV, META),
            shape(MODEL_WIDTH, LANES),
            shape(TOK_DEV, LANES),
        ]
        + [shape(*dims) for dims in saved],
        in_specs=[SMEM] + [VMEM] * 7 + [ANY] * 8,
        out_specs=[VMEM] * 4 + [ANY] * 7,
        scratch_shapes=[pltpu.VMEM(w.shape, BF) for w in weights]
        + [pltpu.VMEM(dims, BF) for dims in saved]
        + [pltpu.SemaphoreType.DMA((22,))],
        compiler_params=pltpu.CompilerParams(vmem_limit_bytes=VMEM_LIMIT),
        cost_estimate=pl.CostEstimate(flops=3_000_000_000, bytes_accessed=20_000_000, transcendentals=1_000_000),
        name="attention_forward",
    )(scalars, x, g1, g2, cosine, sine, routes, router, *weights)


def backward_body(
    scalars, g1_ref, g2_ref, cos_ref, sin_ref, hidden_ref, keep_ref, got_ref, og_ref, orank_ref,
    *refs,
):
    (bo_h, wo_h, ao_h, att_h, q_h, k_h, v_h, probs_h, low_h, bq_h, bkv_h, normed_h, wq_h, wkv_h, aat_h, x_h) = refs[:16]
    gi_ref, mine_ref, send_ref = refs[16:19]
    bo, wo, ao, att, q_ref, k_ref, v_ref, probs_ref, lowrank_ref, bq, bkv, normed, wq, wkv, aat, x_ref = refs[19:35]
    pack, ga_s, gq_s, gk_s, gv_s, sems = refs[35:]
    copies = copies_of(list(zip(refs[:16], refs[19:35])), sems)
    for copy in copies:
        copy.start()
    adapter = scalars[0]
    length = scalars[1]
    side = scalars[2]
    mask = lanes_of(TOK_DEV) // ADAPTER_RANK == adapter

    def masked(values):
        return jnp.where(mask, values, 0.0).astype(BF)

    hidden = hidden_ref[...]
    factor2 = lax.rsqrt(jnp.mean(hidden * hidden, axis=1, keepdims=True) + NORM_EPS)
    live = lax.broadcasted_iota(jnp.int32, (TOK_DEV, 1), 0) < length
    grad_live = jnp.where(live, og_ref[...].astype(F32), 0.0)
    y = (keep_ref[...].astype(F32) + got_ref[...].astype(F32)) * g2_ref[...]
    inner = jnp.mean(y * hidden, axis=1, keepdims=True)
    grad_hidden = grad_live + factor2 * (y - hidden * (factor2 * factor2 * inner))
    gi_ref[...] = grad_hidden
    branch = grad_hidden.astype(BF)
    pack[768:896, :] = tn(orank_ref[...], branch).astype(BF)
    for copy in copies[:4]:
        copy.wait()
    grad_orank = masked(nt(branch, bo[...]))
    pack[640:768, :] = tn(grad_orank, att[...]).astype(BF)
    ga_s[...] = (nt(branch, wo[...]) + nt(grad_orank, ao[...])).astype(BF)
    cosine = cos_ref[...]
    sine = sin_ref[...]
    low = lanes_of(TOK_DEV) < HEAD_WIDTH
    scale = HEAD_WIDTH**-0.5
    for copy in copies[4:8]:
        copy.wait()

    def group(i, carry):
        here = pl.ds(pl.multiple_of(i * LANES, LANES), LANES)
        sums = []
        for odd in range(2):
            j = 2 * i + odd
            there = pl.ds(pl.multiple_of(j * LANES, LANES), LANES)
            pair = stacked(q_ref[:, there])
            key_both = both(k_ref[:, here], odd)
            value_both = both(v_ref[:, here], odd)
            probs = probs_ref[j]
            grad_pair = stacked(ga_s[:, there])
            grad_probs = nt(grad_pair, value_both).astype(BF).astype(F32)
            grad_v = tn(probs, grad_pair)
            wide = probs.astype(F32)
            weighted = wide * grad_probs
            scores = (weighted - wide * jnp.sum(weighted, axis=1, keepdims=True)).astype(BF)
            grad_q = unstacked(nn(scores, key_both)) * scale
            gq_s[:, there] = (grad_q * cosine - swap_halves(grad_q) * sine).astype(BF)
            grad_k = tn(scores, pair) * scale
            sums.append((grad_k + pltpu.roll(grad_k, HEAD_WIDTH, 1), grad_v + pltpu.roll(grad_v, HEAD_WIDTH, 1)))
        block = jnp.where(low, sums[0][0], sums[1][0])
        gk_s[:, here] = (block * cosine - swap_halves(block) * sine).astype(BF)
        gv_s[:, here] = jnp.where(low, sums[0][1], sums[1][1]).astype(BF)
        return carry

    lax.fori_loop(0, 4, group, 0)
    gq = gq_s[...]
    gk = gk_s[...]
    gv = gv_s[...]
    for copy in copies[8:12]:
        copy.wait()
    pack[384:512, :] = tn(lowrank_ref[:, column(0)], gq).astype(BF)
    pack[512:640, :HALF_WIDTH] = tn(lowrank_ref[:, column(1)], gk).astype(BF)
    pack[512:640, HALF_WIDTH:] = tn(lowrank_ref[:, column(2)], gv).astype(BF)
    grad_rank = jnp.concatenate(
        [masked(nt(gq, bq[...])), masked(nt(gk, bkv[0])), masked(nt(gv, bkv[1]))], axis=1
    )
    pack[0:384, :] = tn(grad_rank, normed[...]).astype(BF)
    for copy in copies[12:]:
        copy.wait()
    grad_normed = (
        nt(gq, wq[...])
        + nt(jnp.concatenate([gk, gv], axis=1), wkv[...])
        + nt(grad_rank, aat[...])
    )
    x = x_ref[...].astype(F32)
    factor = lax.rsqrt(jnp.mean(x * x, axis=1, keepdims=True) + NORM_EPS)
    z = grad_normed * g1_ref[...]
    inner = jnp.mean(z * x, axis=1, keepdims=True)
    gi_ref[...] += factor * (z - x * (factor * factor * inner))
    half = ATT_ROWS // 2
    mine_ref[...] = pack[pl.ds(pl.multiple_of(side * half, 16), half), :]
    send_ref[...] = pack[pl.ds(pl.multiple_of((1 - side) * half, 16), half), :]


def attention_backward(scalars, arrays, later):
    half = ATT_ROWS // 2
    return pl.pallas_call(
        backward_body,
        out_shape=[shape(TOK_DEV, MODEL_WIDTH, dtype=F32), shape(half, MODEL_WIDTH), shape(half, MODEL_WIDTH)],
        in_specs=[SMEM] + [VMEM] * len(arrays) + [ANY] * len(later),
        out_specs=[VMEM] * 3,
        scratch_shapes=[pltpu.VMEM(w.shape, BF) for w in later]
        + [
            pltpu.VMEM((ATT_ROWS, MODEL_WIDTH), BF),
            pltpu.VMEM((TOK_DEV, MODEL_WIDTH), BF),
            pltpu.VMEM((TOK_DEV, MODEL_WIDTH), BF),
            pltpu.VMEM((TOK_DEV, HALF_WIDTH), BF),
            pltpu.VMEM((TOK_DEV, HALF_WIDTH), BF),
            pltpu.SemaphoreType.DMA((len(later),)),
        ],
        compiler_params=pltpu.CompilerParams(vmem_limit_bytes=VMEM_LIMIT),
        cost_estimate=pl.CostEstimate(flops=6_000_000_000, bytes_accessed=24_000_000, transcendentals=1_000_000),
        name="attention_backward",
    )(scalars, *arrays, *later)


def expert_body(
    scalars, *refs, expert, start, count, blocks, experts, carried, seeded, emit, last,
):
    refs = list(refs)

    def take(number):
        taken = refs[:number]
        del refs[:number]
        return taken

    x_blocks = take(count)
    g_blocks = take(count)
    ain_h, win_h, bin_h, adn_h, wdn_h, bdn_h = take(6)
    if carried:
        f_in, b_in, c_in = take(3)
    if start:
        take(3)
    seeds = take(4) if seeded else None
    if last:
        wr_ref, f_top, f_low, b_top, b_low = take(5)
    else:
        f_out, b_out, c_out = take(3)
    if emit:
        emitted = take(4)
    else:
        mine_ref, send_ref = take(2)
    xs, gs_buf, ain, win, bin_, adn, wdn, bdn, acc_a, acc_bi, acc_ad, acc_bd, pack, xsem, gsem, wsem = refs[:16]
    if last:
        f_buf, b_buf, fsem, bsem = refs[16:]
    sums = [acc_a, acc_bi, acc_ad, acc_bd]
    step = pl.program_id(0)
    slot = lax.rem(step, 2)
    early = [
        pltpu.make_async_copy(source.at[expert], target, wsem.at[index])
        for index, (source, target) in enumerate([(ain_h, ain), (win_h, win), (bin_h, bin_)])
    ]
    late = [
        pltpu.make_async_copy(source.at[expert], target, wsem.at[3 + index])
        for index, (source, target) in enumerate([(adn_h, adn), (wdn_h, wdn), (bdn_h, bdn)])
    ]

    def fetch(block):
        pltpu.make_async_copy(x_blocks[block], xs.at[block % 2], xsem.at[block % 2]).start()
        pltpu.make_async_copy(g_blocks[block], gs_buf.at[block % 2], gsem.at[block % 2]).start()

    @pl.when(step == 0)
    def _():
        fetch(0)
        for copy in early + late:
            copy.start()
        for index, total in enumerate(sums):
            total[...] = seeds[index][...] if seeded else jnp.zeros_like(total)
        for copy in early:
            copy.wait()

    for block in range(1, count):
        @pl.when(step == block - 1)
        def _(block=block):
            fetch(block)

    pltpu.make_async_copy(x_blocks[0], xs.at[slot], xsem.at[slot]).wait()
    pltpu.make_async_copy(g_blocks[0], gs_buf.at[slot], gsem.at[slot]).wait()
    if last:
        @pl.when(step >= 2)
        def _():
            pltpu.make_async_copy(b_buf.at[slot], b_top.at[pl.ds(0, TOK_DEV)], bsem.at[slot]).wait()
            pltpu.make_async_copy(f_buf.at[slot], f_top.at[pl.ds(0, TOK_DEV)], fsem.at[slot]).wait()

    eid = scalars[0]
    side = scalars[1]
    x = xs[slot, :, :MODEL_WIDTH]
    meta = xs[slot, :, MODEL_WIDTH:].astype(F32)
    lane = lanes_of(TOK_DEV)
    adapter = meta[:, 96:97].astype(jnp.int32)
    mask = lane // ADAPTER_RANK == adapter

    def masked(values):
        return jnp.where(mask, values, 0.0).astype(BF)

    gates = jnp.where(lane < experts, meta + pltpu.roll(meta, 96, 1), 0.0)
    here = lane == eid
    gate_e = jnp.sum(jnp.where(here, gates, 0.0), axis=1, keepdims=True)
    low = nn(x, ain[...])
    low_gate = masked(low[:, :LANES])
    low_up = masked(low[:, LANES:])
    gate = nn(x, win[:, :HALF_WIDTH]) + nn(low_gate, bin_[0])
    up = nn(x, win[:, HALF_WIDTH:]) + nn(low_up, bin_[1])
    sig = 1.0 / (1.0 + jnp.exp(-gate))
    silu = gate * sig
    active = (silu * up).astype(BF)

    @pl.when(step == 0)
    def _():
        for copy in late:
            copy.wait()

    down = masked(nn(active, adn[...]))
    grad = gs_buf[slot].astype(F32)
    out = nn(active, wdn[...]) + nn(down, bdn[...])
    grad_gate_e = jnp.sum(out * grad, axis=1, keepdims=True)
    weighted = gate_e * out
    if carried:
        weighted = weighted + f_in[...]
    if last:
        f_buf[slot] = weighted.astype(BF)
    else:
        f_out[...] = weighted
    slot_grad = (gate_e * grad).astype(BF)
    grad_down = masked(nt(slot_grad, bdn[...]))
    grad_active = nt(slot_grad, wdn[...]) + nt(grad_down, adn[...])
    gate_grad = (grad_active * up * sig * (1.0 + gate * (1.0 - sig))).astype(BF)
    up_grad = (grad_active * silu).astype(BF)
    grad_low = jnp.concatenate([masked(nt(gate_grad, bin_[0])), masked(nt(up_grad, bin_[1]))], axis=1)
    both_grads = jnp.concatenate([gate_grad, up_grad], axis=1)
    rows = nt(both_grads, win[...]) + nt(grad_low, ain[...])
    part = (gate_e * grad_gate_e) * (jnp.where(here, 1.0, 0.0) - gates)
    if carried:
        rows = rows + b_in[...]
        part = part + c_in[...]
    if last:
        rows = rows + nt(part.astype(BF), wr_ref[...])

        b_buf[slot] = rows.astype(BF)
        for block in range(count):
            @pl.when(step == block)
            def _(block=block):
                part_rows = pl.ds(block // 2 * TOK_DEV, TOK_DEV)
                f_to = (f_low if block % 2 else f_top).at[part_rows]
                b_to = (b_low if block % 2 else b_top).at[part_rows]
                pltpu.make_async_copy(b_buf.at[block % 2], b_to, bsem.at[block % 2]).start()
                pltpu.make_async_copy(f_buf.at[block % 2], f_to, fsem.at[block % 2]).start()
    else:
        c_out[...] = part
        b_out[...] = rows
    acc_a[...] += tn(grad_low, x)
    acc_bi[:, :HALF_WIDTH] += tn(low_gate, gate_grad)
    acc_bi[:, HALF_WIDTH:] += tn(low_up, up_grad)
    acc_ad[...] += tn(grad_down, active)
    acc_bd[...] += tn(down, slot_grad)

    @pl.when(step == count - 1)
    def _():
        if emit:
            for target, total in zip(emitted, sums):
                target[...] = total[...]
        else:
            pack[0:256, :] = acc_a[...].astype(BF)
            pack[256:384, :] = acc_bi[...].astype(BF)
            pack[384:512, :] = acc_bd[...].astype(BF)
            pack[512:576, :HALF_WIDTH] = acc_ad[0:64, :].astype(BF)
            pack[512:576, HALF_WIDTH:] = acc_ad[64:128, :].astype(BF)
            half = PACK_ROWS // 2
            mine_ref[...] = pack[pl.ds(pl.multiple_of(side * half, 16), half), :]
            send_ref[...] = pack[pl.ds(pl.multiple_of((1 - side) * half, 16), half), :]
        if last:
            for index in range(2):
                pltpu.make_async_copy(b_buf.at[index], b_top.at[pl.ds(0, TOK_DEV)], bsem.at[index]).wait()
                pltpu.make_async_copy(f_buf.at[index], f_top.at[pl.ds(0, TOK_DEV)], fsem.at[index]).wait()


def expert_call(
    expert, scalars, x_blocks, g_blocks, weights, experts, blocks, start=0,
    carried=None, halves=None, seeds=None, emit=False, router_wide=None,
):
    count = len(x_blocks)
    total = blocks * TOK_DEV
    last = router_wide is not None
    rows = lambda width: pl.BlockSpec((TOK_DEV, width), lambda i, *_: (i + start, 0))
    whole = lambda *dims: pl.BlockSpec(dims, lambda i, *_: (0,) * len(dims), pipeline_mode=pl.Buffered(1))
    fixed = lambda *dims: pl.BlockSpec(dims, lambda i, *_: (0,) * len(dims))
    sum_dims = [(256, MODEL_WIDTH), (128, MODEL_WIDTH), (128, HALF_WIDTH), (128, MODEL_WIDTH)]
    in_specs = [ANY] * (2 * count + 6)
    args = [*x_blocks, *g_blocks, *weights]
    aliases = {}
    if carried is not None:
        in_specs += [rows(MODEL_WIDTH), rows(MODEL_WIDTH), rows(LANES)]
        args += list(carried)
    if start:
        aliases = {1 + len(args) + i: i for i in range(3)}
        in_specs += [ANY] * 3
        args += list(halves)
    if seeds is not None:
        in_specs += [whole(*d) for d in sum_dims]
        args += list(seeds)
    if last:
        in_specs.append(whole(MODEL_WIDTH, LANES))
        args.append(router_wide)
        outs = [shape(total // 2, MODEL_WIDTH)] * 4
        out_specs = [ANY] * 4
    else:
        outs = [
            shape(total, MODEL_WIDTH, dtype=F32),
            shape(total, MODEL_WIDTH, dtype=F32),
            shape(total, LANES, dtype=F32),
        ]
        out_specs = [rows(MODEL_WIDTH), rows(MODEL_WIDTH), rows(LANES)]
    half = PACK_ROWS // 2
    if emit:
        outs += [shape(*d, dtype=F32) for d in sum_dims]
        out_specs += [fixed(*d) for d in sum_dims]
    else:
        outs += [shape(half, MODEL_WIDTH)] * 2
        out_specs += [fixed(half, MODEL_WIDTH)] * 2
    scratch = [pltpu.VMEM((2, TOK_DEV, META), BF), pltpu.VMEM((2, TOK_DEV, MODEL_WIDTH), BF)]
    scratch += [pltpu.VMEM(w.shape[1:], BF) for w in weights]
    scratch += [pltpu.VMEM(d, F32) for d in sum_dims]
    scratch += [
        pltpu.VMEM((PACK_ROWS, MODEL_WIDTH), BF),
        pltpu.SemaphoreType.DMA((2,)),
        pltpu.SemaphoreType.DMA((2,)),
        pltpu.SemaphoreType.DMA((6,)),
    ]
    if last:
        scratch += [pltpu.VMEM((2, TOK_DEV, MODEL_WIDTH), BF)] * 2 + [pltpu.SemaphoreType.DMA((2,))] * 2
    return pl.pallas_call(
        functools.partial(
            expert_body, expert=expert, start=start, count=count, blocks=blocks, experts=experts,
            carried=carried is not None, seeded=seeds is not None, emit=emit, last=last,
        ),
        out_shape=outs,
        grid_spec=pltpu.PrefetchScalarGridSpec(
            num_scalar_prefetch=1, grid=(count,), in_specs=in_specs, out_specs=out_specs, scratch_shapes=scratch
        ),
        input_output_aliases=aliases,
        compiler_params=pltpu.CompilerParams(
            dimension_semantics=("arbitrary",), vmem_limit_bytes=VMEM_LIMIT
        ),
        cost_estimate=pl.CostEstimate(
            flops=count * TOK_DEV * 9_800_000, bytes_accessed=5_000_000 * count, transcendentals=0
        ),
        name="expert_step",
    )(scalars, *args)


def expert_finish_body(scalars, *refs, count, held):
    pieces = refs[: 2 * count]
    a_in, b_in, a_down, b_down, pack = refs[2 * count + held :]
    side = scalars[0]
    half = PACK_ROWS // 2
    step = pl.program_id(0)
    for index in range(count):
        @pl.when(step == index)
        def _(index=index):
            pack[pl.ds(pl.multiple_of(side * half, 16), half), :] = pieces[2 * index][...]
            pack[pl.ds(pl.multiple_of((1 - side) * half, 16), half), :] = pieces[2 * index + 1][...]
    a_in[0] = pack[0:256, :].astype(F32).T
    b_in[0, 0] = pack[256:384, :HALF_WIDTH].astype(F32)
    b_in[0, 1] = pack[256:384, HALF_WIDTH:].astype(F32)
    b_down[0] = pack[384:512, :].astype(F32)
    a_down[0] = jnp.concatenate([pack[512:576, :HALF_WIDTH], pack[512:576, HALF_WIDTH:]], axis=0).astype(F32).T


def expert_finish(side, sums, start=0, held=()):
    half = PACK_ROWS // 2
    count = len(sums)
    pieces = [piece for one in sums for piece in (one.mine, one.got)]
    block = lambda *dims: pl.BlockSpec((1,) + dims, lambda i, *_: (i + start,) + (0,) * len(dims))
    dims = [(MODEL_WIDTH, 256), (2, 128, HALF_WIDTH), (HALF_WIDTH, 128), (128, MODEL_WIDTH)]
    return pl.pallas_call(
        functools.partial(expert_finish_body, count=count, held=len(held)),
        out_shape=[shape(EXP_DEV, *d, dtype=F32) for d in dims],
        grid_spec=pltpu.PrefetchScalarGridSpec(
            num_scalar_prefetch=1,
            grid=(count,),
            in_specs=[
                pl.BlockSpec((half, MODEL_WIDTH), lambda i, *_: (0, 0), pipeline_mode=pl.Buffered(1))
            ] * len(pieces)
            + [ANY] * len(held),
            out_specs=[block(*d) for d in dims],
            scratch_shapes=[pltpu.VMEM((PACK_ROWS, MODEL_WIDTH), BF)],
        ),
        input_output_aliases={1 + len(pieces) + i: i for i in range(len(held))},
        compiler_params=pltpu.CompilerParams(
            dimension_semantics=("arbitrary",), vmem_limit_bytes=VMEM_LIMIT
        ),
        cost_estimate=pl.CostEstimate(flops=1_000_000, bytes_accessed=4_000_000 * count, transcendentals=0),
        name="expert_finish",
    )(side, *pieces, *held)


def attention_finish_body(scalars, mine_ref, got_ref, a_ref, bq_ref, bkv_ref, oa_ref, ob_ref, pack):
    side = scalars[0]
    half = ATT_ROWS // 2
    pack[pl.ds(pl.multiple_of(side * half, 16), half), :] = mine_ref[...]
    pack[pl.ds(pl.multiple_of((1 - side) * half, 16), half), :] = got_ref[...]
    a_ref[...] = pack[0:384, :].astype(F32).T
    bq_ref[...] = pack[384:512, :].astype(F32)
    bkv_ref[0] = pack[512:640, :HALF_WIDTH].astype(F32)
    bkv_ref[1] = pack[512:640, HALF_WIDTH:].astype(F32)
    oa_ref[...] = pack[640:768, :].astype(F32).T
    ob_ref[...] = pack[768:896, :].astype(F32)


def attention_finish(side, mine, got):
    dims = [(MODEL_WIDTH, 384), (128, MODEL_WIDTH), (2, 128, HALF_WIDTH), (MODEL_WIDTH, 128), (128, MODEL_WIDTH)]
    return pl.pallas_call(
        attention_finish_body,
        out_shape=[shape(*d, dtype=F32) for d in dims],
        in_specs=[SMEM, VMEM, VMEM],
        out_specs=[VMEM] * 5,
        scratch_shapes=[pltpu.VMEM((ATT_ROWS, MODEL_WIDTH), BF)],
        compiler_params=pltpu.CompilerParams(vmem_limit_bytes=VMEM_LIMIT),
        cost_estimate=pl.CostEstimate(flops=1_000_000, bytes_accessed=6_000_000, transcendentals=0),
        name="attention_finish",
    )(side, mine, got)


def swap(values, axis, bit):
    size = lax.axis_size(axis)
    return lax.ppermute(values, axis, [(i, i ^ (1 << bit)) for i in range(size)])


def axis_bits(axis):
    return lax.axis_size(axis).bit_length() - 1


def tie(first, second):
    return lax.optimization_barrier((first, second))


def add(first, second):
    return (first.astype(F32) + second.astype(F32)).astype(BF)


def far_blocks(values):
    blocks = {0: values}
    for bit in reversed(range(1, axis_bits("expert"))):
        for index in list(blocks):
            blocks[index ^ (1 << bit)] = swap(blocks[index], "expert", bit)
    return blocks


def near_blocks(far):
    blocks = []
    for index in sorted(far):
        if index:
            blocks += [far[index], swap(far[index], "expert", 0)]
    return blocks


class Return:
    def __init__(self, top, low):
        self.bits = list(reversed(range(1, axis_bits("expert"))))
        self.mine = top
        self.got = swap(low, "expert", 0)

    def advance(self):
        half = self.mine.shape[0] // 2
        send = add(self.mine[half:], self.got[half:])
        self.mine = add(self.mine[:half], self.got[:half])
        return send

    def launch(self, send):
        self.got = swap(send, "expert", self.bits.pop(0))


class Sum:
    def __init__(self, mine, send, stages):
        self.path = []
        self.stages = list(stages)
        self.mine = mine
        self.send = send
        self.down = True
        self.target = self.stages.pop(0)
        self.path.append(self.target)

    def launch(self):
        self.got = swap(self.send, *self.target)
        return self

    def prepare(self):
        if self.down:
            values = add(self.mine, self.got)
            if self.stages:
                self.target = self.stages.pop(0)
                axis, bit = self.target
                rows, width = values.shape
                if rows % 16:
                    self.mine = self.send = values
                    return
                self.path.append(self.target)
                side = (lax.axis_index(axis) >> bit) & 1
                halves = values.reshape(2, rows // 2, width)
                self.mine = lax.dynamic_index_in_dim(halves, side, 0, keepdims=False)
                self.send = lax.dynamic_index_in_dim(halves, 1 - side, 0, keepdims=False)
                return
            self.down = False
        else:
            axis, bit = self.path.pop()
            side = (lax.axis_index(axis) >> bit) & 1
            low = jnp.where(side == 0, self.mine, self.got)
            high = jnp.where(side == 0, self.got, self.mine)
            values = jnp.concatenate([low, high], axis=0)
        self.target = self.path[-1]
        self.mine = self.send = values

    def pending(self):
        return self.down or len(self.path) > 1


def prepare(ones):
    for one in ones:
        one.prepare()


def step(*ones):
    ones = [one for one in ones if one.pending()]
    prepare(ones)
    for one in ones:
        one.launch()


def sync(holders, *extras):
    arrays = tuple(holder.got for holder in holders) + extras
    arrays = lax.optimization_barrier(arrays)
    for holder, got in zip(holders, arrays):
        holder.got = got
    return arrays[len(holders) :]


def on_device(
    inputs,
    lengths,
    routes,
    adapter_of_sequence,
    first_norm_gain,
    query_weight,
    key_value_weight,
    output_weight,
    second_norm_gain,
    router_weight,
    expert_input_weight,
    expert_down_weight,
    attention_first_factors,
    query_second_factors,
    key_value_second_factors,
    output_first_factors,
    output_second_factors,
    expert_input_first_factors,
    expert_input_second_factors,
    expert_down_first_factors,
    expert_down_second_factors,
    output_gradient,
):
    blocks = lax.axis_size("expert")
    experts = EXP_DEV * blocks
    place = lax.axis_index("expert")
    dp_side = lax.axis_index("dp") & 1
    core_side = place & 1
    grad_far = far_blocks(output_gradient)
    cosine, sine = rope_tables()
    scalars = jnp.stack([adapter_of_sequence[0], lengths[0], core_side]).astype(jnp.int32)
    g1 = first_norm_gain[None]
    g2 = second_norm_gain[None]
    weights = [
        attention_first_factors,
        query_weight,
        query_second_factors,
        key_value_weight,
        key_value_second_factors,
        output_first_factors,
        output_weight,
        output_second_factors,
    ]
    hidden, payload, router_wide, out_rank, normed, lowrank, queries, keys, values, attended, probs = attention_forward(
        scalars, inputs, g1, g2, cosine, sine, routes.T, router_weight.T, weights
    )
    for index in grad_far:
        if index:
            grad_far[index], payload = tie(grad_far[index], payload)
    row_far = far_blocks(payload)
    near = [[values, swap(values, "expert", 0)] for values in (payload, output_gradient)]
    expert_weights = [
        expert_input_first_factors,
        expert_input_weight,
        expert_input_second_factors,
        expert_down_first_factors,
        expert_down_weight,
        expert_down_second_factors,
    ]
    dp_stages = [("dp", bit) for bit in range(axis_bits("dp"))]
    sums = []
    first_number = EXP_DEV * place
    number = jnp.stack([first_number, dp_side]).astype(jnp.int32)
    *halves, s0, s1, s2, s3 = expert_call(
        0, number, *near, expert_weights, experts, blocks, emit=True
    )
    for far in (row_far, grad_far):
        for index in far:
            if index:
                far[index], s0 = tie(far[index], s0)
    row_blocks = near[0] + near_blocks(row_far)
    grad_blocks = near[1] + near_blocks(grad_far)
    *carried, mine, send = expert_call(
        0, number, row_blocks[2:], grad_blocks[2:], expert_weights, experts, blocks,
        start=2, halves=halves, seeds=(s0, s1, s2, s3),
    )
    sums.append(Sum(mine, send, dp_stages).launch())
    for local in range(1, EXP_DEV):
        number = jnp.stack([first_number + local, dp_side]).astype(jnp.int32)
        (number,) = sync(sums[: local - 1], number)
        step(*sums[: local - 1])
        *carried, mine, send = expert_call(
            local, number, row_blocks, grad_blocks, expert_weights, experts, blocks, carried=carried,
            router_wide=router_wide if local == EXP_DEV - 1 else None,
        )
        if local < EXP_DEV - 1:
            sums.append(Sum(mine, send, dp_stages).launch())
    mix_top, mix_low, row_top, row_low = carried
    (row_low,) = sync(sums, row_low)
    row = Return(row_top, row_low)
    prepare(sums)
    sums.append(Sum(mine, send, dp_stages))
    row_send = row.advance() if row.bits else row.mine
    row_send, mix_low, newest = lax.optimization_barrier((row_send, mix_low, sums[-1].send))
    while row.bits:
        row.launch(row_send)
        row_send = row.advance() if row.bits else row.mine
    mix = Return(mix_top, mix_low)
    sums[-1].send = newest
    sums[-1].launch()
    sends = sync([mix], *[one.send for one in sums[:-1]])
    for one, one.send in zip(sums, sends):
        one.launch()
    sync(sums + [mix])
    step(*sums)
    mix_send = mix.advance() if mix.bits else mix.mine
    mix_send, *_ = sync([row], mix_send, *[one.send for one in sums])
    while mix.bits:
        mix.launch(mix_send)
        mix_send = mix.advance() if mix.bits else mix.mine
    grad_input, att_mine, att_send = attention_backward(
        scalars,
        [g1, g2, cosine, sine, hidden, row.mine, row.got, output_gradient, out_rank],
        [output_second_factors, output_weight, output_first_factors, attended, queries, keys, values, probs]
        + [lowrank, query_second_factors, key_value_second_factors, normed, query_weight, key_value_weight]
        + [attention_first_factors, inputs],
    )
    (att_send,) = sync(sums + [mix], att_send)
    stages = [("expert", bit) for bit in range(axis_bits("expert"))] + dp_stages
    total = Sum(att_mine, att_send, stages).launch()
    step(*sums)
    step(total)
    sync(sums + [total])
    step(total, *sums[2:])
    sync(sums[2:] + [total])
    step(total, *sums[1:])
    step(total)
    step(total)
    sync(sums[1:] + [total])
    step(total)
    sync([total, sums[3]])
    step(total, sums[3])
    for one in sums:
        while one.pending():
            step(one)
    dp_piece = dp_side[None].astype(jnp.int32)
    held = list(expert_finish(dp_piece, sums[:3]))
    (held[3],) = sync([total, sums[3]], held[3])
    while total.pending():
        step(total)
    expert_grads = expert_finish(dp_piece, sums[3:], 3, held)
    live = (jnp.arange(TOK_DEV, dtype=jnp.int32) < lengths[0]).astype(F32)[:, None]
    output = (live * (hidden + mix.mine.astype(F32) + mix.got.astype(F32))).astype(BF)
    side = core_side[None].astype(jnp.int32)
    attention_grads = attention_finish(side, total.mine, total.got)
    return (output, grad_input, *attention_grads, *expert_grads)


def solution(mesh):
    rows = P(("dp", "expert"), None)
    each = P(("dp", "expert"))
    three = P("expert", None, None)
    four = P("expert", None, None, None)
    return jax.shard_map(
        on_device,
        mesh=mesh,
        in_specs=(
            (rows, each, rows, each)
            + (P(),) * 6
            + (three, three)
            + (P(),) * 5
            + (three, four, three, three, rows)
        ),
        out_specs=(rows, rows) + (P(),) * 5 + (three, four, three, three),
        check_vma=False,
    )
```

```python
import functools

import jax
import jax.numpy as jnp
import numpy as np
from jax import lax
from jax.experimental import pallas as pl
from jax.experimental.pallas import tpu as pltpu
from jax.sharding import PartitionSpec as P

MODEL_WIDTH = 1024
HALF_WIDTH = 512
HEAD_WIDTH = 64
ADAPTER_RANK = 16
TOK_DEV = 256
EXP_DEV = 4
LANES = 128
META = MODEL_WIDTH + LANES
PACK_ROWS = 576
ATT_ROWS = 896
NORM_EPS = 1e-06
ROPE_BASE = 10000.0
F32 = jnp.float32
BF = jnp.bfloat16
ANY = pl.BlockSpec(memory_space=pl.ANY)
SMEM = pl.BlockSpec(memory_space=pltpu.SMEM)
VMEM = pl.BlockSpec(memory_space=pltpu.VMEM)
VMEM_LIMIT = 60 * 1024 * 1024


def nn(a, b):
    return lax.dot_general(a, b, (((1,), (0,)), ((), ())), preferred_element_type=F32)


def nt(a, b):
    return lax.dot_general(a, b, (((1,), (1,)), ((), ())), preferred_element_type=F32)


def tn(a, b):
    return lax.dot_general(a, b, (((0,), (0,)), ((), ())), preferred_element_type=F32)


def shape(*dims, dtype=BF):
    return jax.ShapeDtypeStruct(dims, dtype)


def rope_tables():
    inverse = ROPE_BASE ** (-2.0 * np.arange(HEAD_WIDTH // 2, dtype=np.float64) / HEAD_WIDTH)
    angles = np.arange(TOK_DEV, dtype=np.float64)[:, None] * inverse[None, :]
    cosine = np.tile(np.cos(angles), (1, 4)).astype(np.float32)
    sine = np.sin(angles)
    signed = np.concatenate([-sine, sine, -sine, sine], axis=1).astype(np.float32)
    return cosine, signed


def lanes_of(rows):
    return lax.broadcasted_iota(jnp.int32, (rows, LANES), 1)


def swap_halves(block):
    first = lanes_of(block.shape[0]) % HEAD_WIDTH < HEAD_WIDTH // 2
    return jnp.where(first, pltpu.roll(block, LANES - 32, 1), pltpu.roll(block, 32, 1))


def both(block, odd):
    low = lanes_of(block.shape[0]) < HEAD_WIDTH
    wide = block.astype(F32)
    other = pltpu.roll(wide, HEAD_WIDTH, 1)
    return (jnp.where(low, other, wide) if odd else jnp.where(low, wide, other)).astype(BF)


def stacked(block):
    low = lanes_of(block.shape[0]) < HEAD_WIDTH
    wide = block.astype(F32)
    return jnp.concatenate(
        [jnp.where(low, wide, 0.0).astype(BF), jnp.where(low, 0.0, wide).astype(BF)], axis=0
    )


def unstacked(pair):
    low = lanes_of(TOK_DEV) < HEAD_WIDTH
    return jnp.where(low, pair[:TOK_DEV], pair[TOK_DEV:])


def allowed_keys(length):
    row = lax.broadcasted_iota(jnp.int32, (2 * TOK_DEV, TOK_DEV), 0) % TOK_DEV
    col = lax.broadcasted_iota(jnp.int32, (2 * TOK_DEV, TOK_DEV), 1)
    return (col <= row) & (col < length)


def softmax(query_pair, key_both, allowed):
    scores = jnp.where(allowed, nt(query_pair, key_both) * (HEAD_WIDTH**-0.5), -1e30)
    exponent = jnp.exp(scores - jnp.max(scores, axis=1, keepdims=True))
    return exponent * (1.0 / jnp.sum(exponent, axis=1, keepdims=True))


def column(index):
    return slice(index * LANES, (index + 1) * LANES)


def copies_of(pairs, sems, start=0):
    return [
        pltpu.make_async_copy(source, target, sems.at[start + index]) for index, (source, target) in enumerate(pairs)
    ]


def forward_body(
    scalars, x_ref, g1_ref, g2_ref, cos_ref, sin_ref, routes_ref, router_ref,
    aat_h, wq_h, bq_h, wkv_h, bkv_h, ao_h, wo_h, bo_h,
    hidden_ref, payload_ref, wide_ref, orank_ref, normed_h, lowrank_h, q_h, k_h, v_h, att_h, probs_h,
    aat, wq, bq, wkv, bkv, ao, wo, bo, normed_ref, lowrank_ref, q_ref, k_ref, v_ref, att_ref, probs_ref, sems,
    *, experts,
):
    copies = copies_of(
        [(aat_h, aat), (wq_h, wq), (bq_h, bq), (wkv_h, wkv), (bkv_h, bkv), (ao_h, ao), (wo_h, wo), (bo_h, bo)], sems
    )
    saves = copies_of(
        [(normed_ref, normed_h), (lowrank_ref, lowrank_h), (q_ref, q_h), (k_ref, k_h), (v_ref, v_h), (att_ref, att_h)]
        + [(probs_ref.at[j], probs_h.at[j]) for j in range(8)],
        sems,
        8,
    )
    for copy in copies:
        copy.start()
    adapter = scalars[0]
    length = scalars[1]
    lane = lanes_of(TOK_DEV)
    mask = lane // ADAPTER_RANK == adapter
    x = x_ref[...].astype(F32)
    factor = lax.rsqrt(jnp.mean(x * x, axis=1, keepdims=True) + NORM_EPS)
    normed = (x * factor * g1_ref[...]).astype(BF)
    normed_ref[...] = normed
    saves[0].start()
    copies[0].wait()
    low = nn(normed, aat[...])
    ranks = [jnp.where(mask, low[:, column(i)], 0.0).astype(BF) for i in range(3)]
    for i in range(3):
        lowrank_ref[:, column(i)] = ranks[i]
    saves[1].start()
    cosine = cos_ref[...]
    sine = sin_ref[...]
    copies[1].wait()
    copies[2].wait()
    query_pre = nn(normed, wq[...]) + nn(ranks[0], bq[...])
    for j in range(8):
        block = query_pre[:, column(j)]
        q_ref[:, column(j)] = (block * cosine + swap_halves(block) * sine).astype(BF)
    saves[2].start()
    copies[3].wait()
    copies[4].wait()
    pre = nn(normed, wkv[...])
    key_pre = pre[:, :HALF_WIDTH] + nn(ranks[1], bkv[0])
    v_ref[...] = (pre[:, HALF_WIDTH:] + nn(ranks[2], bkv[1])).astype(BF)
    saves[4].start()
    for j in range(4):
        block = key_pre[:, column(j)]
        k_ref[:, column(j)] = (block * cosine + swap_halves(block) * sine).astype(BF)
    saves[3].start()
    allowed = allowed_keys(length)
    for j in range(8):
        pair = stacked(q_ref[:, column(j)])
        probs = softmax(pair, both(k_ref[:, column(j // 2)], j % 2), allowed).astype(BF)
        probs_ref[j] = probs
        saves[6 + j].start()
        att_ref[:, column(j)] = unstacked(nn(probs, both(v_ref[:, column(j // 2)], j % 2))).astype(BF)
    saves[5].start()
    attended = att_ref[...]
    for copy in copies[5:]:
        copy.wait()
    orank = jnp.where(mask, nn(attended, ao[...]), 0.0).astype(BF)
    orank_ref[...] = orank
    hidden = x + nn(attended, wo[...]) + nn(orank, bo[...])
    hidden_ref[...] = hidden
    factor2 = lax.rsqrt(jnp.mean(hidden * hidden, axis=1, keepdims=True) + NORM_EPS)
    normed2 = (hidden * factor2 * g2_ref[...]).astype(BF)
    spread = jnp.where(
        lax.broadcasted_iota(jnp.int32, (experts, LANES), 0)
        == lax.broadcasted_iota(jnp.int32, (experts, LANES), 1), 1.0, 0.0,
    ).astype(BF)
    wide = tn(router_ref[...], spread).astype(BF)
    wide_ref[...] = wide
    logits = nn(normed2, wide)
    routes = routes_ref[...]
    number = lax.broadcasted_iota(jnp.int32, (LANES, TOK_DEV), 0)
    named = routes[0:1, :] == number
    for k in range(1, routes.shape[0]):
        named = named | (routes[k : k + 1, :] == number)
    selected = jnp.where(named, 1.0, 0.0).T > 0.5
    top = jnp.max(jnp.where(selected, logits, -1e30), axis=1, keepdims=True)
    chosen = jnp.where(selected, jnp.exp(jnp.minimum(logits - top, 0.0)), 0.0)
    live = lax.broadcasted_iota(jnp.int32, (TOK_DEV, 1), 0) < length
    gates = chosen * jnp.where(live, 1.0 / jnp.sum(chosen, axis=1, keepdims=True), 0.0)
    high = gates.astype(BF).astype(F32)
    meta = high + pltpu.roll(gates - high, 32, 1) + jnp.where(lane >= 96, adapter.astype(F32), 0.0)
    payload_ref[:, :MODEL_WIDTH] = normed2
    payload_ref[:, MODEL_WIDTH:] = meta.astype(BF)
    for save in saves:
        save.wait()


def attention_forward(scalars, x, g1, g2, cosine, sine, routes, router, weights):
    experts = router.shape[0]
    saved = [
        (TOK_DEV, MODEL_WIDTH),
        (TOK_DEV, 3 * LANES),
        (TOK_DEV, MODEL_WIDTH),
        (TOK_DEV, HALF_WIDTH),
        (TOK_DEV, HALF_WIDTH),
        (TOK_DEV, MODEL_WIDTH),
        (8, 2 * TOK_DEV, TOK_DEV),
    ]
    return pl.pallas_call(
        functools.partial(forward_body, experts=experts),
        out_shape=[
            shape(TOK_DEV, MODEL_WIDTH, dtype=F32),
            shape(TOK_DEV, META),
            shape(MODEL_WIDTH, LANES),
            shape(TOK_DEV, LANES),
        ]
        + [shape(*dims) for dims in saved],
        in_specs=[SMEM] + [VMEM] * 7 + [ANY] * 8,
        out_specs=[VMEM] * 4 + [ANY] * 7,
        scratch_shapes=[pltpu.VMEM(w.shape, BF) for w in weights]
        + [pltpu.VMEM(dims, BF) for dims in saved]
        + [pltpu.SemaphoreType.DMA((22,))],
        compiler_params=pltpu.CompilerParams(vmem_limit_bytes=VMEM_LIMIT),
        cost_estimate=pl.CostEstimate(flops=3_000_000_000, bytes_accessed=20_000_000, transcendentals=1_000_000),
        name="attention_forward",
    )(scalars, x, g1, g2, cosine, sine, routes, router, *weights)


def backward_body(
    scalars, g1_ref, g2_ref, cos_ref, sin_ref, hidden_ref, keep_ref, near_ref, far_ref, og_ref, orank_ref,
    *refs,
):
    (bo_h, wo_h, ao_h, att_h, q_h, k_h, v_h, probs_h, low_h, bq_h, bkv_h, normed_h, wq_h, wkv_h, aat_h, x_h) = refs[:16]
    gi_ref, mine_ref, send_ref = refs[16:19]
    bo, wo, ao, att, q_ref, k_ref, v_ref, probs_ref, lowrank_ref, bq, bkv, normed, wq, wkv, aat, x_ref = refs[19:35]
    pack, ga_s, gq_s, gk_s, gv_s, sems = refs[35:]
    copies = copies_of(list(zip(refs[:16], refs[19:35])), sems)
    for copy in copies:
        copy.start()
    adapter = scalars[0]
    length = scalars[1]
    side = scalars[2]
    mask = lanes_of(TOK_DEV) // ADAPTER_RANK == adapter

    def masked(values):
        return jnp.where(mask, values, 0.0).astype(BF)

    hidden = hidden_ref[...]
    factor2 = lax.rsqrt(jnp.mean(hidden * hidden, axis=1, keepdims=True) + NORM_EPS)
    live = lax.broadcasted_iota(jnp.int32, (TOK_DEV, 1), 0) < length
    grad_live = jnp.where(live, og_ref[...].astype(F32), 0.0)
    y = (keep_ref[...].astype(F32) + near_ref[...].astype(F32) + far_ref[...].astype(F32)) * g2_ref[...]
    inner = jnp.mean(y * hidden, axis=1, keepdims=True)
    grad_hidden = grad_live + factor2 * (y - hidden * (factor2 * factor2 * inner))
    gi_ref[...] = grad_hidden
    branch = grad_hidden.astype(BF)
    pack[768:896, :] = tn(orank_ref[...], branch).astype(BF)
    for copy in copies[:4]:
        copy.wait()
    grad_orank = masked(nt(branch, bo[...]))
    pack[640:768, :] = tn(grad_orank, att[...]).astype(BF)
    ga_s[...] = (nt(branch, wo[...]) + nt(grad_orank, ao[...])).astype(BF)
    cosine = cos_ref[...]
    sine = sin_ref[...]
    low = lanes_of(TOK_DEV) < HEAD_WIDTH
    scale = HEAD_WIDTH**-0.5
    for copy in copies[4:8]:
        copy.wait()

    def group(i, carry):
        here = pl.ds(pl.multiple_of(i * LANES, LANES), LANES)
        sums = []
        for odd in range(2):
            j = 2 * i + odd
            there = pl.ds(pl.multiple_of(j * LANES, LANES), LANES)
            pair = stacked(q_ref[:, there])
            key_both = both(k_ref[:, here], odd)
            value_both = both(v_ref[:, here], odd)
            probs = probs_ref[j]
            grad_pair = stacked(ga_s[:, there])
            grad_probs = nt(grad_pair, value_both).astype(BF).astype(F32)
            grad_v = tn(probs, grad_pair)
            wide = probs.astype(F32)
            weighted = wide * grad_probs
            scores = (weighted - wide * jnp.sum(weighted, axis=1, keepdims=True)).astype(BF)
            grad_q = unstacked(nn(scores, key_both)) * scale
            gq_s[:, there] = (grad_q * cosine - swap_halves(grad_q) * sine).astype(BF)
            grad_k = tn(scores, pair) * scale
            sums.append((grad_k + pltpu.roll(grad_k, HEAD_WIDTH, 1), grad_v + pltpu.roll(grad_v, HEAD_WIDTH, 1)))
        block = jnp.where(low, sums[0][0], sums[1][0])
        gk_s[:, here] = (block * cosine - swap_halves(block) * sine).astype(BF)
        gv_s[:, here] = jnp.where(low, sums[0][1], sums[1][1]).astype(BF)
        return carry

    lax.fori_loop(0, 4, group, 0)
    gq = gq_s[...]
    gk = gk_s[...]
    gv = gv_s[...]
    for copy in copies[8:12]:
        copy.wait()
    pack[384:512, :] = tn(lowrank_ref[:, column(0)], gq).astype(BF)
    pack[512:640, :HALF_WIDTH] = tn(lowrank_ref[:, column(1)], gk).astype(BF)
    pack[512:640, HALF_WIDTH:] = tn(lowrank_ref[:, column(2)], gv).astype(BF)
    grad_rank = jnp.concatenate(
        [masked(nt(gq, bq[...])), masked(nt(gk, bkv[0])), masked(nt(gv, bkv[1]))], axis=1
    )
    pack[0:384, :] = tn(grad_rank, normed[...]).astype(BF)
    for copy in copies[12:]:
        copy.wait()
    grad_normed = (
        nt(gq, wq[...])
        + nt(jnp.concatenate([gk, gv], axis=1), wkv[...])
        + nt(grad_rank, aat[...])
    )
    x = x_ref[...].astype(F32)
    factor = lax.rsqrt(jnp.mean(x * x, axis=1, keepdims=True) + NORM_EPS)
    z = grad_normed * g1_ref[...]
    inner = jnp.mean(z * x, axis=1, keepdims=True)
    gi_ref[...] += factor * (z - x * (factor * factor * inner))
    half = ATT_ROWS // 2
    mine_ref[...] = pack[pl.ds(pl.multiple_of(side * half, 16), half), :]
    send_ref[...] = pack[pl.ds(pl.multiple_of((1 - side) * half, 16), half), :]


def attention_backward(scalars, arrays, later):
    half = ATT_ROWS // 2
    return pl.pallas_call(
        backward_body,
        out_shape=[shape(TOK_DEV, MODEL_WIDTH, dtype=F32), shape(half, MODEL_WIDTH), shape(half, MODEL_WIDTH)],
        in_specs=[SMEM] + [VMEM] * len(arrays) + [ANY] * len(later),
        out_specs=[VMEM] * 3,
        scratch_shapes=[pltpu.VMEM(w.shape, BF) for w in later]
        + [
            pltpu.VMEM((ATT_ROWS, MODEL_WIDTH), BF),
            pltpu.VMEM((TOK_DEV, MODEL_WIDTH), BF),
            pltpu.VMEM((TOK_DEV, MODEL_WIDTH), BF),
            pltpu.VMEM((TOK_DEV, HALF_WIDTH), BF),
            pltpu.VMEM((TOK_DEV, HALF_WIDTH), BF),
            pltpu.SemaphoreType.DMA((len(later),)),
        ],
        compiler_params=pltpu.CompilerParams(vmem_limit_bytes=VMEM_LIMIT),
        cost_estimate=pl.CostEstimate(flops=6_000_000_000, bytes_accessed=24_000_000, transcendentals=1_000_000),
        name="attention_backward",
    )(scalars, *arrays, *later)


def expert_body(
    scalars, *refs, expert, held, count, experts, carried, seeded, emit, last,
):
    refs = list(refs)

    def take(number):
        taken = refs[:number]
        del refs[:number]
        return taken

    x_blocks = take(count)
    g_blocks = take(count)
    ain_h, win_h, bin_h, adn_h, wdn_h, bdn_h = take(6)
    if carried:
        f_in, b_in, c_in = take(3)
    if held:
        take(3)
    seeds = take(4) if seeded else None
    if last:
        wr_ref, f_top, f_low, b_top, b_low = take(5)
    else:
        f_out, b_out, c_out = take(3)
    if emit:
        emitted = take(4)
    else:
        mine_ref, send_ref = take(2)
    xs, gs_buf, ain, win, bin_, adn, wdn, bdn, acc_a, acc_bi, acc_ad, acc_bd, pack, xsem, gsem, wsem = refs[:16]
    if last:
        f_buf, b_buf, fsem, bsem = refs[16:]
    sums = [acc_a, acc_bi, acc_ad, acc_bd]
    step = pl.program_id(0)
    slot = lax.rem(step, 2)
    early = [
        pltpu.make_async_copy(source.at[expert], target, wsem.at[index])
        for index, (source, target) in enumerate([(ain_h, ain), (win_h, win), (bin_h, bin_)])
    ]
    late = [
        pltpu.make_async_copy(source.at[expert], target, wsem.at[3 + index])
        for index, (source, target) in enumerate([(adn_h, adn), (wdn_h, wdn), (bdn_h, bdn)])
    ]

    def fetch(block):
        pltpu.make_async_copy(x_blocks[block], xs.at[block % 2], xsem.at[block % 2]).start()
        pltpu.make_async_copy(g_blocks[block], gs_buf.at[block % 2], gsem.at[block % 2]).start()

    @pl.when(step == 0)
    def _():
        fetch(0)
        for copy in early + late:
            copy.start()
        for index, total in enumerate(sums):
            total[...] = seeds[index][...] if seeded else jnp.zeros_like(total)
        for copy in early:
            copy.wait()

    for block in range(1, count):
        @pl.when(step == block - 1)
        def _(block=block):
            fetch(block)

    pltpu.make_async_copy(x_blocks[0], xs.at[slot], xsem.at[slot]).wait()
    pltpu.make_async_copy(g_blocks[0], gs_buf.at[slot], gsem.at[slot]).wait()
    if last:
        @pl.when(step >= 2)
        def _():
            pltpu.make_async_copy(b_buf.at[slot], b_top.at[pl.ds(0, TOK_DEV)], bsem.at[slot]).wait()
            pltpu.make_async_copy(f_buf.at[slot], f_top.at[pl.ds(0, TOK_DEV)], fsem.at[slot]).wait()

    eid = scalars[0]
    side = scalars[1]
    x = xs[slot, :, :MODEL_WIDTH]
    meta = xs[slot, :, MODEL_WIDTH:].astype(F32)
    lane = lanes_of(TOK_DEV)
    adapter = meta[:, 96:97].astype(jnp.int32)
    mask = lane // ADAPTER_RANK == adapter

    def masked(values):
        return jnp.where(mask, values, 0.0).astype(BF)

    gates = jnp.where(lane < experts, meta + pltpu.roll(meta, 96, 1), 0.0)
    here = lane == eid
    gate_e = jnp.sum(jnp.where(here, gates, 0.0), axis=1, keepdims=True)
    low = nn(x, ain[...])
    low_gate = masked(low[:, :LANES])
    low_up = masked(low[:, LANES:])
    gate = nn(x, win[:, :HALF_WIDTH]) + nn(low_gate, bin_[0])
    up = nn(x, win[:, HALF_WIDTH:]) + nn(low_up, bin_[1])
    sig = 1.0 / (1.0 + jnp.exp(-gate))
    silu = gate * sig
    active = (silu * up).astype(BF)

    @pl.when(step == 0)
    def _():
        for copy in late:
            copy.wait()

    down = masked(nn(active, adn[...]))
    grad = gs_buf[slot].astype(F32)
    out = nn(active, wdn[...]) + nn(down, bdn[...])
    grad_gate_e = jnp.sum(out * grad, axis=1, keepdims=True)
    weighted = gate_e * out
    if carried:
        weighted = weighted + f_in[...]
    if last:
        f_buf[slot] = weighted.astype(BF)
    else:
        f_out[...] = weighted
    slot_grad = (gate_e * grad).astype(BF)
    grad_down = masked(nt(slot_grad, bdn[...]))
    grad_active = nt(slot_grad, wdn[...]) + nt(grad_down, adn[...])
    gate_grad = (grad_active * up * sig * (1.0 + gate * (1.0 - sig))).astype(BF)
    up_grad = (grad_active * silu).astype(BF)
    grad_low = jnp.concatenate([masked(nt(gate_grad, bin_[0])), masked(nt(up_grad, bin_[1]))], axis=1)
    both_grads = jnp.concatenate([gate_grad, up_grad], axis=1)
    rows = nt(both_grads, win[...]) + nt(grad_low, ain[...])
    part = (gate_e * grad_gate_e) * (jnp.where(here, 1.0, 0.0) - gates)
    if carried:
        rows = rows + b_in[...]
        part = part + c_in[...]
    if last:
        rows = rows + nt(part.astype(BF), wr_ref[...])

        b_buf[slot] = rows.astype(BF)
        for block in range(count):
            @pl.when(step == block)
            def _(block=block):
                part_rows = pl.ds(block // 2 * TOK_DEV, TOK_DEV)
                f_to = (f_low if block % 2 else f_top).at[part_rows]
                b_to = (b_low if block % 2 else b_top).at[part_rows]
                pltpu.make_async_copy(b_buf.at[block % 2], b_to, bsem.at[block % 2]).start()
                pltpu.make_async_copy(f_buf.at[block % 2], f_to, fsem.at[block % 2]).start()
    else:
        c_out[...] = part
        b_out[...] = rows
    acc_a[...] += tn(grad_low, x)
    acc_bi[:, :HALF_WIDTH] += tn(low_gate, gate_grad)
    acc_bi[:, HALF_WIDTH:] += tn(low_up, up_grad)
    acc_ad[...] += tn(grad_down, active)
    acc_bd[...] += tn(down, slot_grad)

    @pl.when(step == count - 1)
    def _():
        if emit:
            for target, total in zip(emitted, sums):
                target[...] = total[...]
        else:
            pack[0:256, :] = acc_a[...].astype(BF)
            pack[256:384, :] = acc_bi[...].astype(BF)
            pack[384:512, :] = acc_bd[...].astype(BF)
            pack[512:576, :HALF_WIDTH] = acc_ad[0:64, :].astype(BF)
            pack[512:576, HALF_WIDTH:] = acc_ad[64:128, :].astype(BF)
            half = PACK_ROWS // 2
            mine_ref[...] = pack[pl.ds(pl.multiple_of(side * half, 16), half), :]
            send_ref[...] = pack[pl.ds(pl.multiple_of((1 - side) * half, 16), half), :]
        if last:
            for index in range(2):
                pltpu.make_async_copy(b_buf.at[index], b_top.at[pl.ds(0, TOK_DEV)], bsem.at[index]).wait()
                pltpu.make_async_copy(f_buf.at[index], f_top.at[pl.ds(0, TOK_DEV)], fsem.at[index]).wait()


def expert_call(
    expert, scalars, x_blocks, g_blocks, weights, experts, blocks, start=0,
    carried=None, halves=None, seeds=None, emit=False, router_wide=None,
):
    count = len(x_blocks)
    total = blocks * TOK_DEV
    last = router_wide is not None
    rows = lambda width: pl.BlockSpec((TOK_DEV, width), lambda i, *_: (i + start, 0))
    whole = lambda *dims: pl.BlockSpec(dims, lambda i, *_: (0,) * len(dims), pipeline_mode=pl.Buffered(1))
    fixed = lambda *dims: pl.BlockSpec(dims, lambda i, *_: (0,) * len(dims))
    sum_dims = [(256, MODEL_WIDTH), (128, MODEL_WIDTH), (128, HALF_WIDTH), (128, MODEL_WIDTH)]
    in_specs = [ANY] * (2 * count + 6)
    args = [*x_blocks, *g_blocks, *weights]
    aliases = {}
    if carried is not None:
        in_specs += [rows(MODEL_WIDTH), rows(MODEL_WIDTH), rows(LANES)]
        args += list(carried)
    if halves is not None:
        aliases = {1 + len(args) + i: i for i in range(3)}
        in_specs += [ANY] * 3
        args += list(halves)
    if seeds is not None:
        in_specs += [whole(*d) for d in sum_dims]
        args += list(seeds)
    if last:
        in_specs.append(whole(MODEL_WIDTH, LANES))
        args.append(router_wide)
        outs = [shape(count // 2 * TOK_DEV, MODEL_WIDTH)] * 4
        out_specs = [ANY] * 4
    else:
        outs = [
            shape(total, MODEL_WIDTH, dtype=F32),
            shape(total, MODEL_WIDTH, dtype=F32),
            shape(total, LANES, dtype=F32),
        ]
        out_specs = [rows(MODEL_WIDTH), rows(MODEL_WIDTH), rows(LANES)]
    half = PACK_ROWS // 2
    if emit:
        outs += [shape(*d, dtype=F32) for d in sum_dims]
        out_specs += [fixed(*d) for d in sum_dims]
    else:
        outs += [shape(half, MODEL_WIDTH)] * 2
        out_specs += [fixed(half, MODEL_WIDTH)] * 2
    scratch = [pltpu.VMEM((2, TOK_DEV, META), BF), pltpu.VMEM((2, TOK_DEV, MODEL_WIDTH), BF)]
    scratch += [pltpu.VMEM(w.shape[1:], BF) for w in weights]
    scratch += [pltpu.VMEM(d, F32) for d in sum_dims]
    scratch += [
        pltpu.VMEM((PACK_ROWS, MODEL_WIDTH), BF),
        pltpu.SemaphoreType.DMA((2,)),
        pltpu.SemaphoreType.DMA((2,)),
        pltpu.SemaphoreType.DMA((6,)),
    ]
    if last:
        scratch += [pltpu.VMEM((2, TOK_DEV, MODEL_WIDTH), BF)] * 2 + [pltpu.SemaphoreType.DMA((2,))] * 2
    return pl.pallas_call(
        functools.partial(
            expert_body, expert=expert, held=halves is not None, count=count, experts=experts,
            carried=carried is not None, seeded=seeds is not None, emit=emit, last=last,
        ),
        out_shape=outs,
        grid_spec=pltpu.PrefetchScalarGridSpec(
            num_scalar_prefetch=1, grid=(count,), in_specs=in_specs, out_specs=out_specs, scratch_shapes=scratch
        ),
        input_output_aliases=aliases,
        compiler_params=pltpu.CompilerParams(
            dimension_semantics=("arbitrary",), vmem_limit_bytes=VMEM_LIMIT
        ),
        cost_estimate=pl.CostEstimate(
            flops=count * TOK_DEV * 9_800_000, bytes_accessed=5_000_000 * count, transcendentals=0
        ),
        name="expert_step",
    )(scalars, *args)


def expert_finish_body(scalars, *refs, count, held):
    pieces = refs[: 2 * count]
    a_in, b_in, a_down, b_down, pack = refs[2 * count + held :]
    side = scalars[0]
    half = PACK_ROWS // 2
    step = pl.program_id(0)
    for index in range(count):
        @pl.when(step == index)
        def _(index=index):
            pack[pl.ds(pl.multiple_of(side * half, 16), half), :] = pieces[2 * index][...]
            pack[pl.ds(pl.multiple_of((1 - side) * half, 16), half), :] = pieces[2 * index + 1][...]
    a_in[0] = pack[0:256, :].astype(F32).T
    b_in[0, 0] = pack[256:384, :HALF_WIDTH].astype(F32)
    b_in[0, 1] = pack[256:384, HALF_WIDTH:].astype(F32)
    b_down[0] = pack[384:512, :].astype(F32)
    a_down[0] = jnp.concatenate([pack[512:576, :HALF_WIDTH], pack[512:576, HALF_WIDTH:]], axis=0).astype(F32).T


def expert_finish(side, sums, start=0, held=()):
    half = PACK_ROWS // 2
    count = len(sums)
    pieces = [piece for one in sums for piece in (one.mine, one.got)]
    block = lambda *dims: pl.BlockSpec((1,) + dims, lambda i, *_: (i + start,) + (0,) * len(dims))
    dims = [(MODEL_WIDTH, 256), (2, 128, HALF_WIDTH), (HALF_WIDTH, 128), (128, MODEL_WIDTH)]
    return pl.pallas_call(
        functools.partial(expert_finish_body, count=count, held=len(held)),
        out_shape=[shape(EXP_DEV, *d, dtype=F32) for d in dims],
        grid_spec=pltpu.PrefetchScalarGridSpec(
            num_scalar_prefetch=1,
            grid=(count,),
            in_specs=[
                pl.BlockSpec((half, MODEL_WIDTH), lambda i, *_: (0, 0), pipeline_mode=pl.Buffered(1))
            ] * len(pieces)
            + [ANY] * len(held),
            out_specs=[block(*d) for d in dims],
            scratch_shapes=[pltpu.VMEM((PACK_ROWS, MODEL_WIDTH), BF)],
        ),
        input_output_aliases={1 + len(pieces) + i: i for i in range(len(held))},
        compiler_params=pltpu.CompilerParams(
            dimension_semantics=("arbitrary",), vmem_limit_bytes=VMEM_LIMIT
        ),
        cost_estimate=pl.CostEstimate(flops=1_000_000, bytes_accessed=4_000_000 * count, transcendentals=0),
        name="expert_finish",
    )(side, *pieces, *held)


def attention_finish_body(scalars, mine_ref, got_ref, a_ref, bq_ref, bkv_ref, oa_ref, ob_ref, pack):
    side = scalars[0]
    half = ATT_ROWS // 2
    pack[pl.ds(pl.multiple_of(side * half, 16), half), :] = mine_ref[...]
    pack[pl.ds(pl.multiple_of((1 - side) * half, 16), half), :] = got_ref[...]
    a_ref[...] = pack[0:384, :].astype(F32).T
    bq_ref[...] = pack[384:512, :].astype(F32)
    bkv_ref[0] = pack[512:640, :HALF_WIDTH].astype(F32)
    bkv_ref[1] = pack[512:640, HALF_WIDTH:].astype(F32)
    oa_ref[...] = pack[640:768, :].astype(F32).T
    ob_ref[...] = pack[768:896, :].astype(F32)


def attention_finish(side, mine, got):
    dims = [(MODEL_WIDTH, 384), (128, MODEL_WIDTH), (2, 128, HALF_WIDTH), (MODEL_WIDTH, 128), (128, MODEL_WIDTH)]
    return pl.pallas_call(
        attention_finish_body,
        out_shape=[shape(*d, dtype=F32) for d in dims],
        in_specs=[SMEM, VMEM, VMEM],
        out_specs=[VMEM] * 5,
        scratch_shapes=[pltpu.VMEM((ATT_ROWS, MODEL_WIDTH), BF)],
        compiler_params=pltpu.CompilerParams(vmem_limit_bytes=VMEM_LIMIT),
        cost_estimate=pl.CostEstimate(flops=1_000_000, bytes_accessed=6_000_000, transcendentals=0),
        name="attention_finish",
    )(side, mine, got)


def swap(values, axis, bit):
    size = lax.axis_size(axis)
    return lax.ppermute(values, axis, [(i, i ^ (1 << bit)) for i in range(size)])


def axis_bits(axis):
    return lax.axis_size(axis).bit_length() - 1


def tie(first, second):
    return lax.optimization_barrier((first, second))


def add(first, second):
    return (first.astype(F32) + second.astype(F32)).astype(BF)


def far_blocks(values):
    blocks = {0: values}
    for bit in reversed(range(1, axis_bits("expert"))):
        for index in list(blocks):
            blocks[index ^ (1 << bit)] = swap(blocks[index], "expert", bit)
    return blocks


def near_blocks(far):
    blocks = []
    for index in sorted(far):
        if index:
            blocks += [far[index], swap(far[index], "expert", 0)]
    return blocks


class Return:
    def __init__(self, top, low):
        self.top = top
        self.got = swap(low, "expert", 0)
        self.bits = list(reversed(range(1, axis_bits("expert"))))
        self.parts = []

    def reduce(self):
        count = self.top.shape[0] // TOK_DEV
        total = add(self.top, self.got)
        self.far = {2 * (i + 1): total[i * TOK_DEV : (i + 1) * TOK_DEV] for i in range(count)}

    def pick(self):
        self.bit = self.bits.pop(0)
        self.sent = [index for index in sorted(self.far) if index >> self.bit & 1]
        blocks = [self.far.pop(index) for index in self.sent]
        return blocks[0] if len(blocks) == 1 else jnp.concatenate(blocks, axis=0)

    def launch(self, send):
        self.got = swap(send, "expert", self.bit)

    def receive(self):
        for i, index in enumerate(self.sent):
            block = self.got[i * TOK_DEV : (i + 1) * TOK_DEV] if len(self.sent) > 1 else self.got
            index ^= 1 << self.bit
            if index:
                self.far[index] = add(self.far[index], block)
            else:
                self.parts.append(block)

    def finish(self):
        while self.bits:
            self.launch(self.pick())
            self.receive()
        total = self.parts[0]
        for part in self.parts[1:]:
            total = add(total, part)
        return total


class Holder:
    def __init__(self, got):
        self.got = got


class Sum:
    def __init__(self, mine, send, stages):
        self.path = []
        self.stages = list(stages)
        self.mine = mine
        self.send = send
        self.down = True
        self.target = self.stages.pop(0)
        self.path.append(self.target)

    def launch(self):
        self.got = swap(self.send, *self.target)
        return self

    def prepare(self):
        if self.down:
            values = add(self.mine, self.got)
            if self.stages:
                self.target = self.stages.pop(0)
                axis, bit = self.target
                rows, width = values.shape
                if rows % 16:
                    self.mine = self.send = values
                    return
                self.path.append(self.target)
                side = (lax.axis_index(axis) >> bit) & 1
                halves = values.reshape(2, rows // 2, width)
                self.mine = lax.dynamic_index_in_dim(halves, side, 0, keepdims=False)
                self.send = lax.dynamic_index_in_dim(halves, 1 - side, 0, keepdims=False)
                return
            self.down = False
        else:
            axis, bit = self.path.pop()
            side = (lax.axis_index(axis) >> bit) & 1
            low = jnp.where(side == 0, self.mine, self.got)
            high = jnp.where(side == 0, self.got, self.mine)
            values = jnp.concatenate([low, high], axis=0)
        self.target = self.path[-1]
        self.mine = self.send = values

    def pending(self):
        return self.down or len(self.path) > 1


def prepare(ones):
    for one in ones:
        one.prepare()


def step(*ones):
    ones = [one for one in ones if one.pending()]
    prepare(ones)
    for one in ones:
        one.launch()


def sync(holders, *extras):
    arrays = tuple(holder.got for holder in holders) + extras
    arrays = lax.optimization_barrier(arrays)
    for holder, got in zip(holders, arrays):
        holder.got = got
    return arrays[len(holders) :]


def on_device(
    inputs,
    lengths,
    routes,
    adapter_of_sequence,
    first_norm_gain,
    query_weight,
    key_value_weight,
    output_weight,
    second_norm_gain,
    router_weight,
    expert_input_weight,
    expert_down_weight,
    attention_first_factors,
    query_second_factors,
    key_value_second_factors,
    output_first_factors,
    output_second_factors,
    expert_input_first_factors,
    expert_input_second_factors,
    expert_down_first_factors,
    expert_down_second_factors,
    output_gradient,
):
    blocks = lax.axis_size("expert")
    experts = EXP_DEV * blocks
    place = lax.axis_index("expert")
    dp_side = lax.axis_index("dp") & 1
    core_side = place & 1
    grad_far = far_blocks(output_gradient)
    cosine, sine = rope_tables()
    scalars = jnp.stack([adapter_of_sequence[0], lengths[0], core_side]).astype(jnp.int32)
    g1 = first_norm_gain[None]
    g2 = second_norm_gain[None]
    weights = [
        attention_first_factors,
        query_weight,
        query_second_factors,
        key_value_weight,
        key_value_second_factors,
        output_first_factors,
        output_weight,
        output_second_factors,
    ]
    hidden, payload, router_wide, out_rank, normed, lowrank, queries, keys, values, attended, probs = attention_forward(
        scalars, inputs, g1, g2, cosine, sine, routes.T, router_weight.T, weights
    )
    for index in grad_far:
        if index:
            grad_far[index], payload = tie(grad_far[index], payload)
    row_far = far_blocks(payload)
    near = [[values, swap(values, "expert", 0)] for values in (payload, output_gradient)]
    expert_weights = [
        expert_input_first_factors,
        expert_input_weight,
        expert_input_second_factors,
        expert_down_first_factors,
        expert_down_weight,
        expert_down_second_factors,
    ]
    dp_stages = [("dp", bit) for bit in range(axis_bits("dp"))]
    sums = []
    first_number = EXP_DEV * place
    number = jnp.stack([first_number, dp_side]).astype(jnp.int32)
    *halves, s0, s1, s2, s3 = expert_call(
        0, number, *near, expert_weights, experts, blocks, emit=True
    )
    for far in (row_far, grad_far):
        for index in far:
            if index:
                far[index], s0 = tie(far[index], s0)
    row_blocks = near[0] + near_blocks(row_far)
    grad_blocks = near[1] + near_blocks(grad_far)
    *carried, mine, send = expert_call(
        0, number, row_blocks[2:], grad_blocks[2:], expert_weights, experts, blocks,
        start=2, halves=halves, seeds=(s0, s1, s2, s3),
    )
    sums.append(Sum(mine, send, dp_stages).launch())
    for local in range(1, EXP_DEV - 1):
        number = jnp.stack([first_number + local, dp_side]).astype(jnp.int32)
        (number,) = sync(sums[: local - 1], number)
        step(*sums[: local - 1])
        *carried, mine, send = expert_call(
            local, number, row_blocks, grad_blocks, expert_weights, experts, blocks, carried=carried
        )
        sums.append(Sum(mine, send, dp_stages).launch())
    local = EXP_DEV - 1
    number = jnp.stack([first_number + local, dp_side]).astype(jnp.int32)
    (number,) = sync(sums[:-1], number)
    step(*sums[:-1])
    mix_top, mix_low, row_top, row_low, s0, s1, s2, s3 = expert_call(
        local, number, row_blocks[2:], grad_blocks[2:], expert_weights, experts, blocks,
        start=2, carried=carried, router_wide=router_wide, emit=True,
    )
    (row_low,) = sync(sums, row_low)
    row = Return(row_top, row_low)
    mix = Return(mix_top, mix_low)
    step(*sums)
    row.reduce()
    row_send = row.pick()
    row_send, number = tie(row_send, number)
    row.launch(row_send)
    mix_top, mix_low, row_top, row_low, mine, send = expert_call(
        local, number, row_blocks[:2], grad_blocks[:2], expert_weights, experts, blocks,
        carried=carried, seeds=(s0, s1, s2, s3), router_wide=router_wide,
    )
    row_low, mix_low = sync(sums + [row, mix], row_low, mix_low)
    row_near = Holder(swap(row_low, "expert", 0))
    sums.append(Sum(mine, send, dp_stages).launch())
    step(*sums[:-1])
    row.receive()
    row_far = row.finish()
    mix_near = Holder(swap(mix_low, "expert", 0))
    mix.reduce()
    mix.launch(mix.pick())
    part_sends = [one.send for one in sums]
    sync([row_near, mix_near], *part_sends)
    grad_input, att_mine, att_send = attention_backward(
        scalars,
        [g1, g2, cosine, sine, hidden, row_top, row_near.got, row_far, output_gradient, out_rank],
        [output_second_factors, output_weight, output_first_factors, attended, queries, keys, values, probs]
        + [lowrank, query_second_factors, key_value_second_factors, normed, query_weight, key_value_weight]
        + [attention_first_factors, inputs],
    )
    (att_send,) = sync(sums + [mix], att_send)
    mix.receive()
    mix_far = mix.finish()
    stages = [("expert", bit) for bit in range(axis_bits("expert"))] + dp_stages
    total = Sum(att_mine, att_send, stages).launch()
    step(*sums)
    step(total)
    sync(sums + [total])
    step(total, *sums[2:])
    sync(sums[2:] + [total])
    step(total, *sums[1:])
    step(total)
    sync([total, sums[3]])
    step(total, sums[3])
    sync(sums[1:] + [total])
    step(total)
    sync([total, sums[3]])
    step(total, sums[3])
    for one in sums:
        while one.pending():
            step(one)
    dp_piece = dp_side[None].astype(jnp.int32)
    held = list(expert_finish(dp_piece, sums[:3]))
    (held[3],) = sync([total, sums[3]], held[3])
    while total.pending():
        step(total)
    expert_grads = expert_finish(dp_piece, sums[3:], 3, held)
    live = (jnp.arange(TOK_DEV, dtype=jnp.int32) < lengths[0]).astype(F32)[:, None]
    mixture = mix_top.astype(F32) + mix_near.got.astype(F32) + mix_far.astype(F32)
    output = (live * (hidden + mixture)).astype(BF)
    side = core_side[None].astype(jnp.int32)
    attention_grads = attention_finish(side, total.mine, total.got)
    return (output, grad_input, *attention_grads, *expert_grads)


def solution(mesh):
    rows = P(("dp", "expert"), None)
    each = P(("dp", "expert"))
    three = P("expert", None, None)
    four = P("expert", None, None, None)
    return jax.shard_map(
        on_device,
        mesh=mesh,
        in_specs=(
            (rows, each, rows, each)
            + (P(),) * 6
            + (three, three)
            + (P(),) * 5
            + (three, four, three, three, rows)
        ),
        out_specs=(rows, rows) + (P(),) * 5 + (three, four, three, three),
        check_vma=False,
    )
```

```python
import functools

import jax
import jax.numpy as jnp
import numpy as np
from jax import lax
from jax.experimental import pallas as pl
from jax.experimental.pallas import tpu as pltpu
from jax.sharding import PartitionSpec as P

MODEL_WIDTH = 1024
HALF_WIDTH = 512
HEAD_WIDTH = 64
ADAPTER_RANK = 16
TOK_DEV = 256
EXP_DEV = 4
LANES = 128
META = MODEL_WIDTH + LANES
PACK_ROWS = 576
ATT_ROWS = 896
NORM_EPS = 1e-06
ROPE_BASE = 10000.0
F32 = jnp.float32
BF = jnp.bfloat16
ANY = pl.BlockSpec(memory_space=pl.ANY)
SMEM = pl.BlockSpec(memory_space=pltpu.SMEM)
VMEM = pl.BlockSpec(memory_space=pltpu.VMEM)
VMEM_LIMIT = 60 * 1024 * 1024


def nn(a, b):
    return lax.dot_general(a, b, (((1,), (0,)), ((), ())), preferred_element_type=F32)


def nt(a, b):
    return lax.dot_general(a, b, (((1,), (1,)), ((), ())), preferred_element_type=F32)


def tn(a, b):
    return lax.dot_general(a, b, (((0,), (0,)), ((), ())), preferred_element_type=F32)


def shape(*dims, dtype=BF):
    return jax.ShapeDtypeStruct(dims, dtype)


def rope_tables():
    inverse = ROPE_BASE ** (-2.0 * np.arange(HEAD_WIDTH // 2, dtype=np.float64) / HEAD_WIDTH)
    angles = np.arange(TOK_DEV, dtype=np.float64)[:, None] * inverse[None, :]
    cosine = np.tile(np.cos(angles), (1, 4)).astype(np.float32)
    sine = np.sin(angles)
    signed = np.concatenate([-sine, sine, -sine, sine], axis=1).astype(np.float32)
    return cosine, signed


def lanes_of(rows):
    return lax.broadcasted_iota(jnp.int32, (rows, LANES), 1)


def swap_halves(block):
    first = lanes_of(block.shape[0]) % HEAD_WIDTH < HEAD_WIDTH // 2
    return jnp.where(first, pltpu.roll(block, LANES - 32, 1), pltpu.roll(block, 32, 1))


def both(block, odd):
    low = lanes_of(block.shape[0]) < HEAD_WIDTH
    wide = block.astype(F32)
    other = pltpu.roll(wide, HEAD_WIDTH, 1)
    return (jnp.where(low, other, wide) if odd else jnp.where(low, wide, other)).astype(BF)


def stacked(block):
    low = lanes_of(block.shape[0]) < HEAD_WIDTH
    wide = block.astype(F32)
    return jnp.concatenate(
        [jnp.where(low, wide, 0.0).astype(BF), jnp.where(low, 0.0, wide).astype(BF)], axis=0
    )


def unstacked(pair):
    low = lanes_of(TOK_DEV) < HEAD_WIDTH
    return jnp.where(low, pair[:TOK_DEV], pair[TOK_DEV:])


def allowed_keys(length):
    row = lax.broadcasted_iota(jnp.int32, (2 * TOK_DEV, TOK_DEV), 0) % TOK_DEV
    col = lax.broadcasted_iota(jnp.int32, (2 * TOK_DEV, TOK_DEV), 1)
    return (col <= row) & (col < length)


def softmax(query_pair, key_both, allowed):
    scores = jnp.where(allowed, nt(query_pair, key_both) * (HEAD_WIDTH**-0.5), -1e30)
    exponent = jnp.exp(scores - jnp.max(scores, axis=1, keepdims=True))
    return exponent * (1.0 / jnp.sum(exponent, axis=1, keepdims=True))


def column(index):
    return slice(index * LANES, (index + 1) * LANES)


def copies_of(pairs, sems, start=0):
    return [
        pltpu.make_async_copy(source, target, sems.at[start + index]) for index, (source, target) in enumerate(pairs)
    ]


def forward_body(
    scalars, x_ref, g1_ref, g2_ref, cos_ref, sin_ref, routes_ref, router_ref,
    aat_h, wq_h, bq_h, wkv_h, bkv_h, ao_h, wo_h, bo_h,
    hidden_ref, payload_ref, wide_ref, orank_ref, normed_h, lowrank_h, q_h, k_h, v_h, att_h, probs_h,
    aat, wq, bq, wkv, bkv, ao, wo, bo, normed_ref, lowrank_ref, q_ref, k_ref, v_ref, att_ref, probs_ref, sems,
    *, experts,
):
    copies = copies_of(
        [(aat_h, aat), (wq_h, wq), (bq_h, bq), (wkv_h, wkv), (bkv_h, bkv), (ao_h, ao), (wo_h, wo), (bo_h, bo)], sems
    )
    saves = copies_of(
        [(normed_ref, normed_h), (lowrank_ref, lowrank_h), (q_ref, q_h), (k_ref, k_h), (v_ref, v_h), (att_ref, att_h)]
        + [(probs_ref.at[j], probs_h.at[j]) for j in range(8)],
        sems,
        8,
    )
    for copy in copies:
        copy.start()
    adapter = scalars[0]
    length = scalars[1]
    lane = lanes_of(TOK_DEV)
    mask = lane // ADAPTER_RANK == adapter
    x = x_ref[...].astype(F32)
    factor = lax.rsqrt(jnp.mean(x * x, axis=1, keepdims=True) + NORM_EPS)
    normed = (x * factor * g1_ref[...]).astype(BF)
    normed_ref[...] = normed
    saves[0].start()
    copies[0].wait()
    low = nn(normed, aat[...])
    ranks = [jnp.where(mask, low[:, column(i)], 0.0).astype(BF) for i in range(3)]
    for i in range(3):
        lowrank_ref[:, column(i)] = ranks[i]
    saves[1].start()
    cosine = cos_ref[...]
    sine = sin_ref[...]
    copies[1].wait()
    copies[2].wait()
    query_pre = nn(normed, wq[...]) + nn(ranks[0], bq[...])
    for j in range(8):
        block = query_pre[:, column(j)]
        q_ref[:, column(j)] = (block * cosine + swap_halves(block) * sine).astype(BF)
    saves[2].start()
    copies[3].wait()
    copies[4].wait()
    pre = nn(normed, wkv[...])
    key_pre = pre[:, :HALF_WIDTH] + nn(ranks[1], bkv[0])
    v_ref[...] = (pre[:, HALF_WIDTH:] + nn(ranks[2], bkv[1])).astype(BF)
    saves[4].start()
    for j in range(4):
        block = key_pre[:, column(j)]
        k_ref[:, column(j)] = (block * cosine + swap_halves(block) * sine).astype(BF)
    saves[3].start()
    allowed = allowed_keys(length)
    for j in range(8):
        pair = stacked(q_ref[:, column(j)])
        probs = softmax(pair, both(k_ref[:, column(j // 2)], j % 2), allowed).astype(BF)
        probs_ref[j] = probs
        saves[6 + j].start()
        att_ref[:, column(j)] = unstacked(nn(probs, both(v_ref[:, column(j // 2)], j % 2))).astype(BF)
    saves[5].start()
    attended = att_ref[...]
    for copy in copies[5:]:
        copy.wait()
    orank = jnp.where(mask, nn(attended, ao[...]), 0.0).astype(BF)
    orank_ref[...] = orank
    hidden = x + nn(attended, wo[...]) + nn(orank, bo[...])
    hidden_ref[...] = hidden
    factor2 = lax.rsqrt(jnp.mean(hidden * hidden, axis=1, keepdims=True) + NORM_EPS)
    normed2 = (hidden * factor2 * g2_ref[...]).astype(BF)
    spread = jnp.where(
        lax.broadcasted_iota(jnp.int32, (experts, LANES), 0)
        == lax.broadcasted_iota(jnp.int32, (experts, LANES), 1), 1.0, 0.0,
    ).astype(BF)
    wide = tn(router_ref[...], spread).astype(BF)
    wide_ref[...] = wide
    logits = nn(normed2, wide)
    routes = routes_ref[...]
    number = lax.broadcasted_iota(jnp.int32, (LANES, TOK_DEV), 0)
    named = routes[0:1, :] == number
    for k in range(1, routes.shape[0]):
        named = named | (routes[k : k + 1, :] == number)
    selected = jnp.where(named, 1.0, 0.0).T > 0.5
    top = jnp.max(jnp.where(selected, logits, -1e30), axis=1, keepdims=True)
    chosen = jnp.where(selected, jnp.exp(jnp.minimum(logits - top, 0.0)), 0.0)
    live = lax.broadcasted_iota(jnp.int32, (TOK_DEV, 1), 0) < length
    gates = chosen * jnp.where(live, 1.0 / jnp.sum(chosen, axis=1, keepdims=True), 0.0)
    high = gates.astype(BF).astype(F32)
    meta = high + pltpu.roll(gates - high, 32, 1) + jnp.where(lane >= 96, adapter.astype(F32), 0.0)
    payload_ref[:, :MODEL_WIDTH] = normed2
    payload_ref[:, MODEL_WIDTH:] = meta.astype(BF)
    for save in saves:
        save.wait()


def attention_forward(scalars, x, g1, g2, cosine, sine, routes, router, weights):
    experts = router.shape[0]
    saved = [
        (TOK_DEV, MODEL_WIDTH),
        (TOK_DEV, 3 * LANES),
        (TOK_DEV, MODEL_WIDTH),
        (TOK_DEV, HALF_WIDTH),
        (TOK_DEV, HALF_WIDTH),
        (TOK_DEV, MODEL_WIDTH),
        (8, 2 * TOK_DEV, TOK_DEV),
    ]
    return pl.pallas_call(
        functools.partial(forward_body, experts=experts),
        out_shape=[
            shape(TOK_DEV, MODEL_WIDTH, dtype=F32),
            shape(TOK_DEV, META),
            shape(MODEL_WIDTH, LANES),
            shape(TOK_DEV, LANES),
        ]
        + [shape(*dims) for dims in saved],
        in_specs=[SMEM] + [VMEM] * 7 + [ANY] * 8,
        out_specs=[VMEM] * 4 + [ANY] * 7,
        scratch_shapes=[pltpu.VMEM(w.shape, BF) for w in weights]
        + [pltpu.VMEM(dims, BF) for dims in saved]
        + [pltpu.SemaphoreType.DMA((22,))],
        compiler_params=pltpu.CompilerParams(vmem_limit_bytes=VMEM_LIMIT),
        cost_estimate=pl.CostEstimate(flops=3_000_000_000, bytes_accessed=20_000_000, transcendentals=1_000_000),
        name="attention_forward",
    )(scalars, x, g1, g2, cosine, sine, routes, router, *weights)


def backward_body(
    scalars, g1_ref, g2_ref, cos_ref, sin_ref, hidden_ref, keep_ref, near_ref, far_ref, og_ref, orank_ref,
    *refs,
):
    (bo_h, wo_h, ao_h, att_h, q_h, k_h, v_h, probs_h, low_h, bq_h, bkv_h, normed_h, wq_h, wkv_h, aat_h, x_h) = refs[:16]
    gi_ref, mine_ref, send_ref = refs[16:19]
    bo, wo, ao, att, q_ref, k_ref, v_ref, probs_ref, lowrank_ref, bq, bkv, normed, wq, wkv, aat, x_ref = refs[19:35]
    pack, ga_s, gq_s, gk_s, gv_s, sems = refs[35:]
    copies = copies_of(list(zip(refs[:16], refs[19:35])), sems)
    for copy in copies:
        copy.start()
    adapter = scalars[0]
    length = scalars[1]
    side = scalars[2]
    mask = lanes_of(TOK_DEV) // ADAPTER_RANK == adapter

    def masked(values):
        return jnp.where(mask, values, 0.0).astype(BF)

    hidden = hidden_ref[...]
    factor2 = lax.rsqrt(jnp.mean(hidden * hidden, axis=1, keepdims=True) + NORM_EPS)
    live = lax.broadcasted_iota(jnp.int32, (TOK_DEV, 1), 0) < length
    grad_live = jnp.where(live, og_ref[...].astype(F32), 0.0)
    y = (keep_ref[...].astype(F32) + near_ref[...].astype(F32) + far_ref[...].astype(F32)) * g2_ref[...]
    inner = jnp.mean(y * hidden, axis=1, keepdims=True)
    grad_hidden = grad_live + factor2 * (y - hidden * (factor2 * factor2 * inner))
    gi_ref[...] = grad_hidden
    branch = grad_hidden.astype(BF)
    pack[768:896, :] = tn(orank_ref[...], branch).astype(BF)
    for copy in copies[:4]:
        copy.wait()
    grad_orank = masked(nt(branch, bo[...]))
    pack[640:768, :] = tn(grad_orank, att[...]).astype(BF)
    ga_s[...] = (nt(branch, wo[...]) + nt(grad_orank, ao[...])).astype(BF)
    cosine = cos_ref[...]
    sine = sin_ref[...]
    low = lanes_of(TOK_DEV) < HEAD_WIDTH
    scale = HEAD_WIDTH**-0.5
    for copy in copies[4:8]:
        copy.wait()

    def group(i, carry):
        here = pl.ds(pl.multiple_of(i * LANES, LANES), LANES)
        sums = []
        for odd in range(2):
            j = 2 * i + odd
            there = pl.ds(pl.multiple_of(j * LANES, LANES), LANES)
            pair = stacked(q_ref[:, there])
            key_both = both(k_ref[:, here], odd)
            value_both = both(v_ref[:, here], odd)
            probs = probs_ref[j]
            grad_pair = stacked(ga_s[:, there])
            grad_probs = nt(grad_pair, value_both).astype(BF).astype(F32)
            grad_v = tn(probs, grad_pair)
            wide = probs.astype(F32)
            weighted = wide * grad_probs
            scores = (weighted - wide * jnp.sum(weighted, axis=1, keepdims=True)).astype(BF)
            grad_q = unstacked(nn(scores, key_both)) * scale
            gq_s[:, there] = (grad_q * cosine - swap_halves(grad_q) * sine).astype(BF)
            grad_k = tn(scores, pair) * scale
            sums.append((grad_k + pltpu.roll(grad_k, HEAD_WIDTH, 1), grad_v + pltpu.roll(grad_v, HEAD_WIDTH, 1)))
        block = jnp.where(low, sums[0][0], sums[1][0])
        gk_s[:, here] = (block * cosine - swap_halves(block) * sine).astype(BF)
        gv_s[:, here] = jnp.where(low, sums[0][1], sums[1][1]).astype(BF)
        return carry

    lax.fori_loop(0, 4, group, 0)
    gq = gq_s[...]
    gk = gk_s[...]
    gv = gv_s[...]
    for copy in copies[8:12]:
        copy.wait()
    pack[384:512, :] = tn(lowrank_ref[:, column(0)], gq).astype(BF)
    pack[512:640, :HALF_WIDTH] = tn(lowrank_ref[:, column(1)], gk).astype(BF)
    pack[512:640, HALF_WIDTH:] = tn(lowrank_ref[:, column(2)], gv).astype(BF)
    grad_rank = jnp.concatenate(
        [masked(nt(gq, bq[...])), masked(nt(gk, bkv[0])), masked(nt(gv, bkv[1]))], axis=1
    )
    pack[0:384, :] = tn(grad_rank, normed[...]).astype(BF)
    for copy in copies[12:]:
        copy.wait()
    grad_normed = (
        nt(gq, wq[...])
        + nt(jnp.concatenate([gk, gv], axis=1), wkv[...])
        + nt(grad_rank, aat[...])
    )
    x = x_ref[...].astype(F32)
    factor = lax.rsqrt(jnp.mean(x * x, axis=1, keepdims=True) + NORM_EPS)
    z = grad_normed * g1_ref[...]
    inner = jnp.mean(z * x, axis=1, keepdims=True)
    gi_ref[...] += factor * (z - x * (factor * factor * inner))
    half = ATT_ROWS // 2
    mine_ref[...] = pack[pl.ds(pl.multiple_of(side * half, 16), half), :]
    send_ref[...] = pack[pl.ds(pl.multiple_of((1 - side) * half, 16), half), :]


def attention_backward(scalars, arrays, later):
    half = ATT_ROWS // 2
    return pl.pallas_call(
        backward_body,
        out_shape=[shape(TOK_DEV, MODEL_WIDTH, dtype=F32), shape(half, MODEL_WIDTH), shape(half, MODEL_WIDTH)],
        in_specs=[SMEM] + [VMEM] * len(arrays) + [ANY] * len(later),
        out_specs=[VMEM] * 3,
        scratch_shapes=[pltpu.VMEM(w.shape, BF) for w in later]
        + [
            pltpu.VMEM((ATT_ROWS, MODEL_WIDTH), BF),
            pltpu.VMEM((TOK_DEV, MODEL_WIDTH), BF),
            pltpu.VMEM((TOK_DEV, MODEL_WIDTH), BF),
            pltpu.VMEM((TOK_DEV, HALF_WIDTH), BF),
            pltpu.VMEM((TOK_DEV, HALF_WIDTH), BF),
            pltpu.SemaphoreType.DMA((len(later),)),
        ],
        compiler_params=pltpu.CompilerParams(vmem_limit_bytes=VMEM_LIMIT),
        cost_estimate=pl.CostEstimate(flops=6_000_000_000, bytes_accessed=24_000_000, transcendentals=1_000_000),
        name="attention_backward",
    )(scalars, *arrays, *later)


def expert_body(
    scalars, *refs, expert, held, count, experts, carried, seeded, emit, last,
):
    refs = list(refs)

    def take(number):
        taken = refs[:number]
        del refs[:number]
        return taken

    x_blocks = take(count)
    g_blocks = take(count)
    ain_h, win_h, bin_h, adn_h, wdn_h, bdn_h = take(6)
    if carried:
        f_in, b_in, c_in = take(3)
    if held:
        take(3)
    seeds = take(4) if seeded else None
    if last:
        wr_ref, f_top, f_low, b_top, b_low = take(5)
    else:
        f_out, b_out, c_out = take(3)
    if emit:
        emitted = take(4)
    else:
        mine_ref, send_ref = take(2)
    xs, gs_buf, ain, win, bin_, adn, wdn, bdn, acc_a, acc_bi, acc_ad, acc_bd, pack, xsem, gsem, wsem = refs[:16]
    if last:
        f_buf, b_buf, fsem, bsem = refs[16:]
    sums = [acc_a, acc_bi, acc_ad, acc_bd]
    step = pl.program_id(0)
    slot = lax.rem(step, 2)
    early = [
        pltpu.make_async_copy(source.at[expert], target, wsem.at[index])
        for index, (source, target) in enumerate([(ain_h, ain), (win_h, win), (bin_h, bin_)])
    ]
    late = [
        pltpu.make_async_copy(source.at[expert], target, wsem.at[3 + index])
        for index, (source, target) in enumerate([(adn_h, adn), (wdn_h, wdn), (bdn_h, bdn)])
    ]

    def fetch(block):
        pltpu.make_async_copy(x_blocks[block], xs.at[block % 2], xsem.at[block % 2]).start()
        pltpu.make_async_copy(g_blocks[block], gs_buf.at[block % 2], gsem.at[block % 2]).start()

    @pl.when(step == 0)
    def _():
        fetch(0)
        for copy in early + late:
            copy.start()
        for index, total in enumerate(sums):
            total[...] = seeds[index][...] if seeded else jnp.zeros_like(total)
        for copy in early:
            copy.wait()

    for block in range(1, count):
        @pl.when(step == block - 1)
        def _(block=block):
            fetch(block)

    pltpu.make_async_copy(x_blocks[0], xs.at[slot], xsem.at[slot]).wait()
    pltpu.make_async_copy(g_blocks[0], gs_buf.at[slot], gsem.at[slot]).wait()
    if last:
        @pl.when(step >= 2)
        def _():
            pltpu.make_async_copy(b_buf.at[slot], b_top.at[pl.ds(0, TOK_DEV)], bsem.at[slot]).wait()
            pltpu.make_async_copy(f_buf.at[slot], f_top.at[pl.ds(0, TOK_DEV)], fsem.at[slot]).wait()

    eid = scalars[0] + expert
    side = scalars[1]
    x = xs[slot, :, :MODEL_WIDTH]
    meta = xs[slot, :, MODEL_WIDTH:].astype(F32)
    lane = lanes_of(TOK_DEV)
    adapter = meta[:, 96:97].astype(jnp.int32)
    mask = lane // ADAPTER_RANK == adapter

    def masked(values):
        return jnp.where(mask, values, 0.0).astype(BF)

    gates = jnp.where(lane < experts, meta + pltpu.roll(meta, 96, 1), 0.0)
    here = lane == eid
    gate_e = jnp.sum(jnp.where(here, gates, 0.0), axis=1, keepdims=True)
    low = nn(x, ain[...])
    low_gate = masked(low[:, :LANES])
    low_up = masked(low[:, LANES:])
    gate = nn(x, win[:, :HALF_WIDTH]) + nn(low_gate, bin_[0])
    up = nn(x, win[:, HALF_WIDTH:]) + nn(low_up, bin_[1])
    sig = 1.0 / (1.0 + jnp.exp(-gate))
    silu = gate * sig
    active = (silu * up).astype(BF)

    @pl.when(step == 0)
    def _():
        for copy in late:
            copy.wait()

    down = masked(nn(active, adn[...]))
    grad = gs_buf[slot].astype(F32)
    out = nn(active, wdn[...]) + nn(down, bdn[...])
    grad_gate_e = jnp.sum(out * grad, axis=1, keepdims=True)
    weighted = gate_e * out
    if carried:
        weighted = weighted + f_in[...]
    if last:
        f_buf[slot] = weighted.astype(BF)
    else:
        f_out[...] = weighted
    slot_grad = (gate_e * grad).astype(BF)
    grad_down = masked(nt(slot_grad, bdn[...]))
    grad_active = nt(slot_grad, wdn[...]) + nt(grad_down, adn[...])
    gate_grad = (grad_active * up * sig * (1.0 + gate * (1.0 - sig))).astype(BF)
    up_grad = (grad_active * silu).astype(BF)
    grad_low = jnp.concatenate([masked(nt(gate_grad, bin_[0])), masked(nt(up_grad, bin_[1]))], axis=1)
    both_grads = jnp.concatenate([gate_grad, up_grad], axis=1)
    rows = nt(both_grads, win[...]) + nt(grad_low, ain[...])
    part = (gate_e * grad_gate_e) * (jnp.where(here, 1.0, 0.0) - gates)
    if carried:
        rows = rows + b_in[...]
        part = part + c_in[...]
    if last:
        rows = rows + nt(part.astype(BF), wr_ref[...])

        b_buf[slot] = rows.astype(BF)
        for block in range(count):
            @pl.when(step == block)
            def _(block=block):
                part_rows = pl.ds(block // 2 * TOK_DEV, TOK_DEV)
                f_to = (f_low if block % 2 else f_top).at[part_rows]
                b_to = (b_low if block % 2 else b_top).at[part_rows]
                pltpu.make_async_copy(b_buf.at[block % 2], b_to, bsem.at[block % 2]).start()
                pltpu.make_async_copy(f_buf.at[block % 2], f_to, fsem.at[block % 2]).start()
    else:
        c_out[...] = part
        b_out[...] = rows
    acc_a[...] += tn(grad_low, x)
    acc_bi[:, :HALF_WIDTH] += tn(low_gate, gate_grad)
    acc_bi[:, HALF_WIDTH:] += tn(low_up, up_grad)
    acc_ad[...] += tn(grad_down, active)
    acc_bd[...] += tn(down, slot_grad)

    @pl.when(step == count - 1)
    def _():
        if emit:
            for target, total in zip(emitted, sums):
                target[...] = total[...]
        else:
            pack[0:256, :] = acc_a[...].astype(BF)
            pack[256:384, :] = acc_bi[...].astype(BF)
            pack[384:512, :] = acc_bd[...].astype(BF)
            pack[512:576, :HALF_WIDTH] = acc_ad[0:64, :].astype(BF)
            pack[512:576, HALF_WIDTH:] = acc_ad[64:128, :].astype(BF)
            half = PACK_ROWS // 2
            mine_ref[...] = pack[pl.ds(pl.multiple_of(side * half, 16), half), :]
            send_ref[...] = pack[pl.ds(pl.multiple_of((1 - side) * half, 16), half), :]
        if last:
            for index in range(2):
                pltpu.make_async_copy(b_buf.at[index], b_top.at[pl.ds(0, TOK_DEV)], bsem.at[index]).wait()
                pltpu.make_async_copy(f_buf.at[index], f_top.at[pl.ds(0, TOK_DEV)], fsem.at[index]).wait()


def expert_call(
    expert, scalars, x_blocks, g_blocks, weights, experts, blocks, start=0,
    carried=None, halves=None, seeds=None, emit=False, router_wide=None,
):
    count = len(x_blocks)
    total = blocks * TOK_DEV
    last = router_wide is not None
    rows = lambda width: pl.BlockSpec((TOK_DEV, width), lambda i, *_: (i + start, 0))
    whole = lambda *dims: pl.BlockSpec(dims, lambda i, *_: (0,) * len(dims), pipeline_mode=pl.Buffered(1))
    fixed = lambda *dims: pl.BlockSpec(dims, lambda i, *_: (0,) * len(dims))
    sum_dims = [(256, MODEL_WIDTH), (128, MODEL_WIDTH), (128, HALF_WIDTH), (128, MODEL_WIDTH)]
    in_specs = [ANY] * (2 * count + 6)
    args = [*x_blocks, *g_blocks, *weights]
    aliases = {}
    if carried is not None:
        in_specs += [rows(MODEL_WIDTH), rows(MODEL_WIDTH), rows(LANES)]
        args += list(carried)
    if halves is not None:
        aliases = {1 + len(args) + i: i for i in range(3)}
        in_specs += [ANY] * 3
        args += list(halves)
    if seeds is not None:
        in_specs += [whole(*d) for d in sum_dims]
        args += list(seeds)
    if last:
        in_specs.append(whole(MODEL_WIDTH, LANES))
        args.append(router_wide)
        outs = [shape(count // 2 * TOK_DEV, MODEL_WIDTH)] * 4
        out_specs = [ANY] * 4
    else:
        outs = [
            shape(total, MODEL_WIDTH, dtype=F32),
            shape(total, MODEL_WIDTH, dtype=F32),
            shape(total, LANES, dtype=F32),
        ]
        out_specs = [rows(MODEL_WIDTH), rows(MODEL_WIDTH), rows(LANES)]
    half = PACK_ROWS // 2
    if emit:
        outs += [shape(*d, dtype=F32) for d in sum_dims]
        out_specs += [fixed(*d) for d in sum_dims]
    else:
        outs += [shape(half, MODEL_WIDTH)] * 2
        out_specs += [fixed(half, MODEL_WIDTH)] * 2
    scratch = [pltpu.VMEM((2, TOK_DEV, META), BF), pltpu.VMEM((2, TOK_DEV, MODEL_WIDTH), BF)]
    scratch += [pltpu.VMEM(w.shape[1:], BF) for w in weights]
    scratch += [pltpu.VMEM(d, F32) for d in sum_dims]
    scratch += [
        pltpu.VMEM((PACK_ROWS, MODEL_WIDTH), BF),
        pltpu.SemaphoreType.DMA((2,)),
        pltpu.SemaphoreType.DMA((2,)),
        pltpu.SemaphoreType.DMA((6,)),
    ]
    if last:
        scratch += [pltpu.VMEM((2, TOK_DEV, MODEL_WIDTH), BF)] * 2 + [pltpu.SemaphoreType.DMA((2,))] * 2
    return pl.pallas_call(
        functools.partial(
            expert_body, expert=expert, held=halves is not None, count=count, experts=experts,
            carried=carried is not None, seeded=seeds is not None, emit=emit, last=last,
        ),
        out_shape=outs,
        grid_spec=pltpu.PrefetchScalarGridSpec(
            num_scalar_prefetch=1, grid=(count,), in_specs=in_specs, out_specs=out_specs, scratch_shapes=scratch
        ),
        input_output_aliases=aliases,
        compiler_params=pltpu.CompilerParams(
            dimension_semantics=("arbitrary",), vmem_limit_bytes=VMEM_LIMIT
        ),
        cost_estimate=pl.CostEstimate(
            flops=count * TOK_DEV * 9_800_000, bytes_accessed=5_000_000 * count, transcendentals=0
        ),
        name="expert_step",
    )(scalars, *args)


def expert_finish_body(scalars, *refs, count, held):
    pieces = refs[: 2 * count]
    a_in, b_in, a_down, b_down, pack = refs[2 * count + held :]
    side = scalars[0]
    half = PACK_ROWS // 2
    step = pl.program_id(0)
    for index in range(count):
        @pl.when(step == index)
        def _(index=index):
            pack[pl.ds(pl.multiple_of(side * half, 16), half), :] = pieces[2 * index][...]
            pack[pl.ds(pl.multiple_of((1 - side) * half, 16), half), :] = pieces[2 * index + 1][...]
    a_in[0] = pack[0:256, :].astype(F32).T
    b_in[0, 0] = pack[256:384, :HALF_WIDTH].astype(F32)
    b_in[0, 1] = pack[256:384, HALF_WIDTH:].astype(F32)
    b_down[0] = pack[384:512, :].astype(F32)
    a_down[0] = jnp.concatenate([pack[512:576, :HALF_WIDTH], pack[512:576, HALF_WIDTH:]], axis=0).astype(F32).T


def expert_finish(side, sums, start=0, held=()):
    half = PACK_ROWS // 2
    count = len(sums)
    pieces = [piece for one in sums for piece in (one.mine, one.got)]
    block = lambda *dims: pl.BlockSpec((1,) + dims, lambda i, *_: (i + start,) + (0,) * len(dims))
    dims = [(MODEL_WIDTH, 256), (2, 128, HALF_WIDTH), (HALF_WIDTH, 128), (128, MODEL_WIDTH)]
    return pl.pallas_call(
        functools.partial(expert_finish_body, count=count, held=len(held)),
        out_shape=[shape(EXP_DEV, *d, dtype=F32) for d in dims],
        grid_spec=pltpu.PrefetchScalarGridSpec(
            num_scalar_prefetch=1,
            grid=(count,),
            in_specs=[
                pl.BlockSpec((half, MODEL_WIDTH), lambda i, *_: (0, 0), pipeline_mode=pl.Buffered(1))
            ] * len(pieces)
            + [ANY] * len(held),
            out_specs=[block(*d) for d in dims],
            scratch_shapes=[pltpu.VMEM((PACK_ROWS, MODEL_WIDTH), BF)],
        ),
        input_output_aliases={1 + len(pieces) + i: i for i in range(len(held))},
        compiler_params=pltpu.CompilerParams(
            dimension_semantics=("arbitrary",), vmem_limit_bytes=VMEM_LIMIT
        ),
        cost_estimate=pl.CostEstimate(flops=1_000_000, bytes_accessed=4_000_000 * count, transcendentals=0),
        name="expert_finish",
    )(side, *pieces, *held)


def attention_finish_body(scalars, mine_ref, got_ref, a_ref, bq_ref, bkv_ref, oa_ref, ob_ref, pack):
    side = scalars[0]
    half = ATT_ROWS // 2
    pack[pl.ds(pl.multiple_of(side * half, 16), half), :] = mine_ref[...]
    pack[pl.ds(pl.multiple_of((1 - side) * half, 16), half), :] = got_ref[...]
    a_ref[...] = pack[0:384, :].astype(F32).T
    bq_ref[...] = pack[384:512, :].astype(F32)
    bkv_ref[0] = pack[512:640, :HALF_WIDTH].astype(F32)
    bkv_ref[1] = pack[512:640, HALF_WIDTH:].astype(F32)
    oa_ref[...] = pack[640:768, :].astype(F32).T
    ob_ref[...] = pack[768:896, :].astype(F32)


def attention_finish(side, mine, got):
    dims = [(MODEL_WIDTH, 384), (128, MODEL_WIDTH), (2, 128, HALF_WIDTH), (MODEL_WIDTH, 128), (128, MODEL_WIDTH)]
    return pl.pallas_call(
        attention_finish_body,
        out_shape=[shape(*d, dtype=F32) for d in dims],
        in_specs=[SMEM, VMEM, VMEM],
        out_specs=[VMEM] * 5,
        scratch_shapes=[pltpu.VMEM((ATT_ROWS, MODEL_WIDTH), BF)],
        compiler_params=pltpu.CompilerParams(vmem_limit_bytes=VMEM_LIMIT),
        cost_estimate=pl.CostEstimate(flops=1_000_000, bytes_accessed=6_000_000, transcendentals=0),
        name="attention_finish",
    )(side, mine, got)


def swap(values, axis, bit):
    size = lax.axis_size(axis)
    return lax.ppermute(values, axis, [(i, i ^ (1 << bit)) for i in range(size)])


def axis_bits(axis):
    return lax.axis_size(axis).bit_length() - 1


def tie(first, second):
    return lax.optimization_barrier((first, second))


def add(first, second):
    return (first.astype(F32) + second.astype(F32)).astype(BF)


def far_blocks(values):
    blocks = {0: values}
    for bit in reversed(range(1, axis_bits("expert"))):
        for index in list(blocks):
            blocks[index ^ (1 << bit)] = swap(blocks[index], "expert", bit)
    return blocks


def near_blocks(far):
    blocks = []
    for index in sorted(far):
        if index:
            blocks += [far[index], swap(far[index], "expert", 0)]
    return blocks


class Return:
    def __init__(self, top, low):
        self.top = top
        self.got = swap(low, "expert", 0)
        self.bits = list(reversed(range(1, axis_bits("expert"))))
        self.parts = []

    def reduce(self):
        count = self.top.shape[0] // TOK_DEV
        total = add(self.top, self.got)
        self.far = {2 * (i + 1): total[i * TOK_DEV : (i + 1) * TOK_DEV] for i in range(count)}

    def pick(self):
        self.bit = self.bits.pop(0)
        self.sent = [index for index in sorted(self.far) if index >> self.bit & 1]
        blocks = [self.far.pop(index) for index in self.sent]
        return blocks[0] if len(blocks) == 1 else jnp.concatenate(blocks, axis=0)

    def launch(self, send):
        self.got = swap(send, "expert", self.bit)

    def receive(self):
        for i, index in enumerate(self.sent):
            block = self.got[i * TOK_DEV : (i + 1) * TOK_DEV] if len(self.sent) > 1 else self.got
            index ^= 1 << self.bit
            if index:
                self.far[index] = add(self.far[index], block)
            else:
                self.parts.append(block)

    def finish(self):
        while self.bits:
            self.launch(self.pick())
            self.receive()
        total = self.parts[0]
        for part in self.parts[1:]:
            total = add(total, part)
        return total


class Holder:
    def __init__(self, got):
        self.got = got


class Sum:
    def __init__(self, mine, send, stages):
        self.path = []
        self.stages = list(stages)
        self.mine = mine
        self.send = send
        self.down = True
        self.target = self.stages.pop(0)
        self.path.append(self.target)

    def launch(self):
        self.got = swap(self.send, *self.target)
        return self

    def prepare(self):
        if self.down:
            values = add(self.mine, self.got)
            if self.stages:
                self.target = self.stages.pop(0)
                axis, bit = self.target
                rows, width = values.shape
                if rows % 16:
                    self.mine = self.send = values
                    return
                self.path.append(self.target)
                side = (lax.axis_index(axis) >> bit) & 1
                halves = values.reshape(2, rows // 2, width)
                self.mine = lax.dynamic_index_in_dim(halves, side, 0, keepdims=False)
                self.send = lax.dynamic_index_in_dim(halves, 1 - side, 0, keepdims=False)
                return
            self.down = False
        else:
            axis, bit = self.path.pop()
            side = (lax.axis_index(axis) >> bit) & 1
            low = jnp.where(side == 0, self.mine, self.got)
            high = jnp.where(side == 0, self.got, self.mine)
            values = jnp.concatenate([low, high], axis=0)
        self.target = self.path[-1]
        self.mine = self.send = values

    def pending(self):
        return self.down or len(self.path) > 1


def prepare(ones):
    for one in ones:
        one.prepare()


def step(*ones):
    ones = [one for one in ones if one.pending()]
    prepare(ones)
    for one in ones:
        one.launch()


def sync(holders, *extras):
    arrays = tuple(holder.got for holder in holders) + extras
    arrays = lax.optimization_barrier(arrays)
    for holder, got in zip(holders, arrays):
        holder.got = got
    return arrays[len(holders) :]


def on_device(
    inputs,
    lengths,
    routes,
    adapter_of_sequence,
    first_norm_gain,
    query_weight,
    key_value_weight,
    output_weight,
    second_norm_gain,
    router_weight,
    expert_input_weight,
    expert_down_weight,
    attention_first_factors,
    query_second_factors,
    key_value_second_factors,
    output_first_factors,
    output_second_factors,
    expert_input_first_factors,
    expert_input_second_factors,
    expert_down_first_factors,
    expert_down_second_factors,
    output_gradient,
):
    blocks = lax.axis_size("expert")
    experts = EXP_DEV * blocks
    place = lax.axis_index("expert")
    dp_side = lax.axis_index("dp") & 1
    core_side = place & 1
    grad_far = far_blocks(output_gradient)
    cosine, sine = rope_tables()
    scalars = jnp.stack([adapter_of_sequence[0], lengths[0], core_side]).astype(jnp.int32)
    g1 = first_norm_gain[None]
    g2 = second_norm_gain[None]
    weights = [
        attention_first_factors,
        query_weight,
        query_second_factors,
        key_value_weight,
        key_value_second_factors,
        output_first_factors,
        output_weight,
        output_second_factors,
    ]
    hidden, payload, router_wide, out_rank, normed, lowrank, queries, keys, values, attended, probs = attention_forward(
        scalars, inputs, g1, g2, cosine, sine, routes.T, router_weight.T, weights
    )
    for index in grad_far:
        if index:
            grad_far[index], payload = tie(grad_far[index], payload)
    row_far = far_blocks(payload)
    near = [[values, swap(values, "expert", 0)] for values in (payload, output_gradient)]
    expert_weights = [
        expert_input_first_factors,
        expert_input_weight,
        expert_input_second_factors,
        expert_down_first_factors,
        expert_down_weight,
        expert_down_second_factors,
    ]
    dp_stages = [("dp", bit) for bit in range(axis_bits("dp"))]
    sums = []
    first_number = EXP_DEV * place
    number = jnp.stack([first_number, dp_side]).astype(jnp.int32)
    *halves, s0, s1, s2, s3 = expert_call(
        0, number, *near, expert_weights, experts, blocks, emit=True
    )
    for far in (row_far, grad_far):
        for index in far:
            if index:
                far[index], s0 = tie(far[index], s0)
    row_blocks = near[0] + near_blocks(row_far)
    grad_blocks = near[1] + near_blocks(grad_far)
    *carried, mine, send = expert_call(
        0, number, row_blocks[2:], grad_blocks[2:], expert_weights, experts, blocks,
        start=2, halves=halves, seeds=(s0, s1, s2, s3),
    )
    sums.append(Sum(mine, send, dp_stages).launch())
    for local in range(1, EXP_DEV - 1):
        (number,) = sync(sums[: local - 1], number)
        step(*sums[: local - 1])
        *carried, mine, send = expert_call(
            local, number, row_blocks, grad_blocks, expert_weights, experts, blocks, carried=carried
        )
        sums.append(Sum(mine, send, dp_stages).launch())
    local = EXP_DEV - 1
    (number,) = sync(sums[:-1], number)
    step(*sums[:-1])
    mix_top, mix_low, row_top, row_low, s0, s1, s2, s3 = expert_call(
        local, number, row_blocks[2:], grad_blocks[2:], expert_weights, experts, blocks,
        start=2, carried=carried, router_wide=router_wide, emit=True,
    )
    (row_low,) = sync(sums, row_low)
    row = Return(row_top, row_low)
    mix = Return(mix_top, mix_low)
    step(*sums)
    row.reduce()
    row_send = row.pick()
    row_send, number = tie(row_send, number)
    row.launch(row_send)
    mix_top, mix_low, row_top, row_low, mine, send = expert_call(
        local, number, row_blocks[:2], grad_blocks[:2], expert_weights, experts, blocks,
        carried=carried, seeds=(s0, s1, s2, s3), router_wide=router_wide,
    )
    row_low, mix_low = sync(sums + [row, mix], row_low, mix_low)
    row_near = Holder(swap(row_low, "expert", 0))
    sums.append(Sum(mine, send, dp_stages).launch())
    step(*sums[:-1])
    row.receive()
    row_far = row.finish()
    mix_near = Holder(swap(mix_low, "expert", 0))
    mix.reduce()
    mix.launch(mix.pick())
    part_sends = [one.send for one in sums]
    sync([row_near, mix_near], *part_sends)
    grad_input, att_mine, att_send = attention_backward(
        scalars,
        [g1, g2, cosine, sine, hidden, row_top, row_near.got, row_far, output_gradient, out_rank],
        [output_second_factors, output_weight, output_first_factors, attended, queries, keys, values, probs]
        + [lowrank, query_second_factors, key_value_second_factors, normed, query_weight, key_value_weight]
        + [attention_first_factors, inputs],
    )
    (att_send,) = sync(sums + [mix], att_send)
    mix.receive()
    mix_far = mix.finish()
    stages = [("expert", bit) for bit in range(axis_bits("expert"))] + dp_stages
    total = Sum(att_mine, att_send, stages).launch()
    step(*sums)
    step(total)
    sync(sums + [total])
    step(total, *sums[2:])
    sync(sums[2:] + [total])
    step(total, *sums[1:])
    step(total)
    sync([total, sums[3]])
    step(total, sums[3])
    sync(sums[1:] + [total])
    step(total)
    sync([total, sums[3]])
    step(total, sums[3])
    for one in sums:
        while one.pending():
            step(one)
    dp_piece = dp_side[None].astype(jnp.int32)
    held = list(expert_finish(dp_piece, sums[:3]))
    (held[3],) = sync([total, sums[3]], held[3])
    while total.pending():
        step(total)
    expert_grads = expert_finish(dp_piece, sums[3:], 3, held)
    live = (jnp.arange(TOK_DEV, dtype=jnp.int32) < lengths[0]).astype(F32)[:, None]
    mixture = mix_top.astype(F32) + mix_near.got.astype(F32) + mix_far.astype(F32)
    output = (live * (hidden + mixture)).astype(BF)
    side = core_side[None].astype(jnp.int32)
    attention_grads = attention_finish(side, total.mine, total.got)
    return (output, grad_input, *attention_grads, *expert_grads)


def solution(mesh):
    rows = P(("dp", "expert"), None)
    each = P(("dp", "expert"))
    three = P("expert", None, None)
    four = P("expert", None, None, None)
    return jax.shard_map(
        on_device,
        mesh=mesh,
        in_specs=(
            (rows, each, rows, each)
            + (P(),) * 6
            + (three, three)
            + (P(),) * 5
            + (three, four, three, three, rows)
        ),
        out_specs=(rows, rows) + (P(),) * 5 + (three, four, three, three),
        check_vma=False,
    )
```
